256 devices in a mesh: expert: 64 (over z, x, core), mp: 4 (over y).
Axes of the slice: x: 4, y: 4, z: 8, core: 2. Of those that a mesh axis runs over, the one named last changes fastest.
Arguments:
- hidden_state: bfloat16 [8192, 2048], P('expert', 'mp'), as said below
- context: bfloat16 [8192, 2048], P('expert', 'mp'), may hold values from -6 to 6
- out_proj: bfloat16 [2048, 2048], P('mp', 'expert'), may hold values from -0.125 to 0.125
- norm_gain: bfloat16 [2048], P('mp'), may hold values from 0.25 to 1.75
- router_weight: float32 [2048, 64], P('mp'), as said below
- expert_in: bfloat16 [64, 2048, 2, 1408], P('expert', None, None, 'mp'), may hold values from -0.125 to 0.125
- expert_out: bfloat16 [64, 1408, 2048], P('expert', 'mp'), may hold values from -0.15625 to 0.15625
- shared_in: bfloat16 [2048, 2, 2816], P('expert', None, 'mp'), may hold values from -0.125 to 0.125
- shared_out: bfloat16 [2816, 2048], P('mp', 'expert'), may hold values from -0.109375 to 0.109375
- route_ids: int32 [8192, 6], P('expert'), may hold values from 0 to 63, all different within a row; in each aligned block of 128 rows (0 to 127, 128 to 255, ...) at most 20 rows name the same one
Outputs:
- output: float32 [8192, 2048], P('expert', 'mp')
The draws below stay inside these ranges and needn't reach their ends.
Inputs may be any that keep to these rules, and one draw needn't show every extreme that they name: `route_ids`: each row names 6 different experts; among the rows of one index of the expert axis no expert is named by more than 20 rows. `router_weight`: finite float32 router columns; no range is promised. `hidden_state`: finite values; no range is promised.
All inputs are finite; a program needn't handle non-finite values.
Results may differ from the reference program's by a relative error of at most 0.0025.
Values may be sent and summed in bfloat16 or wider, within the bound.
A program may use at most 128 MiB of HBM per device.

```python
import math
import jax
import jax.numpy as jnp
import numpy as np
from jax import lax

D = 2048
FFE = 1408
TOP = 6
TOK_DEV = 128
EXPERTS = 64
FFS = 2816
CAP = 20
TOKENS = 8192
N_MP = 4


def draw_router_weight(key, part):
    values = jax.random.normal(jax.random.fold_in(key, 11), (D, EXPERTS), jnp.float32)
    return values * (0.4 / math.sqrt(D))


def draw_hidden_state(key, part):
    column = jnp.arange(D, dtype=jnp.float32) / (D - 1)
    scales = jnp.exp(math.log(0.4) + column * (math.log(3.0) - math.log(0.4)))
    values = jnp.clip(jax.random.normal(key, (TOKENS, D), jnp.float32), -6.0, 6.0)
    return (values * scales[None, :]).astype(jnp.bfloat16)


def block_scale(rng, dims, cuts, smallest, largest):
    def one(dim, shards_of):
        heights = jax.random.uniform(jax.random.fold_in(jax.random.fold_in(rng, 6), dim), (shards_of,), jnp.float32, smallest / len(cuts), largest / len(cuts))
        return jnp.repeat(jnp.exp(heights), dims[dim] // shards_of).reshape((-1,) + (1,) * (len(dims) - dim - 1))

    gain = one(*cuts[0])
    for cut in cuts[1:]:
        gain = gain * one(*cut)
    return gain


def assign_block(key, own, number, rows, amount, top, reach, skew):
    order = jax.random.permutation(key, amount)
    crowded, usual = shares(amount, rows * top, reach, skew, True), shares(amount, rows * top, reach, skew, False)
    places = jnp.arange(amount)

    def named(lengths, offset_by):
        used = int((lengths > 0).sum())
        fixed = max(1, used // 4)
        shifted = fixed + (places - fixed + offset_by * (used - fixed)) % max(1, amount - fixed)
        return jnp.zeros((amount,), jnp.int32).at[order[jnp.where(places < fixed, places, shifted)]].set(jnp.asarray(lengths, jnp.int32))

    lengths = jnp.where(number % 4 == 0, named(crowded, number // 4), named(usual, number - number // 4 - 1))
    mixed = jax.random.permutation(jax.random.fold_in(own, 3), amount)
    giver, sink = mixed[0:amount // 2 * 2:2], mixed[1:amount // 2 * 2:2]
    slack = jnp.minimum(lengths[giver] - 1, reach - lengths[sink]) // 2
    slack = jnp.where((giver == order[0]) | (sink == order[0]) | (lengths[sink] == 0), 0, jnp.maximum(slack, 0))
    shifted = jax.random.randint(jax.random.fold_in(own, 4), (amount // 2,), 0, 1 << 20) % (slack + 1)
    lengths = lengths.at[giver].add(-shifted).at[sink].add(shifted)
    items = jnp.searchsorted(jnp.cumsum(lengths), jnp.arange(rows * top), side="right").astype(jnp.int32)
    table = items.reshape(top, rows).T
    table = table[jax.random.permutation(jax.random.fold_in(own, 1), rows)]
    offset_by = jax.random.randint(jax.random.fold_in(own, 2), (rows, 1), 0, top)
    return jnp.take_along_axis(table, (jnp.arange(top)[None, :] + offset_by) % top, axis=1)


def shares(number_of, total, bound, slope, full):
    loads = [(1 << 20) // math.isqrt(grade ** slope) + 1 for grade in range(1, number_of + 1)]
    largest = bound if full else min(bound, max(-(-total // number_of), total * loads[0] // sum(loads)))
    least = 1 if total - largest >= number_of - 1 else 0
    holding, rest = [largest] + [least] * (number_of - 1), total - largest - least * (number_of - 1)
    while rest > 0:
        candidates = [i for i in range(1, number_of) if holding[i] < largest] or [i for i in range(1, number_of) if holding[i] < bound]
        whole, remaining = sum([loads[i] for i in candidates]), rest
        for i in candidates:
            addition = min(bound - holding[i], max(1, remaining * loads[i] // whole), rest)
            holding[i] = holding[i] + addition
            rest = rest - addition
    return np.array(holding)


def gaussian(key, extent, spread, reach, pieces=(), kind=jnp.bfloat16):
    array = spread * jax.random.normal(key, extent, jnp.float32)
    if pieces:
        array = array * block_scale(key, extent, pieces, -0.22, 0.18)
    return jnp.clip(array, -reach, reach).astype(kind)


def setup_inputs(seed: int = 0) -> dict:
    streams_of = jax.random.split(jax.random.key(seed), 11)
    hidden_state = draw_hidden_state(jax.random.fold_in(streams_of[10], 71), 0)
    context = gaussian(streams_of[1], (TOKENS, D), 1.0, 6.0, ((0, 64), (1, 4)))
    out_proj = gaussian(streams_of[2], (D, D), D ** -0.5, 0.125, ((0, 4), (1, 64)))
    norm_gain = jnp.clip(1.0 + 0.15 * jax.random.normal(streams_of[3], (D,), jnp.float32), 0.25, 1.75).astype(jnp.bfloat16)
    router_weight = draw_router_weight(jax.random.fold_in(streams_of[10], 71), 0)
    expert_in = gaussian(streams_of[5], (EXPERTS, D, 2, FFE), D ** -0.5, 0.125, ((0, 64), (3, 4)))
    expert_out = gaussian(streams_of[6], (EXPERTS, FFE, D), FFE ** -0.5, 0.15625, ((0, 64), (1, 4)))
    shared_in = gaussian(streams_of[7], (D, 2, FFS), D ** -0.5, 0.125, ((0, 64), (2, 4)))
    shared_out = gaussian(streams_of[8], (FFS, D), FFS ** -0.5, 0.109375, ((0, 4), (1, 64)))
    route_ids_keys = jax.random.split(jax.random.fold_in(streams_of[9], 1), TOKENS // TOK_DEV)
    route_ids_turns = jax.random.permutation(jax.random.fold_in(streams_of[9], 3), TOKENS // TOK_DEV)
    route_ids = jax.vmap(lambda own, number: assign_block(jax.random.fold_in(streams_of[9], 2), own, number, TOK_DEV, EXPERTS, TOP, CAP, 2))(route_ids_keys, route_ids_turns).reshape((TOKENS, TOP))
    return {"hidden_state": hidden_state, "context": context, "out_proj": out_proj, "norm_gain": norm_gain, "router_weight": router_weight, "expert_in": expert_in, "expert_out": expert_out, "shared_in": shared_in, "shared_out": shared_out, "route_ids": route_ids}


def reference(hidden_state, context, out_proj, norm_gain, router_weight, expert_in, expert_out, shared_in, shared_out, route_ids):
    attn = jnp.dot(context, out_proj, preferred_element_type=jnp.float32)
    mixed = hidden_state.astype(jnp.float32) + attn
    inverse = lax.rsqrt(lax.optimization_barrier(jnp.mean(mixed * mixed, axis=1, keepdims=True)) + 1e-06)
    normed32 = mixed * inverse * norm_gain.astype(jnp.float32)
    normed = normed32.astype(jnp.bfloat16)
    logits = jnp.dot(normed32, router_weight, precision=lax.Precision.HIGHEST)
    chosen = jnp.take_along_axis(logits, route_ids, axis=1)
    gates = jax.nn.softmax(chosen, axis=1)
    both = jnp.dot(normed, shared_in.reshape(D, 2 * FFS), preferred_element_type=jnp.float32).reshape(-1, 2, FFS)
    shared_hidden = (jax.nn.silu(both[:, 0]) * both[:, 1]).astype(jnp.bfloat16)
    shared = jnp.dot(shared_hidden, shared_out, preferred_element_type=jnp.float32)
    blocks = TOKENS // TOK_DEV
    flat = route_ids.reshape(blocks, TOK_DEV * TOP)
    onehot = (flat[:, :, None] == jnp.arange(EXPERTS, dtype=jnp.int32)[None, None, :]).astype(jnp.int32)
    position = lax.optimization_barrier(jnp.sum(onehot * jnp.cumsum(onehot, axis=1), axis=2)) - 1
    row_of = (jnp.arange(TOK_DEV * TOP, dtype=jnp.int32) // TOP)[None, :] + (jnp.arange(blocks, dtype=jnp.int32) * TOK_DEV)[:, None]
    block_of = jnp.broadcast_to(jnp.arange(blocks, dtype=jnp.int32)[:, None], flat.shape)
    table = jnp.zeros((EXPERTS, blocks, CAP), jnp.int32).at[flat, block_of, position].set(row_of)
    weight_table = jnp.zeros((EXPERTS, blocks, CAP), jnp.float32).at[flat, block_of, position].set(gates.reshape(blocks, TOK_DEV * TOP))
    quarter = FFE // N_MP

    def one_expert(routed, expert):
        rows = table[expert].reshape(-1)
        weights = weight_table[expert].reshape(-1)
        taken = normed[rows]
        inner = jnp.dot(taken, expert_in[expert].reshape(D, 2 * FFE), preferred_element_type=jnp.float32).reshape(-1, 2, FFE)
        hidden = (jax.nn.silu(inner[:, 0]) * inner[:, 1]).astype(jnp.bfloat16)
        parts = jnp.einsum('sqf,qfd->qsd', hidden.reshape(-1, N_MP, quarter).astype(jnp.float32), expert_out[expert].reshape(N_MP, quarter, D).astype(jnp.float32))
        rounded = lax.optimization_barrier(parts.astype(jnp.bfloat16))
        total = lax.optimization_barrier(jnp.sum(rounded.astype(jnp.float32), axis=0))
        total = lax.optimization_barrier(total.astype(jnp.bfloat16)).astype(jnp.float32)
        routed = routed.at[rows].add(weights[:, None] * total)
        return (routed, None)
    routed, _ = lax.scan(one_expert, jnp.zeros((TOKENS, D), jnp.float32), jnp.arange(EXPERTS, dtype=jnp.int32))
    return mixed + routed + shared
```

```python
import jax
import jax.numpy as jnp
from jax import lax
from jax.experimental import pallas as pl
from jax.experimental.pallas import tpu as pltpu
from jax.sharding import PartitionSpec as P

NZ, NX, NC, NY = 8, 4, 2, 4
NE = NZ * NX * NC
ROWS, FEAT, WIDTH = 128, 512, 2048
TOP, CAP, SLOT = 6, 20, 32
QUARTER, QPAD = 352, 384
SWIDTH, SPAD = 704, 768
CHUNK = NX * NC * CAP
HALF = CHUNK // 2
NCH = NZ + 1
F32, BF16 = jnp.float32, jnp.bfloat16
VMEM_LIMIT = 64 * 1024 * 1024 - 65536


def coords():
    e = lax.axis_index("expert")
    y = lax.axis_index("mp")
    z = lax.div(e, NX * NC)
    x = lax.rem(lax.div(e, NC), NX)
    c = lax.rem(e, NC)
    return e, z, x, c, y


def eid(z, x, c):
    return z * (NX * NC) + x * NC + c


def blk(z, c, x):
    return z * (NX * NC) + c * NX + x


def send(src, dst, ssem, rsem, e, y):
    return pltpu.make_async_remote_copy(
        src_ref=src,
        dst_ref=dst,
        send_sem=ssem,
        recv_sem=rsem,
        device_id={"expert": e, "mp": y},
        device_id_type=pl.DeviceIdType.MESH,
    )


def greet(e, y):
    pl.semaphore_signal(
        pltpu.get_barrier_semaphore(),
        inc=1,
        device_id={"expert": e, "mp": y},
        device_id_type=pl.DeviceIdType.MESH,
    )


def nt(a, b):
    return lax.dot_general(a, b, (((1,), (1,)), ((), ())), preferred_element_type=F32)


class XGather:
    def __init__(self, src, buf, own, lft, rgt, opp, half, ssem, rsem, to_r, to_l, y):
        self.own_r = send(src, buf.at[own], ssem.at[0], rsem.at[0], to_r, y)
        self.own_l = send(src, buf.at[own], ssem.at[1], rsem.at[1], to_l, y)
        lo, hi = pl.ds(0, half), pl.ds(half, half)
        self.got_l = send(src, buf.at[lft], ssem.at[0], rsem.at[0], to_r, y)
        self.got_r = send(src, buf.at[rgt], ssem.at[1], rsem.at[1], to_l, y)
        self.fwd_r = send(buf.at[lft, lo], buf.at[lft, lo], ssem.at[2], rsem.at[2], to_r, y)
        self.fwd_l = send(buf.at[rgt, hi], buf.at[rgt, hi], ssem.at[3], rsem.at[3], to_l, y)
        self.end_r = send(buf.at[opp, lo], buf.at[opp, lo], ssem.at[2], rsem.at[2], to_r, y)
        self.end_l = send(buf.at[opp, hi], buf.at[opp, hi], ssem.at[3], rsem.at[3], to_l, y)

    def start(self):
        self.own_r.start()
        self.own_l.start()

    def forward(self):
        self.got_l.wait_recv()
        self.fwd_r.start()
        self.got_r.wait_recv()
        self.fwd_l.start()

    def finish(self):
        self.end_r.wait_recv()
        self.end_l.wait_recv()

    def drain(self):
        for copy in (self.own_r, self.own_l, self.fwd_r, self.fwd_l):
            copy.wait_send()


def pre_kernel(
    ctx, wsh, hid, gain, router,
    normed_o, mixed_o, logits_o, routes_o,
    wg, part, r1, r2, sq, lg,
    lsem, xs, xr, zs, zr, ss, sr, ys, yr, qs, qr,
):
    e, z, x, c, y = coords()
    xr_, xl_ = lax.rem(x + 1, NX), lax.rem(x + NX - 1, NX)
    to_r, to_l = eid(z, xr_, c), eid(z, xl_, c)
    to_u, to_d = eid(lax.rem(z + 1, NZ), x, c), eid(lax.rem(z + NZ - 1, NZ), x, c)
    sib = eid(z, x, 1 - c)
    yu, yd, yo = lax.rem(y + 1, NY), lax.rem(y + NY - 1, NY), lax.rem(y + 2, NY)
    for t in (to_r, to_l, to_u, to_d, sib):
        greet(t, y)
    for t in (yu, yd, yo):
        greet(e, t)
    pl.semaphore_wait(pltpu.get_barrier_semaphore(), 8)

    own = blk(z, c, x)
    mine = pltpu.make_async_copy(wsh, wg.at[own], lsem)
    mine.start()
    gx = XGather(
        wsh, wg, own, blk(z, c, xl_), blk(z, c, xr_), blk(z, c, lax.rem(x + 2, NX)),
        16, xs, xr, to_r, to_l, y,
    )
    gx.start()
    mine.wait()
    gx.forward()
    gx.finish()

    def plane(p, cc, n=NX, off=0):
        return wg.at[pl.ds(p * (NX * NC) + cc * NX + off, n)]

    def up(t):
        p = lax.rem(z + NZ - t, NZ)
        r = plane(p, c) if t < 3 else plane(p, c, 2, 0)
        return send(r, r, zs.at[t], zr.at[t], to_u, y)

    def down(t):
        p = lax.rem(z + t, NZ)
        r = plane(p, c) if t < 3 else plane(p, c, 2, 2)
        return send(r, r, zs.at[4 + t], zr.at[4 + t], to_d, y)

    def got(t, d):
        p = lax.rem(z + NZ + d * (t + 1), NZ)
        base = 0 if d < 0 else 4
        r = plane(p, c) if t < 3 else plane(p, c, 2, 0 if d < 0 else 2)
        send(r, r, zs.at[base + t], zr.at[base + t], to_u, y).wait_recv()

    def across(k, p, cc):
        r = plane(p, cc)
        return send(r, r, ss.at[k], sr.at[k], sib, y)

    up(0).start()
    down(0).start()
    across(0, z, c).start()
    for t in range(3):
        got(t, -1)
        up(t + 1).start()
        got(t, 1)
        down(t + 1).start()
        across(2 * t + 1, lax.rem(z + NZ - t - 1, NZ), c).start()
        across(2 * t + 2, lax.rem(z + t + 1, NZ), c).start()
    got(3, -1)
    got(3, 1)
    across(7, lax.rem(z + 4, NZ), c).start()
    order = [0, -1, 1, -2, 2, -3, 3, 4]
    for k in range(NZ):
        across(k, lax.rem(z + NZ + order[k], NZ), 1 - c).wait_recv()

    def columns(d):
        blocks = []
        for zz in range(2):
            for xx in range(NX):
                for cc in range(NC):
                    blocks.append(wg[(2 * d + zz) * (NX * NC) + cc * NX + xx, :, :FEAT])
        return nt(ctx[...], jnp.concatenate(blocks, axis=0))

    part[yo] = columns(yo)
    hrows = ROWS // 2
    lo, hi = pl.ds(0, hrows), pl.ds(hrows, hrows)
    a_u = send(part.at[yo, lo], r1.at[0], ys.at[0], yr.at[0], e, yu)
    a_d = send(part.at[yo, hi], r1.at[1], ys.at[1], yr.at[1], e, yd)
    a_u.start()
    a_d.start()
    part[yu] = columns(yu)
    part[yd] = columns(yd)
    a_u.wait_recv()
    part[yu, lo] = part[yu, lo] + r1[0]
    b_u = send(part.at[yu], r2.at[0], ys.at[2], yr.at[2], e, yu)
    b_u.start()
    a_d.wait_recv()
    part[yd, hi] = part[yd, hi] + r1[1]
    b_d = send(part.at[yd], r2.at[1], ys.at[3], yr.at[3], e, yd)
    b_d.start()
    attn = columns(y)
    routes_o[...] = wg[:, 0:16, FEAT : FEAT + ROWS]
    b_u.wait_recv()
    b_d.wait_recv()
    mixed = hid[...].astype(F32) + (attn + r2[0] + r2[1])
    mixed_o[...] = mixed

    def spread(buf, base):
        copies = []
        for k, t in enumerate((yu, yd, yo)):
            copies.append(send(buf.at[3], buf.at[k], qs.at[base + k], qr.at[base + k], e, t))
        for copy in copies:
            copy.start()
        for copy in copies:
            copy.wait_recv()
        return copies

    sq[3] = jnp.broadcast_to(jnp.sum(mixed * mixed, axis=1, keepdims=True), (ROWS, 128))
    c1 = spread(sq, 0)
    squares = (sq[0] + sq[1]) + (sq[2] + sq[3])
    inverse = lax.rsqrt(squares[:, :1] / WIDTH + 1e-06)
    normed32 = mixed * inverse * gain[...]
    normed_o[...] = normed32.astype(BF16)
    lg[3] = jnp.dot(
        normed32, router[...], precision=lax.Precision.HIGHEST, preferred_element_type=F32
    )
    c2 = spread(lg, 3)
    logits_o[...] = (lg[0] + lg[1]) + (lg[2] + lg[3])

    gx.drain()
    for t in range(4):
        up(t).wait_send()
        down(t).wait_send()
    for k in range(NZ):
        across(k, lax.rem(z + NZ + order[k], NZ), c).wait_send()
    for copy in [a_u, a_d, b_u, b_d] + c1 + c2:
        copy.wait_send()


def pre(ctx, wsh, hid, gain, router):
    dma = pltpu.SemaphoreType.DMA
    vm = pl.BlockSpec(memory_space=pltpu.VMEM)
    return pl.pallas_call(
        pre_kernel,
        name="attention_norm_router",
        out_shape=[
            jax.ShapeDtypeStruct((ROWS, FEAT), BF16),
            jax.ShapeDtypeStruct((ROWS, FEAT), F32),
            jax.ShapeDtypeStruct((ROWS, 128), F32),
            jax.ShapeDtypeStruct((NE, 16, ROWS), BF16),
        ],
        in_specs=[vm] * 5,
        out_specs=[vm] * 4,
        scratch_shapes=[
            pltpu.VMEM((NE, 32, FEAT + ROWS), BF16),
            pltpu.VMEM((NY, ROWS, FEAT), F32),
            pltpu.VMEM((2, ROWS // 2, FEAT), F32),
            pltpu.VMEM((2, ROWS, FEAT), F32),
            pltpu.VMEM((4, ROWS, 128), F32),
            pltpu.VMEM((4, ROWS, 128), F32),
            dma,
            dma((4,)), dma((4,)),
            dma((8,)), dma((8,)),
            dma((8,)), dma((8,)),
            dma((4,)), dma((4,)),
            dma((6,)), dma((6,)),
        ],
        compiler_params=pltpu.CompilerParams(
            collective_id=0, has_side_effects=True, vmem_limit_bytes=VMEM_LIMIT
        ),
    )(ctx, wsh, hid, gain, router)


def tail_kernel(
    normed, routes, wsh, win, wout,
    res_o, shared_o,
    tok, slot, xg, pb, r1, r2, wb, wi, wo, sbuf, rbuf, acc,
    lsem, wsem, xs, xr, zs, zr, ss, sr, wzs, wzr, wxs, wxr, wss, wsr, gs, gr, ps, pr, os_, or_,
):
    e, z, x, c, y = coords()
    xr_, xl_ = lax.rem(x + 1, NX), lax.rem(x + NX - 1, NX)
    xo_ = lax.rem(x + 2, NX)
    to_r, to_l = eid(z, xr_, c), eid(z, xl_, c)
    to_u, to_d = eid(lax.rem(z + 1, NZ), x, c), eid(lax.rem(z + NZ - 1, NZ), x, c)
    sib = eid(z, x, 1 - c)
    yu, yd, yo = lax.rem(y + 1, NY), lax.rem(y + NY - 1, NY), lax.rem(y + 2, NY)
    lo, hi = pl.ds(0, HALF), pl.ds(HALF, HALF)

    def hello(k, carry):
        greet(lax.rem(e + k, NE), y)
        return carry

    lax.fori_loop(1, NE, hello, 0)
    greet(e, yu)
    greet(e, yd)
    pl.semaphore_wait(pltpu.get_barrier_semaphore(), NE + 1)

    own = blk(z, c, x)
    keep = pltpu.make_async_copy(normed, tok.at[own], lsem.at[0])
    keep.start()
    gx = XGather(
        normed, tok, own, blk(z, c, xl_), blk(z, c, xr_), blk(z, c, xo_),
        ROWS // 2, xs, xr, to_r, to_l, y,
    )
    gx.start()

    def wblk(zz, cc, xx):
        return cc * (NX * NZ) + xx * NZ + zz

    wown = pltpu.make_async_copy(wsh, wb.at[wblk(z, c, x)], lsem.at[1])
    wown.start()
    loads = [
        pltpu.make_async_copy(win.at[0], wi.at[0, pl.ds(0, QUARTER)], wsem.at[0]),
        pltpu.make_async_copy(win.at[1], wi.at[1, pl.ds(0, QUARTER)], wsem.at[1]),
        pltpu.make_async_copy(wout, wo.at[pl.ds(0, QUARTER)], wsem.at[2]),
    ]
    for load in loads:
        load.start()
    pad = pl.ds(QUARTER, QPAD - QUARTER)
    wi[0, pad] = jnp.zeros((QPAD - QUARTER, WIDTH), BF16)
    wi[1, pad] = jnp.zeros((QPAD - QUARTER, WIDTH), BF16)
    wo[pad] = jnp.zeros((QPAD - QUARTER, WIDTH), BF16)

    def mark(b, carry):
        named = (routes[b].astype(F32) == e.astype(F32)).astype(F32)
        slot[pl.ds(b, 1), :] = jnp.sum(named, axis=0, keepdims=True)
        return carry

    lax.fori_loop(0, NE, mark, 0)
    before = lax.broadcasted_iota(jnp.int32, (ROWS, ROWS), 0) < lax.broadcasted_iota(
        jnp.int32, (ROWS, ROWS), 1
    )
    named = slot[...]
    rank = jnp.dot(named.astype(BF16), before.astype(F32).astype(BF16), preferred_element_type=F32)
    slot[...] = jnp.where(named > 0.5, rank, -1000.0)

    keep.wait()
    gx.forward()
    gx.finish()

    def plane(p, cc, n=NX, off=0):
        return tok.at[pl.ds(p * (NX * NC) + cc * NX + off, n)]

    def whole_up(t):
        r = plane(lax.rem(z + NZ - t, NZ), c)
        return send(r, r, zs.at[t], zr.at[t], to_u, y)

    def whole_down(t):
        r = plane(lax.rem(z + t, NZ), c)
        return send(r, r, zs.at[4 + t], zr.at[4 + t], to_d, y)

    def half_up(p):
        r = plane(p, c, 2, 0)
        return send(r, r, zs.at[3], zr.at[3], to_u, y)

    def half_down(p):
        r = plane(p, c, 2, 2)
        return send(r, r, zs.at[7], zr.at[7], to_d, y)

    def across(k, p, cc):
        r = plane(p, cc)
        return send(r, r, ss.at[k], sr.at[k], sib, y)

    def plane_of(k):
        t = lax.div(k + 1, 2)
        return lax.rem(z + NZ + t * (1 - 2 * lax.rem(k, 2)), NZ)

    def stage_tokens(k):
        t = lax.div(k + 1, 2)
        p = plane_of(k)

        @pl.when(k == 0)
        def _():
            whole_up(0).start()
            whole_down(0).start()

        @pl.when((k > 0) & (k < 7) & (lax.rem(k, 2) == 1))
        def _():
            r = plane(p, c)
            send(r, r, zs.at[t - 1], zr.at[t - 1], to_u, y).wait_recv()

            @pl.when(t < 3)
            def _():
                whole_up(t).start()

            @pl.when(t == 3)
            def _():
                half_up(p).start()

        @pl.when((k > 0) & (lax.rem(k, 2) == 0))
        def _():
            r = plane(p, c)
            send(r, r, zs.at[3 + t], zr.at[3 + t], to_d, y).wait_recv()

            @pl.when(t < 3)
            def _():
                whole_down(t).start()

            @pl.when(t == 3)
            def _():
                half_down(p).start()

        @pl.when(k == 7)
        def _():
            half_up(p).wait_recv()
            half_down(p).wait_recv()

        across(k, p, c).start()

    def ag(i, k, who, rows, to):
        r = xg.at[i, who] if rows is None else xg.at[i, who, rows]
        return send(r, r, gs.at[k, i], gr.at[k, i], e, to)

    def stage_rows(i):
        @pl.when(i < NZ)
        def _():
            p = plane_of(i)
            across(i, p, 1 - c).wait_recv()
            rows = lax.broadcasted_iota(jnp.int32, (CHUNK, ROWS), 0).astype(F32)

            def pick(b, total):
                k = p * (NX * NC) + b
                where = slot[pl.ds(k, 1), :] + (CAP * b).astype(F32)
                onehot = (rows == where).astype(F32).astype(BF16)
                return total + jnp.dot(onehot, tok[k], preferred_element_type=F32)

            taken = lax.fori_loop(0, NX * NC, pick, jnp.zeros((CHUNK, FEAT), F32))
            xg[i, y] = taken.astype(BF16)

        @pl.when(i == NZ)
        def _():
            xg[i, y, pl.ds(0, ROWS)] = normed[...]
            xg[i, y, pl.ds(ROWS, CHUNK - ROWS)] = jnp.zeros((CHUNK - ROWS, FEAT), BF16)

        ag(i, 0, y, None, yu).start()
        ag(i, 1, y, None, yd).start()

    def stage_relay(i):
        ag(i, 0, yd, None, yu).wait_recv()
        ag(i, 2, yd, lo, yu).start()
        ag(i, 1, yu, None, yd).wait_recv()
        ag(i, 3, yu, hi, yd).start()

    def rs1(i, k):
        rows, to = (lo, yu) if k == 0 else (hi, yd)
        return send(pb.at[i, yo, rows], r1.at[i, k], ps.at[k, i], pr.at[k, i], e, to)

    def rs2(i, k):
        to = yu if k == 0 else yd
        return send(pb.at[i, to], r2.at[i, k], ps.at[2 + k, i], pr.at[2 + k, i], e, to)

    def gated(gate, value):
        return (gate / (1.0 + jnp.exp(-gate)) * value).astype(BF16)

    def stage_experts(i):
        ag(i, 2, yo, lo, yu).wait_recv()
        ag(i, 3, yo, hi, yd).wait_recv()

        @pl.when(i < NZ)
        def _():
            both = []
            for h in range(2):
                total = jnp.zeros((CHUNK, QPAD), F32)
                for k in range(NY):
                    total = total + nt(xg[i, k], wi[h, :, k * FEAT : (k + 1) * FEAT])
                both.append(total)
            hidden = gated(both[0], both[1])

            def down(d, carry):
                w = wo[:, pl.ds(pl.multiple_of(d * FEAT, FEAT), FEAT)]
                pb[i, d] = jnp.dot(hidden, w, preferred_element_type=F32).astype(BF16)
                return carry

            lax.fori_loop(0, NY, down, 0)

        @pl.when(i == NZ)
        def _():
            for k in range(NX):
                column = wb.at[pl.ds((1 - c) * (NX * NZ) + k * NZ, NZ)]
                send(column, column, wss.at[k], wsr.at[k], sib, y).wait_recv()
            acc[...] = jnp.zeros((CHUNK, 2 * SPAD), F32)

            def into(zz, carry):
                w = jnp.concatenate(
                    [wb[wblk(zz, cc, xx), :, : 2 * SPAD] for xx in range(NX) for cc in range(NC)],
                    axis=0,
                )
                off = pl.multiple_of(lax.rem(zz, 2) * 256, 256)
                acc[...] += jnp.dot(
                    xg[i, lax.div(zz, 2), :, pl.ds(off, 256)], w, preferred_element_type=F32
                )
                return carry

            lax.fori_loop(0, NZ, into, 0)
            hidden = gated(acc[:, :SPAD], acc[:, SPAD:])

            def out(d, carry):
                w = jnp.concatenate(
                    [
                        wb[wblk(2 * d + zz, cc, xx), :, 2 * SPAD :]
                        for zz in range(2)
                        for xx in range(NX)
                        for cc in range(NC)
                    ],
                    axis=0,
                )
                pb[i, d] = nt(hidden, w).astype(BF16)
                return carry

            lax.fori_loop(0, NY, out, 0)

        rs1(i, 0).start()
        rs1(i, 1).start()

    def stage_reduce(i):
        rs1(i, 0).wait_recv()
        pb[i, yu, lo] = (pb[i, yu, lo].astype(F32) + r1[i, 0].astype(F32)).astype(BF16)
        rs2(i, 0).start()
        rs1(i, 1).wait_recv()
        pb[i, yd, hi] = (pb[i, yd, hi].astype(F32) + r1[i, 1].astype(F32)).astype(BF16)
        rs2(i, 1).start()

    def dest(i, b):
        return eid(plane_of(i), lax.rem(b, NX), lax.div(b, NX))

    def back(i, b):
        to = dest(i, b)
        return to, send(sbuf.at[i, b], rbuf.at[e], os_.at[i * (NX * NC) + b], or_.at[e], to, y)

    def stage_return(i):
        rs2(i, 0).wait_recv()
        rs2(i, 1).wait_recv()
        total = pb[i, y].astype(F32) + r2[i, 0].astype(F32) + r2[i, 1].astype(F32)

        @pl.when(i < NZ)
        def _():
            to_row = lax.broadcasted_iota(jnp.int32, (NX * NC * SLOT, CHUNK), 0)
            of_row = lax.broadcasted_iota(jnp.int32, (NX * NC * SLOT, CHUNK), 1)
            inner = of_row - CAP * lax.shift_right_logical(to_row, 5)
            move = (inner == (to_row & (SLOT - 1))) & (inner < CAP) & (inner >= 0)
            spaced = jnp.dot(
                move.astype(F32).astype(BF16), total.astype(BF16), preferred_element_type=F32
            )
            sbuf[i] = spaced.astype(BF16).reshape(NX * NC, SLOT, FEAT)

            def go(b, carry):
                to, copy = back(i, b)

                @pl.when(to != e)
                def _():
                    copy.start()

                @pl.when(to == e)
                def _():
                    rbuf[e] = sbuf[i, b]

                return carry

            lax.fori_loop(0, NX * NC, go, 0)

        @pl.when(i == NZ)
        def _():
            shared_o[...] = total[:ROWS]

    def wz(t, d, half):
        p = lax.rem(z + NZ - d * t, NZ)
        r = wb.at[wblk(p, c, x)]
        if half:
            r = wb.at[wblk(p, c, x), pl.ds(0 if d > 0 else 16, 16)]
        k = (0 if d > 0 else 4) + t
        return send(r, r, wzs.at[k], wzr.at[k], to_u if d > 0 else to_d, y)

    def wz_got(t, d, half):
        p = lax.rem(z + NZ - d * (t + 1), NZ)
        r = wb.at[wblk(p, c, x)]
        if half:
            r = wb.at[wblk(p, c, x), pl.ds(0 if d > 0 else 16, 16)]
        k = (0 if d > 0 else 4) + t
        send(r, r, wzs.at[k], wzr.at[k], to_u if d > 0 else to_d, y).wait_recv()

    def col(xx, n=NZ, off=0):
        return wb.at[pl.ds(c * (NX * NZ) + xx * NZ + off, n)]

    def wx(k):
        r, to = [
            (col(x), to_r), (col(x), to_l), (col(xl_, 4, 0), to_r), (col(xr_, 4, 4), to_l)
        ][k]
        return send(r, r, wxs.at[k], wxr.at[k], to, y)

    def wx_got(k):
        r = [col(xl_), col(xr_), col(xo_, 4, 0), col(xo_, 4, 4)][k]
        send(r, r, wxs.at[k], wxr.at[k], to_r, y).wait_recv()

    def wsib(xx):
        r = col(xx)
        return send(r, r, wss.at[xx], wsr.at[xx], sib, y)

    def stage_weights(j):
        @pl.when(j == 0)
        def _():
            wown.wait()
            wz(0, 1, False).start()
            wz(0, -1, False).start()

        for t in range(3):

            @pl.when(j == t + 1)
            def _(t=t):
                wz_got(t, 1, False)
                wz(t + 1, 1, t == 2).start()
                wz_got(t, -1, False)
                wz(t + 1, -1, t == 2).start()

        @pl.when(j == 4)
        def _():
            wz_got(3, 1, True)
            wz_got(3, -1, True)
            wx(0).start()
            wx(1).start()
            wsib(x).start()

        @pl.when(j == 7)
        def _():
            wx_got(0)
            wx(2).start()
            wx_got(1)
            wx(3).start()
            wsib(xl_).start()
            wsib(xr_).start()

        @pl.when(j == 10)
        def _():
            wx_got(2)
            wx_got(3)
            wsib(xo_).start()

    stage_tokens(jnp.int32(0))

    def step(j, carry):
        @pl.when(j + 1 < NZ)
        def _():
            stage_tokens(j + 1)

        @pl.when(j < NCH)
        def _():
            stage_rows(j)

        stage_weights(j)

        @pl.when((j >= 1) & (j < NCH + 1))
        def _():
            stage_relay(j - 1)

        @pl.when(j == 2)
        def _():
            for load in loads:
                load.wait()

        @pl.when((j >= 2) & (j < NCH + 2))
        def _():
            stage_experts(j - 2)

        @pl.when((j >= 3) & (j < NCH + 3))
        def _():
            stage_reduce(j - 3)

        @pl.when(j >= 4)
        def _():
            stage_return(j - 4)

        return carry

    lax.fori_loop(0, NCH + 4, step, 0)

    def arrive(k, carry):
        s = lax.rem(e + k, NE)
        send(rbuf.at[s], rbuf.at[s], os_.at[0], or_.at[s], sib, y).wait_recv()
        return carry

    lax.fori_loop(1, NE, arrive, 0)
    res_o[...] = rbuf[...]

    gx.drain()
    for t in range(3):
        whole_up(t).wait_send()
        whole_down(t).wait_send()
    half_up(lax.rem(z + NZ - 3, NZ)).wait_send()
    half_down(lax.rem(z + 3, NZ)).wait_send()
    for t in range(4):
        wz(t, 1, t == 3).wait_send()
        wz(t, -1, t == 3).wait_send()
        wx(t).wait_send()
        wsib(t).wait_send()

    def drain(i, carry):
        @pl.when(i < NZ)
        def _():
            across(i, plane_of(i), c).wait_send()

            def sent(b, inner):
                to, copy = back(i, b)

                @pl.when(to != e)
                def _():
                    copy.wait_send()

                return inner

            lax.fori_loop(0, NX * NC, sent, 0)

        ag(i, 0, y, None, yu).wait_send()
        ag(i, 1, y, None, yd).wait_send()
        ag(i, 2, yd, lo, yu).wait_send()
        ag(i, 3, yu, hi, yd).wait_send()
        for k in range(2):
            rs1(i, k).wait_send()
            rs2(i, k).wait_send()
        return carry

    lax.fori_loop(0, NCH, drain, 0)


def tail(normed, routes, wsh, win, wout):
    dma = pltpu.SemaphoreType.DMA
    vm = pl.BlockSpec(memory_space=pltpu.VMEM)
    hbm = pl.BlockSpec(memory_space=pl.ANY)
    return pl.pallas_call(
        tail_kernel,
        name="routed_and_shared_experts",
        out_shape=[
            jax.ShapeDtypeStruct((NE, SLOT, FEAT), BF16),
            jax.ShapeDtypeStruct((ROWS, FEAT), F32),
        ],
        in_specs=[vm, vm, vm, hbm, hbm],
        out_specs=[vm] * 2,
        scratch_shapes=[
            pltpu.VMEM((NE, ROWS, FEAT), BF16),
            pltpu.VMEM((NE, ROWS), F32),
            pltpu.VMEM((NCH, NY, CHUNK, FEAT), BF16),
            pltpu.VMEM((NCH, NY, CHUNK, FEAT), BF16),
            pltpu.VMEM((NCH, 2, HALF, FEAT), BF16),
            pltpu.VMEM((NCH, 2, CHUNK, FEAT), BF16),
            pltpu.VMEM((NE, 32, 3 * SPAD), BF16),
            pltpu.VMEM((2, QPAD, WIDTH), BF16),
            pltpu.VMEM((QPAD, WIDTH), BF16),
            pltpu.VMEM((NZ, NX * NC, SLOT, FEAT), BF16),
            pltpu.VMEM((NE, SLOT, FEAT), BF16),
            pltpu.VMEM((CHUNK, 2 * SPAD), F32),
            dma((2,)), dma((3,)),
            dma((4,)), dma((4,)),
            dma((8,)), dma((8,)),
            dma((8,)), dma((8,)),
            dma((8,)), dma((8,)),
            dma((4,)), dma((4,)),
            dma((4,)), dma((4,)),
            dma((4, NCH)), dma((4, NCH)),
            dma((4, NCH)), dma((4, NCH)),
            dma((NE,)), dma((NE,)),
        ],
        compiler_params=pltpu.CompilerParams(
            collective_id=1, has_side_effects=True, vmem_limit_bytes=VMEM_LIMIT
        ),
    )(normed, routes, wsh, win, wout)


def combine(logits, route_ids, res):
    ids = jnp.arange(NE, dtype=jnp.int32)
    chosen = jnp.any(route_ids[:, :, None] == ids[None, None, :], axis=1)
    masked = jnp.where(chosen, logits, -jnp.inf)
    weight = jnp.where(chosen, jnp.exp(logits - jnp.max(masked, axis=1, keepdims=True)), 0.0)
    gates = weight / jnp.sum(weight, axis=1, keepdims=True)
    rows = jnp.arange(ROWS, dtype=jnp.int32)
    before = (rows[None, :] < rows[:, None]).astype(BF16)
    rank = jnp.dot(before, chosen.astype(BF16), preferred_element_type=F32)
    lane = jnp.arange(NE * SLOT, dtype=jnp.int32)
    expand = (ids[:, None] == lane[None, :] // SLOT).astype(BF16)
    high = lax.reduce_precision(gates, 8, 7)
    low = gates - high
    stacked = jnp.concatenate(
        [jnp.where(chosen, rank, 255.0).astype(BF16), high.astype(BF16), low.astype(BF16)], axis=0
    )
    wide = jnp.dot(stacked, expand, preferred_element_type=F32).reshape(3, ROWS, NE * SLOT)
    here = wide[0] == (lane % SLOT).astype(F32)[None, :]
    table = jnp.where(here[None], wide[1:], 0.0).astype(BF16)
    out = jnp.dot(
        table.reshape(2 * ROWS, NE * SLOT),
        res.reshape(NE * SLOT, FEAT),
        preferred_element_type=F32,
    )
    return out[:ROWS] + out[ROWS:]


def per_device(
    hidden_state, context, out_proj, norm_gain, router_weight,
    expert_in, expert_out, shared_in, shared_out, route_ids,
):
    ids = jnp.pad(
        route_ids.T.astype(BF16), ((0, 32 - TOP), (0, 0)), constant_values=-1.0
    )
    wsh = jnp.concatenate([out_proj.T, ids], axis=1)
    router = jnp.pad(router_weight, ((0, 0), (0, 128 - NE)))
    gain = norm_gain.astype(F32)[None, :]
    normed, mixed, logits, routes = pre(context, wsh, hidden_state, gain, router)
    gap = ((0, 0), (0, 0), (0, SPAD - SWIDTH))
    shard = jnp.concatenate(
        [
            jnp.pad(shared_in, gap).reshape(32, 2 * SPAD),
            jnp.pad(shared_out.T, ((0, 0), (0, SPAD - SWIDTH))),
        ],
        axis=1,
    )
    win = jnp.transpose(expert_in[0], (1, 2, 0))
    res, shared = tail(normed, routes, shard, win, expert_out[0])
    return mixed + combine(logits[:, :NE], route_ids, res) + shared


def solution(mesh):
    return jax.shard_map(
        per_device,
        mesh=mesh,
        in_specs=(
            P("expert", "mp"),
            P("expert", "mp"),
            P("mp", "expert"),
            P("mp"),
            P("mp", None),
            P("expert", None, None, "mp"),
            P("expert", "mp", None),
            P("expert", None, "mp"),
            P("mp", "expert"),
            P("expert", None),
        ),
        out_specs=P("expert", "mp"),
        check_vma=False,
    )
```

```python
import jax
import jax.numpy as jnp
from jax import lax
from jax.experimental import pallas as pl
from jax.experimental.pallas import tpu as pltpu
from jax.sharding import PartitionSpec as P

NZ, NX, NC, NY = 8, 4, 2, 4
NE = NZ * NX * NC
ROWS, FEAT, WIDTH = 128, 512, 2048
TOP, CAP, PACK, PWIDTH = 6, 20, 16, 640
QUARTER, QPAD = 352, 384
SWIDTH, SPAD = 704, 768
CHUNK = NX * NC * CAP
HALF = CHUNK // 2
NCH = NZ + 1
SHARED_AT = 7
ORDER = sum(d << (3 * k) for k, d in enumerate((0, 7, 1, 6, 5, 4, 3, 2)))
F32, BF16 = jnp.float32, jnp.bfloat16
VMEM_LIMIT = 64 * 1024 * 1024 - 65536


def coords():
    e = lax.axis_index("expert")
    y = lax.axis_index("mp")
    z = lax.div(e, NX * NC)
    x = lax.rem(lax.div(e, NC), NX)
    c = lax.rem(e, NC)
    return e, z, x, c, y


def eid(z, x, c):
    return z * (NX * NC) + x * NC + c


def blk(z, c, x):
    return z * (NX * NC) + c * NX + x


def send(src, dst, ssem, rsem, e, y):
    return pltpu.make_async_remote_copy(
        src_ref=src,
        dst_ref=dst,
        send_sem=ssem,
        recv_sem=rsem,
        device_id={"expert": e, "mp": y},
        device_id_type=pl.DeviceIdType.MESH,
    )


def greet(e, y):
    pl.semaphore_signal(
        pltpu.get_barrier_semaphore(),
        inc=1,
        device_id={"expert": e, "mp": y},
        device_id_type=pl.DeviceIdType.MESH,
    )


def nt(a, b):
    return lax.dot_general(a, b, (((1,), (1,)), ((), ())), preferred_element_type=F32)


def mixer_kernel(
    ctx, opt, ids, hid, gain, router, wsh, win, wout,
    out,
    wga, wgb, part, p1, p2, sq, lg, mixed, shared, tab,
    tok, slot, xg, pb, r1, r2, wb, wi, wo, sbuf, rbuf, acc,
    wsem,
    axs, axr, azs, azr, ass, asr, bzs, bzr, bxs, bxr, bss, bsr,
    ys, yr, qs, qr,
    xs, xr, z0s, z0r, zs, zr, ss, sr,
    wzs, wzr, wxs, wxr, wss, wsr,
    gs, gr, ps, pr, os_, or_,
):
    e, z, x, c, y = coords()
    xr_, xl_, xo_ = lax.rem(x + 1, NX), lax.rem(x + NX - 1, NX), lax.rem(x + 2, NX)
    to_r, to_l = eid(z, xr_, c), eid(z, xl_, c)
    to_u, to_d = eid(lax.rem(z + 1, NZ), x, c), eid(lax.rem(z + NZ - 1, NZ), x, c)
    sib = eid(z, x, 1 - c)
    yu, yd, yo = lax.rem(y + 1, NY), lax.rem(y + NY - 1, NY), lax.rem(y + 2, NY)
    lo, hi = pl.ds(0, HALF), pl.ds(HALF, HALF)
    far = lax.rem(z + 4, NZ)

    def zat(d):
        return lax.rem(z + NZ + d, NZ)

    def hello(k, carry):
        greet(lax.rem(e + k, NE), y)
        return carry

    lax.fori_loop(1, NE, hello, 0)
    for t in (yu, yd, yo):
        greet(e, t)

    loads = [
        pltpu.make_async_copy(win.at[0], wi.at[0, pl.ds(0, QUARTER)], wsem.at[0]),
        pltpu.make_async_copy(win.at[1], wi.at[1, pl.ds(0, QUARTER)], wsem.at[1]),
        pltpu.make_async_copy(wout, wo.at[pl.ds(0, QUARTER)], wsem.at[2]),
    ]
    for load in loads:
        load.start()

    def wblk(zz, cc, xx):
        return cc * (NX * NZ) + xx * NZ + zz

    own, wown = blk(z, c, x), wblk(z, c, x)
    names = jnp.concatenate(
        [ids[...].astype(F32), jnp.full((ROWS - TOP, ROWS), -1.0, F32)], axis=0
    )
    wga[own, :, pl.ds(0, FEAT)] = opt[0:16, :]
    wga[own, :, pl.ds(FEAT, ROWS)] = names[:16].astype(BF16)
    wgb[wown] = opt[16:32, :]
    wb[wown] = wsh[...]
    pl.semaphore_wait(pltpu.get_barrier_semaphore(), NE + 2)

    def ax(k):
        b, to = [(own, to_r), (own, to_l), (blk(z, c, xl_), to_r)][k]
        return send(wga.at[b], wga.at[b], axs.at[k], axr.at[k], to, y)

    def ax_got(k):
        b = blk(z, c, [xl_, xr_, xo_][k])
        send(wga.at[b], wga.at[b], axs.at[k], axr.at[k], to_r, y).wait_recv()

    def a_plane(p, cc, n=NX, off=0):
        return wga.at[pl.ds(p * (NX * NC) + cc * NX + off, n)]

    def az(t, d):
        p = zat(-d * t)
        r = a_plane(p, c) if t < 3 else a_plane(p, c, 2, 0 if d > 0 else 2)
        k = t if d > 0 else 4 + t
        return send(r, r, azs.at[k], azr.at[k], to_u if d > 0 else to_d, y)

    def az_got(t, d):
        p = zat(-d * (t + 1))
        r = a_plane(p, c) if t < 3 else a_plane(p, c, 2, 0 if d > 0 else 2)
        k = t if d > 0 else 4 + t
        send(r, r, azs.at[k], azr.at[k], to_u, y).wait_recv()

    def a_sib(d, cc):
        r = a_plane(zat(d), cc)
        return send(r, r, ass.at[d % NZ], asr.at[d % NZ], sib, y)

    def bz(t, d):
        r = wgb.at[wblk(zat(-d * t), c, x)]
        k = t if d > 0 else 4 + t
        return send(r, r, bzs.at[k], bzr.at[k], to_u if d > 0 else to_d, y)

    def bz_got(t, d):
        r = wgb.at[wblk(zat(-d * (t + 1)), c, x)]
        k = t if d > 0 else 4 + t
        send(r, r, bzs.at[k], bzr.at[k], to_u, y).wait_recv()

    def b_col(xx, cc, n=NZ, off=0):
        return wgb.at[pl.ds(cc * (NX * NZ) + xx * NZ + off, n)]

    def bx(k):
        r, to = [
            (b_col(x, c), to_r), (b_col(x, c), to_l),
            (b_col(xl_, c, 4, 0), to_r), (b_col(xr_, c, 4, 4), to_l),
        ][k]
        return send(r, r, bxs.at[k], bxr.at[k], to, y)

    def bx_got(k):
        r = [b_col(xl_, c), b_col(xr_, c), b_col(xo_, c, 4, 0), b_col(xo_, c, 4, 4)][k]
        send(r, r, bxs.at[k], bxr.at[k], to_r, y).wait_recv()

    xoff = (x, xr_, xo_, xl_)

    def b_sib(k, cc):
        r = b_col(xoff[k], cc)
        return send(r, r, bss.at[k], bsr.at[k], sib, y)

    ax(0).start()
    ax(1).start()
    bz(0, 1).start()
    bz(0, -1).start()
    ax_got(0)
    ax(2).start()
    ax_got(1)
    bz_got(0, 1)
    bz(1, 1).start()
    bz_got(0, -1)
    bz(1, -1).start()
    ax_got(2)
    az(0, 1).start()
    az(0, -1).start()
    a_sib(0, c).start()
    bz_got(1, 1)
    bz(2, 1).start()
    bz_got(1, -1)
    bz(2, -1).start()
    az_got(0, 1)
    az(1, 1).start()
    az_got(0, -1)
    az(1, -1).start()
    a_sib(-1, c).start()
    a_sib(1, c).start()
    bz_got(2, 1)
    bz(3, 1).start()
    bz_got(2, -1)
    az_got(1, 1)
    az(2, 1).start()
    az_got(1, -1)
    az(2, -1).start()
    bz_got(3, 1)
    bx(0).start()
    bx(1).start()
    a_sib(-2, c).start()
    a_sib(2, c).start()
    b_sib(0, c).start()
    az_got(2, 1)
    az(3, 1).start()
    az_got(2, -1)
    az(3, -1).start()
    a_sib(-3, c).start()
    a_sib(3, c).start()
    bx_got(0)
    bx(2).start()
    bx_got(1)
    bx(3).start()
    b_sib(3, c).start()
    b_sib(1, c).start()
    az_got(3, 1)
    az_got(3, -1)
    a_sib(4, c).start()
    bx_got(2)
    bx_got(3)
    b_sib(2, c).start()

    def wz(t, d):
        r = wb.at[wblk(zat(-d * t), c, x)]
        if t == 3:
            r = wb.at[wblk(zat(-d * t), c, x), pl.ds(0 if d > 0 else 16, 16)]
        k = t if d > 0 else 4 + t
        return send(r, r, wzs.at[k], wzr.at[k], to_u if d > 0 else to_d, y)

    def wz_got(t, d):
        r = wb.at[wblk(zat(-d * (t + 1)), c, x)]
        if t == 3:
            r = wb.at[wblk(zat(-d * (t + 1)), c, x), pl.ds(0 if d > 0 else 16, 16)]
        k = t if d > 0 else 4 + t
        send(r, r, wzs.at[k], wzr.at[k], to_u, y).wait_recv()

    def wz_step(t):
        for d in (1, -1):
            wz_got(t - 1, d)
            wz(t, d).start()

    def col(xx, cc, n=NZ, off=0):
        return wb.at[pl.ds(cc * (NX * NZ) + xx * NZ + off, n)]

    def wx(k):
        r, to = [
            (col(x, c), to_r), (col(x, c), to_l),
            (col(xl_, c, 4, 0), to_r), (col(xr_, c, 4, 4), to_l),
        ][k]
        return send(r, r, wxs.at[k], wxr.at[k], to, y)

    def wx_got(k):
        r = [col(xl_, c), col(xr_, c), col(xo_, c, 4, 0), col(xo_, c, 4, 4)][k]
        send(r, r, wxs.at[k], wxr.at[k], to_r, y).wait_recv()

    def wsib(k, cc):
        r = col(xoff[k], cc)
        return send(r, r, wss.at[k], wsr.at[k], sib, y)

    wz(0, 1).start()
    wz(0, -1).start()
    for d in (0, -1, 1, -2, 2, -3, 3, 4):
        a_sib(d, 1 - c).wait_recv()
    for k in range(NX):
        b_sib(k, 1 - c).wait_recv()

    def columns(d):
        blocks = []
        for zz in range(2):
            for xx in range(NX):
                for cc in range(NC):
                    p = 2 * d + zz
                    blocks.append(wga[blk(p, cc, xx), :, pl.ds(0, FEAT)])
                    blocks.append(wgb[wblk(p, cc, xx)])
        return nt(ctx[...], jnp.concatenate(blocks, axis=0))

    hrows = ROWS // 2
    plo, phi = pl.ds(0, hrows), pl.ds(hrows, hrows)

    def pa(k):
        rows, to = [(plo, yu), (phi, yd)][k]
        return send(part.at[yo, rows], p1.at[k], ys.at[k], yr.at[k], e, to)

    def pb2(k):
        to = [yu, yd][k]
        return send(part.at[to], p2.at[k], ys.at[2 + k], yr.at[2 + k], e, to)

    part[yo] = columns(yo)
    pa(0).start()
    pa(1).start()
    part[yu] = columns(yu)
    part[yd] = columns(yd)
    pa(0).wait_recv()
    part[yu, plo] = part[yu, plo] + p1[0]
    pb2(0).start()
    pa(1).wait_recv()
    part[yd, phi] = part[yd, phi] + p1[1]
    pb2(1).start()
    part[y] = columns(y)
    wz_step(1)

    def mark(b, carry):
        same = (wga[b, :, pl.ds(FEAT, ROWS)].astype(F32) == e.astype(F32)).astype(F32)
        slot[pl.ds(b, 1), :] = jnp.sum(same, axis=0, keepdims=True)
        return carry

    lax.fori_loop(0, NE, mark, 0)
    r_i = lax.broadcasted_iota(jnp.int32, (ROWS, ROWS), 0)
    c_i = lax.broadcasted_iota(jnp.int32, (ROWS, ROWS), 1)
    named = slot[...]
    rank = jnp.dot(
        named.astype(BF16), (r_i < c_i).astype(F32).astype(BF16), preferred_element_type=F32
    )
    slot[...] = jnp.where(named > 0.5, rank, -1000.0)
    gap = pl.ds(QUARTER, QPAD - QUARTER)
    wi[0, gap] = jnp.zeros((QPAD - QUARTER, WIDTH), BF16)
    wi[1, gap] = jnp.zeros((QPAD - QUARTER, WIDTH), BF16)
    wo[gap] = jnp.zeros((QPAD - QUARTER, WIDTH), BF16)
    xg[NZ, y, pl.ds(ROWS, CHUNK - ROWS)] = jnp.zeros((CHUNK - ROWS, FEAT), BF16)

    pb2(0).wait_recv()
    pb2(1).wait_recv()
    mix = hid[...].astype(F32) + (part[y] + p2[0] + p2[1])
    mixed[...] = mix

    def spread(buf, base, k):
        return send(
            buf.at[3], buf.at[k], qs.at[base + k], qr.at[base + k], e, (yu, yd, yo)[k]
        )

    sums = jnp.broadcast_to(jnp.sum(mix * mix, axis=1, keepdims=True), (ROWS, ROWS))
    sq[3] = jnp.transpose(sums)[:8]
    for k in range(3):
        spread(sq, 0, k).start()
    wz_step(2)
    for k in range(3):
        spread(sq, 0, k).wait_recv()
    inverse = lax.rsqrt(((sq[0] + sq[1]) + (sq[2] + sq[3])) / WIDTH + 1e-06)
    inverse = jnp.transpose(jnp.broadcast_to(inverse[:1], (ROWS, ROWS)))[:, :1]
    normed32 = mix * inverse * gain[...].astype(F32)
    tok[own] = normed32.astype(BF16)
    xg[NZ, y, pl.ds(0, ROWS)] = normed32.astype(BF16)

    def tx(k):
        half = ROWS // 2
        r, to = [
            (tok.at[own], to_r), (tok.at[own], to_l),
            (tok.at[blk(z, c, xl_), pl.ds(0, half)], to_r),
            (tok.at[blk(z, c, xr_), pl.ds(half, half)], to_l),
        ][k]
        return send(r, r, xs.at[k], xr.at[k], to, y)

    def tx_got(k):
        half = ROWS // 2
        r = [
            tok.at[blk(z, c, xl_)], tok.at[blk(z, c, xr_)],
            tok.at[blk(z, c, xo_), pl.ds(0, half)], tok.at[blk(z, c, xo_), pl.ds(half, half)],
        ][k]
        send(r, r, xs.at[k], xr.at[k], to_r, y).wait_recv()

    def tz0(k, d):
        r = tok.at[blk(z, c, xoff[k])]
        q = k if d > 0 else NX + k
        return send(r, r, z0s.at[q], z0r.at[q], to_u if d > 0 else to_d, y)

    def tz0_got(k, d):
        r = tok.at[blk(zat(-d), c, xoff[k])]
        q = k if d > 0 else NX + k
        send(r, r, z0s.at[q], z0r.at[q], to_u, y).wait_recv()

    def plane(p, cc, n=NX, off=0):
        return tok.at[pl.ds(p * (NX * NC) + cc * NX + off, n)]

    def tz(t, d):
        p = zat(-d * t)
        r = plane(p, c) if t < 3 else plane(p, c, 2, 0 if d > 0 else 2)
        k = t - 1 if d > 0 else 2 + t
        return send(r, r, zs.at[k], zr.at[k], to_u if d > 0 else to_d, y)

    def tz_got(t, d):
        p = zat(-d * (t + 1))
        r = plane(p, c) if t < 3 else plane(p, c, 2, 0 if d > 0 else 2)
        k = t - 1 if d > 0 else 2 + t
        send(r, r, zs.at[k], zr.at[k], to_u, y).wait_recv()

    def across(d, p, cc):
        r = plane(p, cc)
        return send(r, r, ss.at[d], sr.at[d], sib, y)

    def ag(i, k, who, rows, to):
        r = xg.at[i, who] if rows is None else xg.at[i, who, rows]
        return send(r, r, gs.at[k, i], gr.at[k, i], e, to)

    tx(0).start()
    tx(1).start()
    tz0(0, 1).start()
    tz0(0, -1).start()
    ag(NZ, 0, y, None, yu).start()
    ag(NZ, 1, y, None, yd).start()
    wide = jnp.concatenate([router[...], jnp.zeros((ROWS - NE, FEAT), F32)], axis=0)
    lg[3] = lax.dot_general(
        normed32, wide, (((1,), (1,)), ((), ())),
        precision=lax.Precision.HIGHEST, preferred_element_type=F32,
    )
    for k in range(3):
        spread(lg, 3, k).start()
    tx_got(0)
    tx(2).start()
    tz0(3, 1).start()
    tz0(3, -1).start()
    tx_got(1)
    tx(3).start()
    tz0(1, 1).start()
    tz0(1, -1).start()
    tx_got(2)
    tx_got(3)
    tz0(2, 1).start()
    tz0(2, -1).start()
    across(0, z, c).start()
    wz_step(3)

    def ring(t):
        for d in (1, -1):
            if t == 1:
                for k in (0, 3, 1, 2):
                    tz0_got(k, d)
            else:
                tz_got(t - 1, d)
            if t < 4:
                tz(t, d).start()
                p = zat(-d * t)
                across((-d * t) % NZ, p, c).start()
        if t == 4:
            across(4, far, c).start()

    def offset_of(k):
        return lax.shift_right_logical(jnp.int32(ORDER), 3 * k) & 7

    def plane_of(k):
        return lax.rem(z + offset_of(k), NZ)

    def stage_rows(i):
        p = plane_of(i)
        across(offset_of(i), p, 1 - c).wait_recv()
        rows = lax.broadcasted_iota(jnp.int32, (CHUNK, ROWS), 0).astype(F32)
        total = jnp.zeros((CHUNK, FEAT), F32)
        for b in range(0, NX * NC, 2):
            k = p * (NX * NC) + b
            onehot = jnp.concatenate(
                [
                    (rows == slot[pl.ds(k + h, 1), :] + float(CAP * (b + h))).astype(F32)
                    for h in range(2)
                ],
                axis=1,
            ).astype(BF16)
            pair = tok[pl.ds(k, 2)].reshape(2 * ROWS, FEAT)
            total = total + jnp.dot(onehot, pair, preferred_element_type=F32)
        xg[i, y] = total.astype(BF16)
        ag(i, 0, y, None, yu).start()
        ag(i, 1, y, None, yd).start()

    def stage_relay(i):
        ag(i, 0, yd, None, yu).wait_recv()
        ag(i, 2, yd, lo, yu).start()
        ag(i, 1, yu, None, yd).wait_recv()
        ag(i, 3, yu, hi, yd).start()

    def rs1(i, k):
        rows, to = (lo, yu) if k == 0 else (hi, yd)
        return send(pb.at[i, yo, rows], r1.at[i, k], ps.at[k, i], pr.at[k, i], e, to)

    def rs2(i, k):
        to = yu if k == 0 else yd
        return send(pb.at[i, to], r2.at[i, k], ps.at[2 + k, i], pr.at[2 + k, i], e, to)

    def gated(gate, value):
        return (gate / (1.0 + jnp.exp(-gate)) * value).astype(BF16)

    def stage_experts(i):
        ag(i, 2, yo, lo, yu).wait_recv()
        ag(i, 3, yo, hi, yd).wait_recv()
        both = []
        for h in range(2):
            total = jnp.zeros((CHUNK, QPAD), F32)
            for k in range(NY):
                total = total + nt(xg[i, k], wi[h, :, k * FEAT : (k + 1) * FEAT])
            both.append(total)
        hidden = gated(both[0], both[1])

        def down(k, carry):
            d = lax.rem(yo + k, NY)
            w = wo[:, pl.ds(pl.multiple_of(d * FEAT, FEAT), FEAT)]
            pb[i, d] = jnp.dot(hidden, w, preferred_element_type=F32).astype(BF16)
            return carry

        lax.fori_loop(0, 1, down, 0)
        rs1(i, 0).start()
        rs1(i, 1).start()
        lax.fori_loop(1, NY, down, 0)

    def stage_shared():
        ag(NZ, 2, yo, lo, yu).wait_recv()
        ag(NZ, 3, yo, hi, yd).wait_recv()
        for k in range(NX):
            wsib(k, 1 - c).wait_recv()
        acc[...] = jnp.zeros((ROWS, 2 * SPAD), F32)

        def into(zz, carry):
            w = jnp.concatenate(
                [
                    wb[wblk(zz, cc, xx), :, pl.ds(0, 2 * SPAD)]
                    for xx in range(NX)
                    for cc in range(NC)
                ],
                axis=0,
            )
            off = pl.multiple_of(lax.rem(zz, 2) * 256, 256)
            acc[...] += jnp.dot(
                xg[NZ, lax.div(zz, 2), pl.ds(0, ROWS), pl.ds(off, 256)],
                w,
                preferred_element_type=F32,
            )
            return carry

        lax.fori_loop(0, NZ, into, 0)
        hidden = gated(acc[:, :SPAD], acc[:, SPAD:])

        def project(k, carry):
            d = lax.rem(yo + k, NY)
            w = jnp.concatenate(
                [
                    wb[wblk(2 * d + zz, cc, xx), :, pl.ds(2 * SPAD, SPAD)]
                    for zz in range(2)
                    for xx in range(NX)
                    for cc in range(NC)
                ],
                axis=0,
            )
            pb[NZ, d, pl.ds(0, ROWS)] = nt(hidden, w).astype(BF16)
            pb[NZ, d, pl.ds(ROWS, CHUNK - ROWS)] = jnp.zeros((CHUNK - ROWS, FEAT), BF16)
            return carry

        lax.fori_loop(0, NY, project, 0)
        rs1(NZ, 0).start()
        rs1(NZ, 1).start()

    def stage_reduce(i):
        rs1(i, 0).wait_recv()
        pb[i, yu, lo] = (pb[i, yu, lo].astype(F32) + r1[i, 0].astype(F32)).astype(BF16)
        rs2(i, 0).start()
        rs1(i, 1).wait_recv()
        pb[i, yd, hi] = (pb[i, yd, hi].astype(F32) + r1[i, 1].astype(F32)).astype(BF16)
        rs2(i, 1).start()

    def back(i, b):
        to = eid(plane_of(i), lax.rem(b, NX), lax.div(b, NX))
        return to, send(sbuf.at[i, b], rbuf.at[e], os_.at[i * (NX * NC) + b], or_.at[e], to, y)

    def reduced(i):
        rs2(i, 0).wait_recv()
        rs2(i, 1).wait_recv()
        return pb[i, y].astype(F32) + r2[i, 0].astype(F32) + r2[i, 1].astype(F32)

    def stage_return(i):
        total = reduced(i).astype(BF16)
        to_row = lax.broadcasted_iota(jnp.int32, (ROWS, CHUNK), 0)
        of_row = lax.broadcasted_iota(jnp.int32, (ROWS, CHUNK), 1)
        base = CAP * lax.shift_right_logical(to_row, 4)
        inner = to_row & (PACK - 1)

        def move(hit, values):
            return jnp.dot(hit.astype(F32).astype(BF16), values, preferred_element_type=F32)

        first = move(of_row == base + inner, total)
        sbuf[i, :, :, pl.ds(0, FEAT)] = first.astype(BF16).reshape(NX * NC, PACK, FEAT)
        last = jnp.zeros((ROWS, ROWS), F32)
        for q in range(4):
            hit = (of_row == base + PACK + inner - 4 * q) & (inner >= 4 * q) & (inner < 4 * q + 4)
            last = last + move(hit, total[:, q * 128 : (q + 1) * 128])
        sbuf[i, :, :, pl.ds(FEAT, 128)] = last.astype(BF16).reshape(NX * NC, PACK, 128)

        def go(b, carry):
            to, copy = back(i, b)

            @pl.when(to != e)
            def _():
                copy.start()

            @pl.when(to == e)
            def _():
                rbuf[e] = sbuf[i, b]

            return carry

        lax.fori_loop(0, NX * NC, go, 0)

    def stage_tables():
        for k in range(3):
            spread(lg, 3, k).wait_recv()
        logits = (lg[0] + lg[1]) + (lg[2] + lg[3])
        mine = jnp.transpose(names)
        lane = c_i.astype(F32)
        count = jnp.zeros((ROWS, ROWS), F32)
        for k in range(TOP):
            count = count + (mine[:, k : k + 1] == lane).astype(F32)
        chosen = count > 0.5
        top = jnp.max(jnp.where(chosen, logits, -jnp.inf), axis=1, keepdims=True)
        weight = jnp.where(chosen, jnp.exp(jnp.where(chosen, logits - top, 0.0)), 0.0)
        gates = weight / jnp.sum(weight, axis=1, keepdims=True)
        place = jnp.dot(
            (c_i < r_i).astype(F32).astype(BF16), count.astype(BF16), preferred_element_type=F32
        )
        place = jnp.where(chosen, place, 255.0).astype(BF16)
        high = gates.astype(BF16)
        low = (gates - high.astype(F32)).astype(BF16)

        def fill(b, carry):
            ee = lax.broadcasted_iota(jnp.int32, (ROWS, 256), 0)
            jj = lax.broadcasted_iota(jnp.int32, (ROWS, 256), 1)
            inner = jj & (PACK - 1)
            mat = (ee == lax.shift_right_logical(jj, 4) + b * PACK).astype(F32).astype(BF16)
            where = jnp.dot(place, mat, preferred_element_type=F32)
            at = pl.ds(pl.multiple_of(b * 256, 256), 256)
            for h, g in enumerate((high, low)):
                spaced = jnp.dot(g, mat, preferred_element_type=F32)
                for q, want in enumerate((inner, PACK + (inner & 3))):
                    hit = jnp.where(where == want.astype(F32), spaced, 0.0)
                    tab[q, pl.ds(h * ROWS, ROWS), at] = hit.astype(BF16)
            return carry

        lax.fori_loop(0, NE * PACK // 256, fill, 0)

    def step(j, carry):
        @pl.when(j < NZ)
        def _():
            stage_rows(j)

        @pl.when(j == 0)
        def _():
            stage_relay(NZ)
            for d in (1, -1):
                wz_got(3, d)
            wx(0).start()
            wx(1).start()
            wsib(0, c).start()
            for load in loads:
                load.wait()

        @pl.when(j == 3)
        def _():
            wx_got(0)
            wx(2).start()
            wx_got(1)
            wx(3).start()
            wsib(3, c).start()
            wsib(1, c).start()

        @pl.when(j == 5)
        def _():
            wx_got(2)
            wx_got(3)
            wsib(2, c).start()

        @pl.when((j >= 1) & (j < NZ + 1))
        def _():
            stage_relay(j - 1)

        @pl.when((j >= 2) & (j < NZ + 2))
        def _():
            stage_experts(j - 2)

        @pl.when((j >= 3) & (j < NZ + 3))
        def _():
            stage_reduce(j - 3)

        @pl.when(j >= 4)
        def _():
            stage_return(j - 4)

        @pl.when(j == 1)
        def _():
            stage_tables()

        @pl.when(j == SHARED_AT)
        def _():
            stage_shared()

        @pl.when(j == SHARED_AT + 1)
        def _():
            stage_reduce(NZ)

        @pl.when(j == SHARED_AT + 2)
        def _():
            shared[...] = reduced(NZ)[:ROWS]

        for t, at in ((1, 0), (2, 2), (3, 3), (4, 4)):

            @pl.when(j == at)
            def _(t=t):
                ring(t)

        return carry

    lax.fori_loop(0, NZ + 4, step, 0)

    def arrive(k, carry):
        s = lax.rem(e + k, NE)
        send(rbuf.at[s], rbuf.at[s], os_.at[0], or_.at[s], sib, y).wait_recv()
        return carry

    lax.fori_loop(1, NE, arrive, 0)
    back_rows = rbuf[:, :, pl.ds(0, FEAT)].reshape(NE * PACK, FEAT)
    pieces = rbuf[:, :, pl.ds(FEAT, 128)].reshape(NE * PACK, 128).astype(F32)
    part_of = lax.shift_right_logical(
        lax.broadcasted_iota(jnp.int32, (NE * PACK, 128), 0) & (PACK - 1), 2
    )
    extra = jnp.concatenate(
        [jnp.where(part_of == q, pieces, 0.0).astype(BF16) for q in range(4)], axis=1
    )
    both = jnp.dot(tab[0], back_rows, preferred_element_type=F32) + jnp.dot(
        tab[1], extra, preferred_element_type=F32
    )
    out[...] = mixed[...] + (both[:ROWS] + both[ROWS:]) + shared[...]

    for k in range(3):
        ax(k).wait_send()
        spread(sq, 0, k).wait_send()
        spread(lg, 3, k).wait_send()
    for t in range(4):
        for d in (1, -1):
            az(t, d).wait_send()
            if t < 3 or d > 0:
                bz(t, d).wait_send()
            wz(t, d).wait_send()
            tz0(t, d).wait_send()
            if t > 0:
                tz(t, d).wait_send()
        bx(t).wait_send()
        b_sib(t, c).wait_send()
        wx(t).wait_send()
        wsib(t, c).wait_send()
        tx(t).wait_send()
    for d in (0, -1, 1, -2, 2, -3, 3, 4):
        a_sib(d, c).wait_send()
    for k in range(2):
        pa(k).wait_send()
        pb2(k).wait_send()

    def drain(i, carry):
        @pl.when(i < NZ)
        def _():
            across(i, lax.rem(z + i, NZ), c).wait_send()

            def sent(b, inner):
                to, copy = back(i, b)

                @pl.when(to != e)
                def _():
                    copy.wait_send()

                return inner

            lax.fori_loop(0, NX * NC, sent, 0)

        ag(i, 0, y, None, yu).wait_send()
        ag(i, 1, y, None, yd).wait_send()
        ag(i, 2, yd, lo, yu).wait_send()
        ag(i, 3, yu, hi, yd).wait_send()
        for k in range(2):
            rs1(i, k).wait_send()
            rs2(i, k).wait_send()
        return carry

    lax.fori_loop(0, NCH, drain, 0)


def mixer(ctx, opt, ids, hid, gain, router, wsh, win, wout):
    vm = pl.BlockSpec(memory_space=pltpu.VMEM)
    hbm = pl.BlockSpec(memory_space=pl.ANY)

    def pairs(*shapes):
        return [pltpu.SemaphoreType.DMA(s) for s in shapes for _ in range(2)]

    return pl.pallas_call(
        mixer_kernel,
        name="mixer_tail",
        out_shape=jax.ShapeDtypeStruct((ROWS, FEAT), F32),
        in_specs=[vm] * 7 + [hbm] * 2,
        out_specs=vm,
        scratch_shapes=[
            pltpu.VMEM((NE, 16, FEAT + ROWS), BF16),
            pltpu.VMEM((NE, 16, FEAT), BF16),
            pltpu.VMEM((NY, ROWS, FEAT), F32),
            pltpu.VMEM((2, ROWS // 2, FEAT), F32),
            pltpu.VMEM((2, ROWS, FEAT), F32),
            pltpu.VMEM((4, 8, ROWS), F32),
            pltpu.VMEM((4, ROWS, ROWS), F32),
            pltpu.VMEM((ROWS, FEAT), F32),
            pltpu.VMEM((ROWS, FEAT), F32),
            pltpu.VMEM((2, 2 * ROWS, NE * PACK), BF16),
            pltpu.VMEM((NE, ROWS, FEAT), BF16),
            pltpu.VMEM((NE, ROWS), F32),
            pltpu.VMEM((NCH, NY, CHUNK, FEAT), BF16),
            pltpu.VMEM((NCH, NY, CHUNK, FEAT), BF16),
            pltpu.VMEM((NCH, 2, HALF, FEAT), BF16),
            pltpu.VMEM((NCH, 2, CHUNK, FEAT), BF16),
            pltpu.VMEM((NE, 32, 3 * SPAD), BF16),
            pltpu.VMEM((2, QPAD, WIDTH), BF16),
            pltpu.VMEM((QPAD, WIDTH), BF16),
            pltpu.VMEM((NZ, NX * NC, PACK, PWIDTH), BF16),
            pltpu.VMEM((NE, PACK, PWIDTH), BF16),
            pltpu.VMEM((ROWS, 2 * SPAD), F32),
            pltpu.SemaphoreType.DMA((3,)),
        ]
        + pairs((3,), (8,), (8,), (8,), (4,), (4,), (4,), (6,))
        + pairs((4,), (8,), (6,), (8,), (8,), (4,), (4,))
        + pairs((4, NCH), (4, NCH), (NE,)),
        compiler_params=pltpu.CompilerParams(
            collective_id=0, has_side_effects=True, vmem_limit_bytes=VMEM_LIMIT
        ),
    )(ctx, opt, ids, hid, gain, router, wsh, win, wout)


def per_device(
    hidden_state, context, out_proj, norm_gain, router_weight,
    expert_in, expert_out, shared_in, shared_out, route_ids,
):
    gap = ((0, 0), (0, 0), (0, SPAD - SWIDTH))
    shard = jnp.concatenate(
        [
            jnp.pad(shared_in, gap).reshape(32, 2 * SPAD),
            jnp.pad(shared_out.T, ((0, 0), (0, SPAD - SWIDTH))),
        ],
        axis=1,
    )
    win = jnp.transpose(expert_in[0], (1, 2, 0))
    return mixer(
        context, out_proj.T, route_ids.T, hidden_state, norm_gain[None, :],
        router_weight.T, shard, win, expert_out[0],
    )


def solution(mesh):
    return jax.shard_map(
        per_device,
        mesh=mesh,
        in_specs=(
            P("expert", "mp"),
            P("expert", "mp"),
            P("mp", "expert"),
            P("mp"),
            P("mp", None),
            P("expert", None, None, "mp"),
            P("expert", "mp", None),
            P("expert", None, "mp"),
            P("mp", "expert"),
            P("expert", None),
        ),
        out_specs=P("expert", "mp"),
        check_vma=False,
    )
```

```python
import jax
import jax.numpy as jnp
from jax import lax
from jax.experimental import pallas as pl
from jax.experimental.pallas import tpu as pltpu
from jax.sharding import PartitionSpec as P

NZ, NX, NC, NY = 8, 4, 2, 4
NE = NZ * NX * NC
ROWS, FEAT, WIDTH = 128, 512, 2048
TOP, CAP, PACK, PWIDTH = 6, 20, 16, 640
QUARTER, QPAD = 352, 768
EIGHTH = QUARTER // 2
SWIDTH, SPAD = 704, 768
CHUNK = NX * NC * CAP
HALF = CHUNK // 2
SHARED_AT = 8
ORDER = sum(d << (3 * k) for k, d in enumerate((0, 7, 1, 2, 5, 4, 3, 6)))
F32, BF16 = jnp.float32, jnp.bfloat16
VMEM_LIMIT = 64 * 1024 * 1024 - 65536


def coords():
    e = lax.axis_index("expert")
    y = lax.axis_index("mp")
    z = lax.div(e, NX * NC)
    x = lax.rem(lax.div(e, NC), NX)
    c = lax.rem(e, NC)
    return e, z, x, c, y


def eid(z, x, c):
    return z * (NX * NC) + x * NC + c


def blk(z, c, x):
    return z * (NX * NC) + c * NX + x


def send(src, dst, ssem, rsem, e, y):
    return pltpu.make_async_remote_copy(
        src_ref=src,
        dst_ref=dst,
        send_sem=ssem,
        recv_sem=rsem,
        device_id={"expert": e, "mp": y},
        device_id_type=pl.DeviceIdType.MESH,
    )


def greet(e, y):
    pl.semaphore_signal(
        pltpu.get_barrier_semaphore(),
        inc=1,
        device_id={"expert": e, "mp": y},
        device_id_type=pl.DeviceIdType.MESH,
    )


def nt(a, b):
    return lax.dot_general(a, b, (((1,), (1,)), ((), ())), preferred_element_type=F32)


def mixer_kernel(
    ctx, opt, ids, hid, gain, router, wsh, win, wout,
    out, base_o,
    wga, wgb, part, p1, p2, sq, lg, mixed, shared, tab,
    tok, slot, xo, xg, tr, pb, ra, rb, tq, xsh, psh, s1, s2,
    wb, wi, wo, sbuf, rbuf, acc, tot,
    wsem,
    axs, axr, azs, azr, ass, asr, bzs, bzr, bxs, bxr, bss, bsr,
    ys, yr, qs, qr,
    xs, xr, z0s, z0r, zs, zr, ss, sr,
    wzs, wzr, wxs, wxr, wss, wsr,
    hs, hr, gs, gr, ps, pr, vs, vr, os_, or_,
):
    e, z, x, c, y = coords()
    xr_, xl_, xo_ = lax.rem(x + 1, NX), lax.rem(x + NX - 1, NX), lax.rem(x + 2, NX)
    to_r, to_l = eid(z, xr_, c), eid(z, xl_, c)
    to_u, to_d = eid(lax.rem(z + 1, NZ), x, c), eid(lax.rem(z + NZ - 1, NZ), x, c)
    sib = eid(z, x, 1 - c)
    yu, yd, yo = lax.rem(y + 1, NY), lax.rem(y + NY - 1, NY), lax.rem(y + 2, NY)
    left_, right_ = pl.ds(0, 256), pl.ds(256, 256)
    par = lax.rem(y, 2)
    mine = pl.ds(pl.multiple_of(par * HALF, 16), HALF)
    other = pl.ds(pl.multiple_of((1 - par) * HALF, 16), HALF)
    near = y + 1 - 2 * par
    next_ = lax.rem(y + 3 + 2 * par, NY)
    far = lax.rem(z + 4, NZ)

    def zat(d):
        return lax.rem(z + NZ + d, NZ)

    def hello(k, carry):
        greet(lax.rem(e + k, NE), y)
        return carry

    lax.fori_loop(1, NE, hello, 0)
    for t in (yu, yd, yo):
        greet(e, t)

    loads = [
        pltpu.make_async_copy(win.at[0], wi.at[0, pl.ds(0, QUARTER)], wsem.at[0]),
        pltpu.make_async_copy(win.at[1], wi.at[1, pl.ds(0, QUARTER)], wsem.at[1]),
        pltpu.make_async_copy(wout, wo.at[pl.ds(0, QUARTER)], wsem.at[2]),
    ]
    for load in loads:
        load.start()

    def wblk(zz, cc, xx):
        return cc * (NX * NZ) + xx * NZ + zz

    own, wown = blk(z, c, x), wblk(z, c, x)
    names = jnp.concatenate(
        [ids[...].astype(F32), jnp.full((ROWS - TOP, ROWS), -1.0, F32)], axis=0
    )
    wga[own, :, pl.ds(0, FEAT)] = opt[0:16, :]
    wga[own, :, pl.ds(FEAT, ROWS)] = names[:16].astype(BF16)
    wgb[wown] = opt[16:32, :]
    wb[wown] = wsh[...]
    pl.semaphore_wait(pltpu.get_barrier_semaphore(), NE + 2)

    def pair(k):
        src, dst, at, to, n, where = (
            (win.at[0], wi.at[0], 0, near, EIGHTH, QUARTER),
            (win.at[0], wi.at[0], EIGHTH, next_, EIGHTH, QUARTER + EIGHTH),
            (win.at[1], wi.at[1], 0, near, 80, QUARTER),
            (win.at[1], wi.at[1], EIGHTH, next_, 80, QUARTER + EIGHTH),
            (win.at[1], wi.at[1], 80, near, EIGHTH - 80, QUARTER + 80),
            (win.at[1], wi.at[1], EIGHTH + 80, next_, EIGHTH - 80, QUARTER + EIGHTH + 80),
            (wout, wo, 0, near, EIGHTH, QUARTER),
            (wout, wo, EIGHTH, next_, EIGHTH, QUARTER + EIGHTH),
        )[k]
        return send(src.at[pl.ds(at, n)], dst.at[pl.ds(where, n)], hs.at[k], hr.at[k], e, to)

    def ax(k):
        b, to = [(own, to_r), (own, to_l), (blk(z, c, xl_), to_r)][k]
        return send(wga.at[b], wga.at[b], axs.at[k], axr.at[k], to, y)

    def ax_got(k):
        b = blk(z, c, [xl_, xr_, xo_][k])
        send(wga.at[b], wga.at[b], axs.at[k], axr.at[k], to_r, y).wait_recv()

    def a_plane(p, cc, n=NX, off=0):
        return wga.at[pl.ds(p * (NX * NC) + cc * NX + off, n)]

    def az(t, d):
        p = zat(-d * t)
        r = a_plane(p, c) if t < 3 else a_plane(p, c, 2, 0 if d > 0 else 2)
        k = t if d > 0 else 4 + t
        return send(r, r, azs.at[k], azr.at[k], to_u if d > 0 else to_d, y)

    def az_got(t, d):
        p = zat(-d * (t + 1))
        r = a_plane(p, c) if t < 3 else a_plane(p, c, 2, 0 if d > 0 else 2)
        k = t if d > 0 else 4 + t
        send(r, r, azs.at[k], azr.at[k], to_u, y).wait_recv()

    def a_sib(d, cc):
        r = a_plane(zat(d), cc)
        return send(r, r, ass.at[d % NZ], asr.at[d % NZ], sib, y)

    def bz(t, d):
        r = wgb.at[wblk(zat(-d * t), c, x)]
        k = t if d > 0 else 4 + t
        return send(r, r, bzs.at[k], bzr.at[k], to_u if d > 0 else to_d, y)

    def bz_got(t, d):
        r = wgb.at[wblk(zat(-d * (t + 1)), c, x)]
        k = t if d > 0 else 4 + t
        send(r, r, bzs.at[k], bzr.at[k], to_u, y).wait_recv()

    def b_col(xx, cc, n=NZ, off=0):
        return wgb.at[pl.ds(cc * (NX * NZ) + xx * NZ + off, n)]

    def bx(k):
        r, to = [
            (b_col(x, c), to_r), (b_col(x, c), to_l),
            (b_col(xl_, c, 4, 0), to_r), (b_col(xr_, c, 4, 4), to_l),
        ][k]
        return send(r, r, bxs.at[k], bxr.at[k], to, y)

    def bx_got(k):
        r = [b_col(xl_, c), b_col(xr_, c), b_col(xo_, c, 4, 0), b_col(xo_, c, 4, 4)][k]
        send(r, r, bxs.at[k], bxr.at[k], to_r, y).wait_recv()

    xoff = (x, xr_, xo_, xl_)

    def b_sib(k, cc):
        r = b_col(xoff[k], cc)
        return send(r, r, bss.at[k], bsr.at[k], sib, y)

    for k in range(4):
        pair(k).start()
    ax(0).start()
    ax(1).start()
    bz(0, 1).start()
    bz(0, -1).start()
    ax_got(0)
    ax(2).start()
    ax_got(1)
    bz_got(0, 1)
    bz(1, 1).start()
    bz_got(0, -1)
    bz(1, -1).start()
    ax_got(2)
    az(0, 1).start()
    az(0, -1).start()
    a_sib(0, c).start()
    bz_got(1, 1)
    bz(2, 1).start()
    bz_got(1, -1)
    bz(2, -1).start()
    az_got(0, 1)
    az(1, 1).start()
    az_got(0, -1)
    az(1, -1).start()
    a_sib(-1, c).start()
    a_sib(1, c).start()
    bz_got(2, 1)
    bz(3, 1).start()
    bz_got(2, -1)
    az_got(1, 1)
    az(2, 1).start()
    az_got(1, -1)
    az(2, -1).start()
    bz_got(3, 1)
    bx(0).start()
    bx(1).start()
    a_sib(-2, c).start()
    a_sib(2, c).start()
    b_sib(0, c).start()
    az_got(2, 1)
    az(3, 1).start()
    az_got(2, -1)
    az(3, -1).start()
    a_sib(-3, c).start()
    a_sib(3, c).start()
    bx_got(0)
    bx(2).start()
    bx_got(1)
    bx(3).start()
    b_sib(3, c).start()
    b_sib(1, c).start()
    az_got(3, 1)
    az_got(3, -1)
    a_sib(4, c).start()
    bx_got(2)
    bx_got(3)
    b_sib(2, c).start()

    def wz(t, d):
        r = wb.at[wblk(zat(-d * t), c, x)]
        if t == 3:
            r = wb.at[wblk(zat(-d * t), c, x), pl.ds(0 if d > 0 else 16, 16)]
        k = t if d > 0 else 4 + t
        return send(r, r, wzs.at[k], wzr.at[k], to_u if d > 0 else to_d, y)

    def wz_got(t, d):
        r = wb.at[wblk(zat(-d * (t + 1)), c, x)]
        if t == 3:
            r = wb.at[wblk(zat(-d * (t + 1)), c, x), pl.ds(0 if d > 0 else 16, 16)]
        k = t if d > 0 else 4 + t
        send(r, r, wzs.at[k], wzr.at[k], to_u, y).wait_recv()

    def wz_step(t):
        for d in (1, -1):
            wz_got(t - 1, d)
            wz(t, d).start()

    def col(xx, cc, n=NZ, off=0):
        return wb.at[pl.ds(cc * (NX * NZ) + xx * NZ + off, n)]

    def wx(k):
        r, to = [
            (col(x, c), to_r), (col(x, c), to_l),
            (col(xl_, c, 4, 0), to_r), (col(xr_, c, 4, 4), to_l),
        ][k]
        return send(r, r, wxs.at[k], wxr.at[k], to, y)

    def wx_got(k):
        r = [col(xl_, c), col(xr_, c), col(xo_, c, 4, 0), col(xo_, c, 4, 4)][k]
        send(r, r, wxs.at[k], wxr.at[k], to_r, y).wait_recv()

    def wsib(k, cc):
        r = col(xoff[k], cc)
        return send(r, r, wss.at[k], wsr.at[k], sib, y)

    wz(0, 1).start()
    wz(0, -1).start()
    for d in (0, -1, 1, -2, 2, -3, 3, 4):
        a_sib(d, 1 - c).wait_recv()
    for k in range(NX):
        b_sib(k, 1 - c).wait_recv()

    def columns(d):
        blocks = []
        for zz in range(2):
            for xx in range(NX):
                for cc in range(NC):
                    p = 2 * d + zz
                    blocks.append(wga[blk(p, cc, xx), :, pl.ds(0, FEAT)])
                    blocks.append(wgb[wblk(p, cc, xx)])
        return nt(ctx[...], jnp.concatenate(blocks, axis=0))

    hrows = ROWS // 2
    plo, phi = pl.ds(0, hrows), pl.ds(hrows, hrows)

    def pa(k):
        rows, to = [(plo, yu), (phi, yd)][k]
        return send(part.at[yo, rows], p1.at[k], ys.at[k], yr.at[k], e, to)

    def pb2(k):
        to = [yu, yd][k]
        return send(part.at[to], p2.at[k], ys.at[2 + k], yr.at[2 + k], e, to)

    part[yo] = columns(yo)
    pa(0).start()
    pa(1).start()
    part[yu] = columns(yu)
    part[yd] = columns(yd)
    pa(0).wait_recv()
    part[yu, plo] = part[yu, plo] + p1[0]
    pb2(0).start()
    pa(1).wait_recv()
    part[yd, phi] = part[yd, phi] + p1[1]
    pb2(1).start()
    part[y] = columns(y)
    wz_step(1)

    def mark(b, carry):
        same = (wga[b, :, pl.ds(FEAT, ROWS)].astype(F32) == e.astype(F32)).astype(F32)
        slot[pl.ds(b, 1), :] = jnp.sum(same, axis=0, keepdims=True)
        return carry

    lax.fori_loop(0, NE, mark, 0)
    r_i = lax.broadcasted_iota(jnp.int32, (ROWS, ROWS), 0)
    c_i = lax.broadcasted_iota(jnp.int32, (ROWS, ROWS), 1)
    named = slot[...]
    rank = jnp.dot(
        named.astype(BF16), (r_i < c_i).astype(F32).astype(BF16), preferred_element_type=F32
    )
    slot[...] = jnp.where(named > 0.5, rank, -1000.0)
    gap = pl.ds(2 * QUARTER, QPAD - 2 * QUARTER)
    wi[0, gap] = jnp.zeros((QPAD - 2 * QUARTER, WIDTH), BF16)
    wi[1, gap] = jnp.zeros((QPAD - 2 * QUARTER, WIDTH), BF16)
    wo[gap] = jnp.zeros((QPAD - 2 * QUARTER, WIDTH), BF16)

    pb2(0).wait_recv()
    pb2(1).wait_recv()
    mix = hid[...].astype(F32) + (part[y] + p2[0] + p2[1])
    mixed[...] = mix

    def spread(buf, base, k):
        return send(
            buf.at[3], buf.at[k], qs.at[base + k], qr.at[base + k], e, (yu, yd, yo)[k]
        )

    sums = jnp.broadcast_to(jnp.sum(mix * mix, axis=1, keepdims=True), (ROWS, ROWS))
    sq[3] = jnp.transpose(sums)[:8]
    for k in range(3):
        spread(sq, 0, k).start()
    for k in range(4, 8):
        pair(k).start()
    wz_step(2)
    for k in range(3):
        spread(sq, 0, k).wait_recv()
    inverse = lax.rsqrt(((sq[0] + sq[1]) + (sq[2] + sq[3])) / WIDTH + 1e-06)
    inverse = jnp.transpose(jnp.broadcast_to(inverse[:1], (ROWS, ROWS)))[:, :1]
    normed32 = mix * inverse * gain[...].astype(F32)
    tok[own] = normed32.astype(BF16)
    xsh[y] = normed32.astype(BF16)

    def tx(k):
        half = ROWS // 2
        r, to = [
            (tok.at[own], to_r), (tok.at[own], to_l),
            (tok.at[blk(z, c, xl_), pl.ds(0, half)], to_r),
            (tok.at[blk(z, c, xr_), pl.ds(half, half)], to_l),
        ][k]
        return send(r, r, xs.at[k], xr.at[k], to, y)

    def tx_got(k):
        half = ROWS // 2
        r = [
            tok.at[blk(z, c, xl_)], tok.at[blk(z, c, xr_)],
            tok.at[blk(z, c, xo_), pl.ds(0, half)], tok.at[blk(z, c, xo_), pl.ds(half, half)],
        ][k]
        send(r, r, xs.at[k], xr.at[k], to_r, y).wait_recv()

    def tz0(k, d):
        r = tok.at[blk(z, c, xoff[k])]
        q = k if d > 0 else NX + k
        return send(r, r, z0s.at[q], z0r.at[q], to_u if d > 0 else to_d, y)

    def tz0_got(k, d):
        r = tok.at[blk(zat(-d), c, xoff[k])]
        q = k if d > 0 else NX + k
        send(r, r, z0s.at[q], z0r.at[q], to_u, y).wait_recv()

    def plane(p, cc, n=NX, off=0):
        return tok.at[pl.ds(p * (NX * NC) + cc * NX + off, n)]

    def tz(t, d):
        p = zat(-d * t)
        r = plane(p, c) if t < 3 else plane(p, c, 2, 0 if d > 0 else 2)
        k = t - 1 if d > 0 else 2 + t
        return send(r, r, zs.at[k], zr.at[k], to_u if d > 0 else to_d, y)

    def tz_got(t, d):
        p = zat(-d * (t + 1))
        r = plane(p, c) if t < 3 else plane(p, c, 2, 0 if d > 0 else 2)
        k = t - 1 if d > 0 else 2 + t
        send(r, r, zs.at[k], zr.at[k], to_u, y).wait_recv()

    def across(d, p, cc):
        r = plane(p, cc)
        return send(r, r, ss.at[d], sr.at[d], sib, y)

    def ag(i, k, copy=True):
        src, dst, to = (
            (xo.at[i, other], xg.at[i, y if copy else yd], yu),
            (xo.at[i, other], xg.at[i, y if copy else yu], yd),
            (xo.at[i, mine, left_], tr.at[i, 0], yu),
            (xo.at[i, mine, right_], tr.at[i, 1], yd),
            (tr.at[i, 0], xg.at[i, yd if copy else yo, :, left_], yu),
            (tr.at[i, 1], xg.at[i, yu if copy else yo, :, right_], yd),
        )[k]
        return send(src, dst, gs.at[k, i], gr.at[k, i], e, to)

    def rs(i, k):
        src, dst, to = (
            (pb.at[i, yu], ra.at[i, 0], yu),
            (pb.at[i, yd], ra.at[i, 1], yd),
            (pb.at[i, yo, :, left_], tq.at[i, 0], yu),
            (pb.at[i, yo, :, right_], tq.at[i, 1], yd),
            (tq.at[i, 0], rb.at[i, :, left_], yu),
            (tq.at[i, 1], rb.at[i, :, right_], yd),
        )[k]
        return send(src, dst, ps.at[k, i], pr.at[k, i], e, to)

    def sh(k, who=None):
        src, dst, to = (
            (xsh.at[y], xsh.at[y if who is None else who], yu),
            (xsh.at[y], xsh.at[y if who is None else who], yd),
            (xsh.at[yd, plo], xsh.at[yd if who is None else who, plo], yu),
            (xsh.at[yu, phi], xsh.at[yu if who is None else who, phi], yd),
            (psh.at[yo, plo], s1.at[0], yu),
            (psh.at[yo, phi], s1.at[1], yd),
            (psh.at[yu], s2.at[0], yu),
            (psh.at[yd], s2.at[1], yd),
        )[k]
        return send(src, dst, vs.at[k], vr.at[k], e, to)

    tx(0).start()
    tx(1).start()
    tz0(0, 1).start()
    tz0(0, -1).start()
    sh(0).start()
    sh(1).start()
    wide = jnp.concatenate([router[...], jnp.zeros((ROWS - NE, FEAT), F32)], axis=0)
    lg[3] = lax.dot_general(
        normed32, wide, (((1,), (1,)), ((), ())),
        precision=lax.Precision.HIGHEST, preferred_element_type=F32,
    )
    for k in range(3):
        spread(lg, 3, k).start()
    tx_got(0)
    tx(2).start()
    tz0(3, 1).start()
    tz0(3, -1).start()
    tx_got(1)
    tx(3).start()
    tz0(1, 1).start()
    tz0(1, -1).start()
    tx_got(2)
    tx_got(3)
    tz0(2, 1).start()
    tz0(2, -1).start()
    across(0, z, c).start()

    def ring(t):
        for d in (1, -1):
            if t == 1:
                for k in (0, 3, 1, 2):
                    tz0_got(k, d)
            else:
                tz_got(t - 1, d)
            if t < 4:
                tz(t, d).start()
                p = zat(-d * t)
                across((-d * t) % NZ, p, c).start()
        if t == 4:
            across(4, far, c).start()

    def offset_of(k):
        return lax.shift_right_logical(jnp.int32(ORDER), 3 * k) & 7

    def plane_of(k):
        return lax.rem(z + offset_of(k), NZ)

    def stage_rows(i):
        p = plane_of(i)
        across(offset_of(i), p, 1 - c).wait_recv()
        rows = lax.broadcasted_iota(jnp.int32, (CHUNK, ROWS), 0).astype(F32)
        total = jnp.zeros((CHUNK, FEAT), F32)
        for b in range(0, NX * NC, 2):
            k = p * (NX * NC) + b
            onehot = jnp.concatenate(
                [
                    (rows == slot[pl.ds(k + h, 1), :] + float(CAP * (b + h))).astype(F32)
                    for h in range(2)
                ],
                axis=1,
            ).astype(BF16)
            pair = tok[pl.ds(k, 2)].reshape(2 * ROWS, FEAT)
            total = total + jnp.dot(onehot, pair, preferred_element_type=F32)
        xo[i] = total.astype(BF16)
        for k in (2, 3, 0, 1):
            ag(i, k).start()
        xg[i, y] = xo[i, mine]

    def stage_relay(i):
        for k in (2, 3):
            ag(i, k, False).wait_recv()
            ag(i, k + 2).start()

    def gated(gate, value):
        return (gate / (1.0 + jnp.exp(-gate)) * value).astype(BF16)

    def stage_experts(i):
        for k in (0, 1, 4, 5):
            ag(i, k, False).wait_recv()
        both = []
        for h in range(2):
            total = jnp.zeros((HALF, QPAD), F32)
            for k in range(NY):
                total = total + nt(xg[i, k], wi[h, :, k * FEAT : (k + 1) * FEAT])
            both.append(total)
        hidden = gated(both[0], both[1])

        def down(k, carry):
            d = lax.rem(yo + k, NY)
            w = wo[:, pl.ds(pl.multiple_of(d * FEAT, FEAT), FEAT)]
            pb[i, d] = jnp.dot(hidden, w, preferred_element_type=F32).astype(BF16)
            return carry

        lax.fori_loop(0, 1, down, 0)
        rs(i, 2).start()
        rs(i, 3).start()
        lax.fori_loop(1, NY, down, 0)
        rs(i, 0).start()
        rs(i, 1).start()

    def stage_shared():
        sh(2, yo).wait_recv()
        sh(3, yo).wait_recv()
        for k in range(NX):
            wsib(k, 1 - c).wait_recv()
        acc[...] = jnp.zeros((ROWS, 2 * SPAD), F32)

        def into(zz, carry):
            w = jnp.concatenate(
                [
                    wb[wblk(zz, cc, xx), :, pl.ds(0, 2 * SPAD)]
                    for xx in range(NX)
                    for cc in range(NC)
                ],
                axis=0,
            )
            off = pl.multiple_of(lax.rem(zz, 2) * 256, 256)
            acc[...] += jnp.dot(
                xsh[lax.div(zz, 2), :, pl.ds(off, 256)],
                w,
                preferred_element_type=F32,
            )
            return carry

        lax.fori_loop(0, NZ, into, 0)
        hidden = gated(acc[:, :SPAD], acc[:, SPAD:])

        def project(k, carry):
            d = lax.rem(yo + k, NY)
            w = jnp.concatenate(
                [
                    wb[wblk(2 * d + zz, cc, xx), :, pl.ds(2 * SPAD, SPAD)]
                    for zz in range(2)
                    for xx in range(NX)
                    for cc in range(NC)
                ],
                axis=0,
            )
            psh[d] = nt(hidden, w).astype(BF16)
            return carry

        lax.fori_loop(0, NY, project, 0)
        sh(4).start()
        sh(5).start()

    def stage_reduce(i):
        for k in (2, 3):
            rs(i, k).wait_recv()
            rs(i, k + 2).start()

    def shared_relay():
        sh(0, yd).wait_recv()
        sh(2).start()
        sh(1, yu).wait_recv()
        sh(3).start()

    def shared_reduce():
        sh(4).wait_recv()
        psh[yu, plo] = (psh[yu, plo].astype(F32) + s1[0].astype(F32)).astype(BF16)
        sh(6).start()
        sh(5).wait_recv()
        psh[yd, phi] = (psh[yd, phi].astype(F32) + s1[1].astype(F32)).astype(BF16)
        sh(7).start()

    def shared_total():
        sh(6).wait_recv()
        sh(7).wait_recv()
        shared[...] = psh[y].astype(F32) + s2[0].astype(F32) + s2[1].astype(F32)

    def back(i, b):
        to = eid(plane_of(i), lax.rem(b, NX), lax.div(b, NX))
        return to, send(sbuf.at[i, b], rbuf.at[e], os_.at[i * (NX * NC) + b], or_.at[e], to, y)

    def stage_return(i):
        for k in (0, 1, 4, 5):
            rs(i, k).wait_recv()
        tot[mine] = pb[i, y].astype(F32) + rb[i].astype(F32)
        tot[other] = ra[i, 0].astype(F32) + ra[i, 1].astype(F32)
        total = tot[...].astype(BF16)
        to_row = lax.broadcasted_iota(jnp.int32, (ROWS, CHUNK), 0)
        of_row = lax.broadcasted_iota(jnp.int32, (ROWS, CHUNK), 1)
        base = CAP * lax.shift_right_logical(to_row, 4)
        inner = to_row & (PACK - 1)

        def move(hit, values):
            return jnp.dot(hit.astype(F32).astype(BF16), values, preferred_element_type=F32)

        first = move(of_row == base + inner, total)
        sbuf[i, :, :, pl.ds(0, FEAT)] = first.astype(BF16).reshape(NX * NC, PACK, FEAT)
        last = jnp.zeros((ROWS, ROWS), F32)
        for q in range(4):
            hit = (of_row == base + PACK + inner - 4 * q) & (inner >= 4 * q) & (inner < 4 * q + 4)
            last = last + move(hit, total[:, q * 128 : (q + 1) * 128])
        sbuf[i, :, :, pl.ds(FEAT, 128)] = last.astype(BF16).reshape(NX * NC, PACK, 128)

        def go(b, carry):
            to, copy = back(i, b)

            @pl.when(to != e)
            def _():
                copy.start()

            @pl.when(to == e)
            def _():
                rbuf[e] = sbuf[i, b]

            return carry

        lax.fori_loop(0, NX * NC, go, 0)

    def stage_tables():
        for k in range(3):
            spread(lg, 3, k).wait_recv()
        logits = (lg[0] + lg[1]) + (lg[2] + lg[3])
        mine = jnp.transpose(names)
        lane = c_i.astype(F32)
        count = jnp.zeros((ROWS, ROWS), F32)
        for k in range(TOP):
            count = count + (mine[:, k : k + 1] == lane).astype(F32)
        chosen = count > 0.5
        top = jnp.max(jnp.where(chosen, logits, -jnp.inf), axis=1, keepdims=True)
        weight = jnp.where(chosen, jnp.exp(jnp.where(chosen, logits - top, 0.0)), 0.0)
        gates = weight / jnp.sum(weight, axis=1, keepdims=True)
        place = jnp.dot(
            (c_i < r_i).astype(F32).astype(BF16), count.astype(BF16), preferred_element_type=F32
        )
        place = jnp.where(chosen, place, 255.0).astype(BF16)
        high = gates.astype(BF16)
        low = (gates - high.astype(F32)).astype(BF16)

        def fill(b, carry):
            ee = lax.broadcasted_iota(jnp.int32, (ROWS, 256), 0)
            jj = lax.broadcasted_iota(jnp.int32, (ROWS, 256), 1)
            inner = jj & (PACK - 1)
            mat = (ee == lax.shift_right_logical(jj, 4) + b * PACK).astype(F32).astype(BF16)
            where = jnp.dot(place, mat, preferred_element_type=F32)
            at = pl.ds(pl.multiple_of(b * 256, 256), 256)
            for h, g in enumerate((high, low)):
                spaced = jnp.dot(g, mat, preferred_element_type=F32)
                for q, want in enumerate((inner, PACK + (inner & 3))):
                    hit = jnp.where(where == want.astype(F32), spaced, 0.0)
                    tab[q, pl.ds(h * ROWS, ROWS), at] = hit.astype(BF16)
            return carry

        lax.fori_loop(0, NE * PACK // 256, fill, 0)

    def step(j, carry):
        @pl.when(j < NZ)
        def _():
            stage_rows(j)

        @pl.when(j == 0)
        def _():
            shared_relay()
            wz_step(3)

        @pl.when(j == 1)
        def _():
            for d in (1, -1):
                wz_got(3, d)
            wx(0).start()
            wx(1).start()
            wsib(0, c).start()

        @pl.when(j == 5)
        def _():
            wx_got(0)
            wx(2).start()
            wx_got(1)
            wx(3).start()
            wsib(3, c).start()
            wsib(1, c).start()

        @pl.when(j == 7)
        def _():
            wx_got(2)
            wx_got(3)
            wsib(2, c).start()

        @pl.when((j >= 1) & (j < NZ + 1))
        def _():
            stage_relay(j - 1)

        @pl.when(j == 2)
        def _():
            for load in loads:
                load.wait()
            for k in range(8):
                pair(k).wait_recv()

        @pl.when((j >= 2) & (j < NZ + 2))
        def _():
            stage_experts(j - 2)

        @pl.when((j >= 3) & (j < NZ + 3))
        def _():
            stage_reduce(j - 3)

        @pl.when(j >= 4)
        def _():
            stage_return(j - 4)

        @pl.when(j == 1)
        def _():
            stage_tables()

        @pl.when(j == SHARED_AT)
        def _():
            stage_shared()

        @pl.when(j == SHARED_AT + 1)
        def _():
            shared_reduce()

        @pl.when(j == SHARED_AT + 2)
        def _():
            shared_total()

        for t, at in ((1, 0), (2, 2), (3, 3), (4, 4)):

            @pl.when(j == at)
            def _(t=t):
                ring(t)

        return carry

    lax.fori_loop(0, NZ + 4, step, 0)

    def arrive(k, carry):
        s = lax.rem(e + k, NE)
        send(rbuf.at[s], rbuf.at[s], os_.at[0], or_.at[s], sib, y).wait_recv()
        return carry

    lax.fori_loop(1, NE, arrive, 0)
    back_rows = rbuf[:, :, pl.ds(0, FEAT)].reshape(NE * PACK, FEAT)
    pieces = rbuf[:, :, pl.ds(FEAT, 128)].reshape(NE * PACK, 128).astype(F32)
    part_of = lax.shift_right_logical(
        lax.broadcasted_iota(jnp.int32, (NE * PACK, 128), 0) & (PACK - 1), 2
    )
    extra = jnp.concatenate(
        [jnp.where(part_of == q, pieces, 0.0).astype(BF16) for q in range(4)], axis=1
    )
    both = jnp.dot(tab[0], back_rows, preferred_element_type=F32) + jnp.dot(
        tab[1], extra, preferred_element_type=F32
    )
    base_o[...] = mixed[...] + shared[...]
    out[...] = both[:ROWS] + both[ROWS:]

    for k in range(3):
        ax(k).wait_send()
        spread(sq, 0, k).wait_send()
        spread(lg, 3, k).wait_send()
    for t in range(4):
        for d in (1, -1):
            az(t, d).wait_send()
            if t < 3 or d > 0:
                bz(t, d).wait_send()
            wz(t, d).wait_send()
            tz0(t, d).wait_send()
            if t > 0:
                tz(t, d).wait_send()
        bx(t).wait_send()
        b_sib(t, c).wait_send()
        wx(t).wait_send()
        wsib(t, c).wait_send()
        tx(t).wait_send()
    for d in (0, -1, 1, -2, 2, -3, 3, 4):
        a_sib(d, c).wait_send()
    for k in range(2):
        pa(k).wait_send()
        pb2(k).wait_send()

    def drain(i, carry):
        across(i, lax.rem(z + i, NZ), c).wait_send()

        def sent(b, inner):
            to, copy = back(i, b)

            @pl.when(to != e)
            def _():
                copy.wait_send()

            return inner

        lax.fori_loop(0, NX * NC, sent, 0)
        for k in range(6):
            ag(i, k).wait_send()
            rs(i, k).wait_send()
        return carry

    lax.fori_loop(0, NZ, drain, 0)
    for k in range(8):
        pair(k).wait_send()
        sh(k).wait_send()


def mixer(ctx, opt, ids, hid, gain, router, wsh, win, wout):
    vm = pl.BlockSpec(memory_space=pltpu.VMEM)
    hbm = pl.BlockSpec(memory_space=pl.ANY)

    def pairs(*shapes):
        return [pltpu.SemaphoreType.DMA(s) for s in shapes for _ in range(2)]

    return pl.pallas_call(
        mixer_kernel,
        name="mixer_tail",
        out_shape=[jax.ShapeDtypeStruct((ROWS, FEAT), F32)] * 2,
        in_specs=[vm] * 7 + [hbm] * 2,
        out_specs=[vm] * 2,
        scratch_shapes=[
            pltpu.VMEM((NE, 16, FEAT + ROWS), BF16),
            pltpu.VMEM((NE, 16, FEAT), BF16),
            pltpu.VMEM((NY, ROWS, FEAT), F32),
            pltpu.VMEM((2, ROWS // 2, FEAT), F32),
            pltpu.VMEM((2, ROWS, FEAT), F32),
            pltpu.VMEM((4, 8, ROWS), F32),
            pltpu.VMEM((4, ROWS, ROWS), F32),
            pltpu.VMEM((ROWS, FEAT), F32),
            pltpu.VMEM((ROWS, FEAT), F32),
            pltpu.VMEM((2, 2 * ROWS, NE * PACK), BF16),
            pltpu.VMEM((NE, ROWS, FEAT), BF16),
            pltpu.VMEM((NE, ROWS), F32),
            pltpu.VMEM((NZ, CHUNK, FEAT), BF16),
            pltpu.VMEM((NZ, NY, HALF, FEAT), BF16),
            pltpu.VMEM((NZ, 2, HALF, 256), BF16),
            pltpu.VMEM((NZ, NY, HALF, FEAT), BF16),
            pltpu.VMEM((NZ, 2, HALF, FEAT), BF16),
            pltpu.VMEM((NZ, HALF, FEAT), BF16),
            pltpu.VMEM((NZ, 2, HALF, 256), BF16),
            pltpu.VMEM((NY, ROWS, FEAT), BF16),
            pltpu.VMEM((NY, ROWS, FEAT), BF16),
            pltpu.VMEM((2, ROWS // 2, FEAT), BF16),
            pltpu.VMEM((2, ROWS, FEAT), BF16),
            pltpu.VMEM((NE, 32, 3 * SPAD), BF16),
            pltpu.VMEM((2, QPAD, WIDTH), BF16),
            pltpu.VMEM((QPAD, WIDTH), BF16),
            pltpu.VMEM((NZ, NX * NC, PACK, PWIDTH), BF16),
            pltpu.VMEM((NE, PACK, PWIDTH), BF16),
            pltpu.VMEM((ROWS, 2 * SPAD), F32),
            pltpu.VMEM((CHUNK, FEAT), F32),
            pltpu.SemaphoreType.DMA((3,)),
        ]
        + pairs((3,), (8,), (8,), (8,), (4,), (4,), (4,), (6,))
        + pairs((4,), (8,), (6,), (8,), (8,), (4,), (4,))
        + pairs((8,), (6, NZ), (6, NZ), (8,), (NE,)),
        compiler_params=pltpu.CompilerParams(
            collective_id=0, has_side_effects=True, vmem_limit_bytes=VMEM_LIMIT
        ),
    )(ctx, opt, ids, hid, gain, router, wsh, win, wout)


def per_device(
    hidden_state, context, out_proj, norm_gain, router_weight,
    expert_in, expert_out, shared_in, shared_out, route_ids,
):
    gap = ((0, 0), (0, 0), (0, SPAD - SWIDTH))
    shard = jnp.concatenate(
        [
            jnp.pad(shared_in, gap).reshape(32, 2 * SPAD),
            jnp.pad(shared_out.T, ((0, 0), (0, SPAD - SWIDTH))),
        ],
        axis=1,
    )
    win = jnp.transpose(expert_in[0], (1, 2, 0))
    routed, base = mixer(
        context, out_proj.T, route_ids.T, hidden_state, norm_gain[None, :],
        router_weight.T, shard, win, expert_out[0],
    )
    return base + routed


def solution(mesh):
    return jax.shard_map(
        per_device,
        mesh=mesh,
        in_specs=(
            P("expert", "mp"),
            P("expert", "mp"),
            P("mp", "expert"),
            P("mp"),
            P("mp", None),
            P("expert", None, None, "mp"),
            P("expert", "mp", None),
            P("expert", None, "mp"),
            P("mp", "expert"),
            P("expert", None),
        ),
        out_specs=P("expert", "mp"),
        check_vma=False,
    )
```

```python
import jax
import jax.numpy as jnp
from jax import lax
from jax.experimental import pallas as pl
from jax.experimental.pallas import tpu as pltpu
from jax.sharding import PartitionSpec as P

NZ, NX, NC, NY = 8, 4, 2, 4
NE = NZ * NX * NC
ROWS, FEAT, WIDTH = 128, 512, 2048
TOP, CAP, PACK, PWIDTH = 6, 20, 16, 640
QUARTER, QPAD = 352, 768
EIGHTH = QUARTER // 2
SWIDTH, SPAD = 704, 768
CHUNK = NX * NC * CAP
HALF = CHUNK // 2
SHARED_AT = 7
BXRIGHT = (True, True, True, False, False, False, False, True)
ORDER = sum(d << (3 * k) for k, d in enumerate((0, 6, 2, 5, 4, 3, 7, 1)))
F32, BF16 = jnp.float32, jnp.bfloat16
VMEM_LIMIT = 64 * 1024 * 1024 - 65536


def coords():
    e = lax.axis_index("expert")
    y = lax.axis_index("mp")
    z = lax.div(e, NX * NC)
    x = lax.rem(lax.div(e, NC), NX)
    c = lax.rem(e, NC)
    return e, z, x, c, y


def eid(z, x, c):
    return z * (NX * NC) + x * NC + c


def blk(z, c, x):
    return z * (NX * NC) + c * NX + x


def send(src, dst, ssem, rsem, e, y):
    return pltpu.make_async_remote_copy(
        src_ref=src,
        dst_ref=dst,
        send_sem=ssem,
        recv_sem=rsem,
        device_id={"expert": e, "mp": y},
        device_id_type=pl.DeviceIdType.MESH,
    )


def greet(e, y):
    pl.semaphore_signal(
        pltpu.get_barrier_semaphore(),
        inc=1,
        device_id={"expert": e, "mp": y},
        device_id_type=pl.DeviceIdType.MESH,
    )


def nt(a, b):
    return lax.dot_general(a, b, (((1,), (1,)), ((), ())), preferred_element_type=F32)


def mixer_kernel(
    ctx, opt, ids, hid, gain, router, wsh, win, wout,
    out, base_o,
    wga, wgb, part, p1, p2, sq, lg, mixed, shared, tab,
    tok, slot, xo, xg, tr, pb, ra, rb, tq, xsh, psh, s1, s2,
    wb, wi, wo, sbuf, rbuf, acc, tot,
    wsem,
    axs, axr, azs, azr, ass, asr, bzs, bzr, bxs, bxr, bss, bsr,
    ys, yr, qs, qr,
    xs, xr, z0s, z0r, zs, zr, ss, sr,
    wzs, wzr, wxs, wxr, wss, wsr,
    hs, hr, gs, gr, ps, pr, vs, vr, os_, or_,
):
    e, z, x, c, y = coords()
    xr_, xl_, xo_ = lax.rem(x + 1, NX), lax.rem(x + NX - 1, NX), lax.rem(x + 2, NX)
    to_r, to_l = eid(z, xr_, c), eid(z, xl_, c)
    to_u, to_d = eid(lax.rem(z + 1, NZ), x, c), eid(lax.rem(z + NZ - 1, NZ), x, c)
    sib = eid(z, x, 1 - c)
    yu, yd, yo = lax.rem(y + 1, NY), lax.rem(y + NY - 1, NY), lax.rem(y + 2, NY)
    left_, right_ = pl.ds(0, 256), pl.ds(256, 256)
    par = lax.rem(y, 2)
    mine = pl.ds(pl.multiple_of(par * HALF, 16), HALF)
    other = pl.ds(pl.multiple_of((1 - par) * HALF, 16), HALF)
    near = y + 1 - 2 * par
    next_ = lax.rem(y + 3 + 2 * par, NY)
    far = lax.rem(z + 4, NZ)

    def zat(d):
        return lax.rem(z + NZ + d, NZ)

    def hello(k, carry):
        greet(lax.rem(e + k, NE), y)
        return carry

    lax.fori_loop(1, NE, hello, 0)
    for t in (yu, yd, yo):
        greet(e, t)

    loads = [
        pltpu.make_async_copy(win.at[0], wi.at[0, pl.ds(0, QUARTER)], wsem.at[0]),
        pltpu.make_async_copy(win.at[1], wi.at[1, pl.ds(0, QUARTER)], wsem.at[1]),
        pltpu.make_async_copy(wout, wo.at[pl.ds(0, QUARTER)], wsem.at[2]),
    ]
    for load in loads:
        load.start()

    def wblk(zz, cc, xx):
        return cc * (NX * NZ) + xx * NZ + zz

    own, wown = blk(z, c, x), wblk(z, c, x)
    names = jnp.concatenate(
        [ids[...].astype(F32), jnp.full((ROWS - TOP, ROWS), -1.0, F32)], axis=0
    )
    wga[own, :, pl.ds(0, FEAT)] = opt[0:16, :]
    wga[own, :, pl.ds(FEAT, ROWS)] = names[:16].astype(BF16)
    wgb[wown] = opt[16:32, :]
    wb[wown] = wsh[...]
    pl.semaphore_wait(pltpu.get_barrier_semaphore(), NE + 2)

    def pair(k):
        src, dst, at, to, n, where = (
            (win.at[0], wi.at[0], 0, near, EIGHTH, QUARTER),
            (win.at[0], wi.at[0], EIGHTH, next_, EIGHTH, QUARTER + EIGHTH),
            (win.at[1], wi.at[1], 0, near, 80, QUARTER),
            (win.at[1], wi.at[1], EIGHTH, next_, 80, QUARTER + EIGHTH),
            (win.at[1], wi.at[1], 80, near, EIGHTH - 80, QUARTER + 80),
            (win.at[1], wi.at[1], EIGHTH + 80, next_, EIGHTH - 80, QUARTER + EIGHTH + 80),
            (wout, wo, 0, near, EIGHTH, QUARTER),
            (wout, wo, EIGHTH, next_, EIGHTH, QUARTER + EIGHTH),
        )[k]
        return send(src.at[pl.ds(at, n)], dst.at[pl.ds(where, n)], hs.at[k], hr.at[k], e, to)

    xoff = (x, xr_, xo_, xl_)

    def ax(k):
        b, to = [(own, to_r), (own, to_l), (blk(z, c, xl_), to_r)][k]
        return send(wga.at[b], wga.at[b], axs.at[k], axr.at[k], to, y)

    def ax_got(k):
        b = blk(z, c, [xl_, xr_, xo_][k])
        send(wga.at[b], wga.at[b], axs.at[k], axr.at[k], to_r, y).wait_recv()

    def az(k, t, d, hop=0):
        r = wga.at[blk(zat(-d * (t + hop)), c, xoff[k])]
        q = (t if d > 0 else 4 + t) * NX + k
        return send(r, r, azs.at[q], azr.at[q], to_u if d > 0 else to_d, y)

    def az_goes(k, t, d):
        return t < 3 or (k < 2) == (d > 0)

    def a_sib(d, cc):
        r = wga.at[pl.ds(zat(d) * (NX * NC) + cc * NX, NX)]
        return send(r, r, ass.at[d % NZ], asr.at[d % NZ], sib, y)

    def bz(t, d, hop=0):
        r = wgb.at[wblk(zat(-d * (t + hop)), c, x)]
        q = t if d > 0 else 4 + t
        return send(r, r, bzs.at[q], bzr.at[q], to_u if d > 0 else to_d, y)

    def bx(q, k, copy=True):
        right = BXRIGHT[q]
        src, dst, to = (
            (x, xl_, to_r), (x, xr_, to_l), (xl_ if right else xr_, xo_, to_r if right else to_l),
        )[k]
        r = wgb.at[wblk(lax.rem(z + q, NZ), c, src if copy else dst)]
        return send(r, r, bxs.at[k, q], bxr.at[k, q], to, y)

    def b_sib(k, cc):
        r = wgb.at[pl.ds(cc * (NX * NZ) + xoff[k] * NZ, NZ)]
        return send(r, r, bss.at[k], bsr.at[k], sib, y)

    pair(0).start()
    pair(1).start()
    events = []

    def at(when, *args):
        events.append((when, len(events), args))

    level = 1.9
    begun = {0: 0.0, 3: level, 1: level, 2: 2 * level}
    at(0, "ax", 0)
    at(0, "ax", 1)
    at(level, "axl")
    at(level, "axr")
    at(2 * level, "axo")
    for t in range(4):
        for k, q in ((0, 0), (3, 1), (1, 2), (2, 3)):
            for d in (1, -1):
                if az_goes(k, t, d):
                    at(begun[k] + (t + 1) * level + 0.15 * q, "az", k, t, d)
    at(begun[2] + 4 * level + 0.5, "asib", 4)
    for d in (1, -1):
        at(0, "bz0", d)
        for t in range(4):
            if t < 3 or d > 0:
                at((t + 1) * level, "bz", t, d)
    for q in range(NZ):
        seen = min(q, NZ - q) * level
        at(seen + 0.01, "bx", q)
        at(seen + level + 0.1, "bxl", q)
        at(seen + level + 0.1, "bxr", q)
        at(seen + 2 * level + 0.2, "bxo", q)
    at(4 * level + 0.02, "bsib", 0)
    at(5 * level + 0.12, "bsib", 3)
    at(5 * level + 0.12, "bsib", 1)
    at(6 * level + 0.22, "bsib", 2)
    for _, _, (what, *v) in sorted(events):
        if what == "ax":
            ax(v[0]).start()
            if v[0] == 0:
                az(0, 0, 1).start()
                az(0, 0, -1).start()
        elif what in ("axl", "axr", "axo"):
            n = ("axl", "axr", "axo").index(what)
            ax_got(n)
            if n == 0:
                ax(2).start()
            k = (3, 1, 2)[n]
            az(k, 0, 1).start()
            az(k, 0, -1).start()
            if n == 2:
                a_sib(0, c).start()
        elif what == "az":
            k, t, d = v
            az(k, t, d, 1).wait_recv()
            if t < 3 and az_goes(k, t + 1, d):
                az(k, t + 1, d).start()
            if t < 3 and k == 2:
                a_sib(-d * (t + 1), c).start()
        elif what == "asib":
            a_sib(v[0], c).start()
        elif what == "bz0":
            bz(0, v[0]).start()
        elif what == "bz":
            t, d = v
            bz(t, d, 1).wait_recv()
            if t < 2 or (t == 2 and d > 0):
                bz(t + 1, d).start()
        elif what == "bx":
            bx(v[0], 0).start()
            bx(v[0], 1).start()
        elif what in ("bxl", "bxr"):
            n = ("bxl", "bxr").index(what)
            bx(v[0], n, False).wait_recv()
            if BXRIGHT[v[0]] == (n == 0):
                bx(v[0], 2).start()
        elif what == "bxo":
            bx(v[0], 2, False).wait_recv()
        else:
            b_sib(v[0], c).start()

    def wz(t, d):
        r = wb.at[wblk(zat(-d * t), c, x)]
        if t == 3:
            r = wb.at[wblk(zat(-d * t), c, x), pl.ds(0 if d > 0 else 16, 16)]
        k = t if d > 0 else 4 + t
        return send(r, r, wzs.at[k], wzr.at[k], to_u if d > 0 else to_d, y)

    def wz_got(t, d):
        r = wb.at[wblk(zat(-d * (t + 1)), c, x)]
        if t == 3:
            r = wb.at[wblk(zat(-d * (t + 1)), c, x), pl.ds(0 if d > 0 else 16, 16)]
        k = t if d > 0 else 4 + t
        send(r, r, wzs.at[k], wzr.at[k], to_u, y).wait_recv()

    def wz_step(t):
        for d in (1, -1):
            wz_got(t - 1, d)
            wz(t, d).start()

    def col(xx, cc, n=NZ, off=0):
        return wb.at[pl.ds(cc * (NX * NZ) + xx * NZ + off, n)]

    def wx(k):
        r, to = [
            (col(x, c), to_r), (col(x, c), to_l),
            (col(xl_, c, 4, 0), to_r), (col(xr_, c, 4, 4), to_l),
        ][k]
        return send(r, r, wxs.at[k], wxr.at[k], to, y)

    def wx_got(k):
        r = [col(xl_, c), col(xr_, c), col(xo_, c, 4, 0), col(xo_, c, 4, 4)][k]
        send(r, r, wxs.at[k], wxr.at[k], to_r, y).wait_recv()

    def wsib(k, cc):
        r = col(xoff[k], cc)
        return send(r, r, wss.at[k], wsr.at[k], sib, y)

    wz(0, 1).start()
    wz(0, -1).start()
    for d in (0, -1, 1, -2, 2, -3, 3, 4):
        a_sib(d, 1 - c).wait_recv()
    for k in range(NX):
        b_sib(k, 1 - c).wait_recv()

    def columns(d):
        blocks = []
        for zz in range(2):
            for xx in range(NX):
                for cc in range(NC):
                    p = 2 * d + zz
                    blocks.append(wga[blk(p, cc, xx), :, pl.ds(0, FEAT)])
                    blocks.append(wgb[wblk(p, cc, xx)])
        return nt(ctx[...], jnp.concatenate(blocks, axis=0))

    hrows = ROWS // 2
    plo, phi = pl.ds(0, hrows), pl.ds(hrows, hrows)

    def pa(k):
        rows, to = [(plo, yu), (phi, yd)][k]
        return send(part.at[yo, rows], p1.at[k], ys.at[k], yr.at[k], e, to)

    def pb2(k):
        to = [yu, yd][k]
        return send(part.at[to], p2.at[k], ys.at[2 + k], yr.at[2 + k], e, to)

    part[yo] = columns(yo)
    pa(0).start()
    pa(1).start()
    part[yu] = columns(yu)
    part[yd] = columns(yd)
    pa(0).wait_recv()
    part[yu, plo] = part[yu, plo] + p1[0]
    pb2(0).start()
    pa(1).wait_recv()
    part[yd, phi] = part[yd, phi] + p1[1]
    pb2(1).start()
    part[y] = columns(y)
    wz_step(1)

    def mark(b, carry):
        same = (wga[b, :, pl.ds(FEAT, ROWS)].astype(F32) == e.astype(F32)).astype(F32)
        slot[pl.ds(b, 1), :] = jnp.sum(same, axis=0, keepdims=True)
        return carry

    lax.fori_loop(0, NE, mark, 0)
    r_i = lax.broadcasted_iota(jnp.int32, (ROWS, ROWS), 0)
    c_i = lax.broadcasted_iota(jnp.int32, (ROWS, ROWS), 1)
    named = slot[...]
    rank = jnp.dot(
        named.astype(BF16), (r_i < c_i).astype(F32).astype(BF16), preferred_element_type=F32
    )
    slot[...] = jnp.where(named > 0.5, rank, -1000.0)
    gap = pl.ds(2 * QUARTER, QPAD - 2 * QUARTER)
    wi[0, gap] = jnp.zeros((QPAD - 2 * QUARTER, WIDTH), BF16)
    wi[1, gap] = jnp.zeros((QPAD - 2 * QUARTER, WIDTH), BF16)
    wo[gap] = jnp.zeros((QPAD - 2 * QUARTER, WIDTH), BF16)

    pb2(0).wait_recv()
    pb2(1).wait_recv()
    mix = hid[...].astype(F32) + (part[y] + p2[0] + p2[1])
    mixed[...] = mix

    def spread(buf, base, k):
        return send(
            buf.at[3], buf.at[k], qs.at[base + k], qr.at[base + k], e, (yu, yd, yo)[k]
        )

    sums = jnp.broadcast_to(jnp.sum(mix * mix, axis=1, keepdims=True), (ROWS, ROWS))
    sq[3] = jnp.transpose(sums)[:8]
    for k in range(3):
        spread(sq, 0, k).start()
    for k in range(2, 8):
        pair(k).start()
    wz_step(2)
    for k in range(3):
        spread(sq, 0, k).wait_recv()
    inverse = lax.rsqrt(((sq[0] + sq[1]) + (sq[2] + sq[3])) / WIDTH + 1e-06)
    inverse = jnp.transpose(jnp.broadcast_to(inverse[:1], (ROWS, ROWS)))[:, :1]
    normed32 = mix * inverse * gain[...].astype(F32)
    tok[own] = normed32.astype(BF16)
    xsh[y] = normed32.astype(BF16)

    def tx(k):
        half = ROWS // 2
        r, to = [
            (tok.at[own], to_r), (tok.at[own], to_l),
            (tok.at[blk(z, c, xl_), pl.ds(0, half)], to_r),
            (tok.at[blk(z, c, xr_), pl.ds(half, half)], to_l),
        ][k]
        return send(r, r, xs.at[k], xr.at[k], to, y)

    def tx_got(k):
        half = ROWS // 2
        r = [
            tok.at[blk(z, c, xl_)], tok.at[blk(z, c, xr_)],
            tok.at[blk(z, c, xo_), pl.ds(0, half)], tok.at[blk(z, c, xo_), pl.ds(half, half)],
        ][k]
        send(r, r, xs.at[k], xr.at[k], to_r, y).wait_recv()

    def tz0(k, d):
        r = tok.at[blk(z, c, xoff[k])]
        q = k if d > 0 else NX + k
        return send(r, r, z0s.at[q], z0r.at[q], to_u if d > 0 else to_d, y)

    def tz0_got(k, d):
        r = tok.at[blk(zat(-d), c, xoff[k])]
        q = k if d > 0 else NX + k
        send(r, r, z0s.at[q], z0r.at[q], to_u, y).wait_recv()

    def plane(p, cc, n=NX, off=0):
        return tok.at[pl.ds(p * (NX * NC) + cc * NX + off, n)]

    def tz(t, d):
        p = zat(-d * t)
        r = plane(p, c) if t < 3 else plane(p, c, 2, 0 if d > 0 else 2)
        k = t - 1 if d > 0 else 2 + t
        return send(r, r, zs.at[k], zr.at[k], to_u if d > 0 else to_d, y)

    def tz_got(t, d):
        p = zat(-d * (t + 1))
        r = plane(p, c) if t < 3 else plane(p, c, 2, 0 if d > 0 else 2)
        k = t - 1 if d > 0 else 2 + t
        send(r, r, zs.at[k], zr.at[k], to_u, y).wait_recv()

    def across(d, p, cc):
        r = plane(p, cc)
        return send(r, r, ss.at[d], sr.at[d], sib, y)

    def ag(i, k, copy=True):
        src, dst, to = (
            (xo.at[i, other], xg.at[i, y if copy else yd], yu),
            (xo.at[i, other], xg.at[i, y if copy else yu], yd),
            (xo.at[i, mine, left_], tr.at[i, 0], yu),
            (xo.at[i, mine, right_], tr.at[i, 1], yd),
            (tr.at[i, 0], xg.at[i, yd if copy else yo, :, left_], yu),
            (tr.at[i, 1], xg.at[i, yu if copy else yo, :, right_], yd),
        )[k]
        return send(src, dst, gs.at[k, i], gr.at[k, i], e, to)

    def rs(i, k):
        src, dst, to = (
            (pb.at[i, yu], ra.at[i, 0], yu),
            (pb.at[i, yd], ra.at[i, 1], yd),
            (pb.at[i, yo, :, left_], tq.at[i, 0], yu),
            (pb.at[i, yo, :, right_], tq.at[i, 1], yd),
            (tq.at[i, 0], rb.at[i, :, left_], yu),
            (tq.at[i, 1], rb.at[i, :, right_], yd),
        )[k]
        return send(src, dst, ps.at[k, i], pr.at[k, i], e, to)

    def sh(k, who=None):
        src, dst, to = (
            (xsh.at[y], xsh.at[y if who is None else who], yu),
            (xsh.at[y], xsh.at[y if who is None else who], yd),
            (xsh.at[yd, plo], xsh.at[yd if who is None else who, plo], yu),
            (xsh.at[yu, phi], xsh.at[yu if who is None else who, phi], yd),
            (psh.at[yo, plo], s1.at[0], yu),
            (psh.at[yo, phi], s1.at[1], yd),
            (psh.at[yu], s2.at[0], yu),
            (psh.at[yd], s2.at[1], yd),
        )[k]
        return send(src, dst, vs.at[k], vr.at[k], e, to)

    tx(0).start()
    tx(1).start()
    tz0(0, 1).start()
    tz0(0, -1).start()
    sh(0).start()
    sh(1).start()
    wide = jnp.concatenate([router[...], jnp.zeros((ROWS - NE, FEAT), F32)], axis=0)
    lg[3] = lax.dot_general(
        normed32, wide, (((1,), (1,)), ((), ())),
        precision=lax.Precision.HIGHEST, preferred_element_type=F32,
    )
    for k in range(3):
        spread(lg, 3, k).start()
    tx_got(0)
    tx(2).start()
    tz0(3, 1).start()
    tz0(3, -1).start()
    tx_got(1)
    tx(3).start()
    tz0(1, 1).start()
    tz0(1, -1).start()
    tx_got(2)
    tx_got(3)
    tz0(2, 1).start()
    tz0(2, -1).start()
    across(0, z, c).start()

    def ring(t):
        for d in (1, -1):
            if t == 1:
                for k in (0, 3, 1, 2):
                    tz0_got(k, d)
            else:
                tz_got(t - 1, d)
            if t < 4:
                tz(t, d).start()
                p = zat(-d * t)
                across((-d * t) % NZ, p, c).start()
        if t == 4:
            across(4, far, c).start()

    def offset_of(k):
        return lax.shift_right_logical(jnp.int32(ORDER), 3 * k) & 7

    def plane_of(k):
        return lax.rem(z + offset_of(k), NZ)

    def stage_rows(i):
        p = plane_of(i)
        across(offset_of(i), p, 1 - c).wait_recv()
        rows = lax.broadcasted_iota(jnp.int32, (CHUNK, ROWS), 0).astype(F32)
        total = jnp.zeros((CHUNK, FEAT), F32)
        for b in range(0, NX * NC, 2):
            k = p * (NX * NC) + b
            onehot = jnp.concatenate(
                [
                    (rows == slot[pl.ds(k + h, 1), :] + float(CAP * (b + h))).astype(F32)
                    for h in range(2)
                ],
                axis=1,
            ).astype(BF16)
            pair = tok[pl.ds(k, 2)].reshape(2 * ROWS, FEAT)
            total = total + jnp.dot(onehot, pair, preferred_element_type=F32)
        xo[i] = total.astype(BF16)
        for k in (2, 3, 0, 1):
            ag(i, k).start()
        xg[i, y] = xo[i, mine]

    def stage_relay(i):
        for k in (2, 3):
            ag(i, k, False).wait_recv()
            ag(i, k + 2).start()

    def gated(gate, value):
        return (gate / (1.0 + jnp.exp(-gate)) * value).astype(BF16)

    def stage_experts(i):
        for k in (0, 1, 4, 5):
            ag(i, k, False).wait_recv()
        both = []
        for h in range(2):
            total = jnp.zeros((HALF, QPAD), F32)
            for k in range(NY):
                total = total + nt(xg[i, k], wi[h, :, k * FEAT : (k + 1) * FEAT])
            both.append(total)
        hidden = gated(both[0], both[1])

        def down(k, carry):
            d = lax.rem(yo + k, NY)
            w = wo[:, pl.ds(pl.multiple_of(d * FEAT, FEAT), FEAT)]
            pb[i, d] = jnp.dot(hidden, w, preferred_element_type=F32).astype(BF16)
            return carry

        lax.fori_loop(0, 1, down, 0)
        rs(i, 2).start()
        rs(i, 3).start()
        lax.fori_loop(1, NY, down, 0)
        rs(i, 0).start()
        rs(i, 1).start()

    def stage_shared():
        sh(2, yo).wait_recv()
        sh(3, yo).wait_recv()
        for k in range(NX):
            wsib(k, 1 - c).wait_recv()
        acc[...] = jnp.zeros((ROWS, 2 * SPAD), F32)

        def into(zz, carry):
            w = jnp.concatenate(
                [
                    wb[wblk(zz, cc, xx), :, pl.ds(0, 2 * SPAD)]
                    for xx in range(NX)
                    for cc in range(NC)
                ],
                axis=0,
            )
            off = pl.multiple_of(lax.rem(zz, 2) * 256, 256)
            acc[...] += jnp.dot(
                xsh[lax.div(zz, 2), :, pl.ds(off, 256)],
                w,
                preferred_element_type=F32,
            )
            return carry

        lax.fori_loop(0, NZ, into, 0)
        hidden = gated(acc[:, :SPAD], acc[:, SPAD:])

        def project(k, carry):
            d = lax.rem(yo + k, NY)
            w = jnp.concatenate(
                [
                    wb[wblk(2 * d + zz, cc, xx), :, pl.ds(2 * SPAD, SPAD)]
                    for zz in range(2)
                    for xx in range(NX)
                    for cc in range(NC)
                ],
                axis=0,
            )
            psh[d] = nt(hidden, w).astype(BF16)
            return carry

        lax.fori_loop(0, NY, project, 0)
        sh(4).start()
        sh(5).start()

    def stage_reduce(i):
        for k in (2, 3):
            rs(i, k).wait_recv()
            rs(i, k + 2).start()

    def shared_relay():
        sh(0, yd).wait_recv()
        sh(2).start()
        sh(1, yu).wait_recv()
        sh(3).start()

    def shared_reduce():
        sh(4).wait_recv()
        psh[yu, plo] = (psh[yu, plo].astype(F32) + s1[0].astype(F32)).astype(BF16)
        sh(6).start()
        sh(5).wait_recv()
        psh[yd, phi] = (psh[yd, phi].astype(F32) + s1[1].astype(F32)).astype(BF16)
        sh(7).start()

    def shared_total():
        sh(6).wait_recv()
        sh(7).wait_recv()
        shared[...] = psh[y].astype(F32) + s2[0].astype(F32) + s2[1].astype(F32)

    def back(i, b):
        to = eid(plane_of(i), lax.rem(b, NX), lax.div(b, NX))
        return to, send(sbuf.at[i, b], rbuf.at[e], os_.at[i * (NX * NC) + b], or_.at[e], to, y)

    def stage_return(i):
        for k in (0, 1, 4, 5):
            rs(i, k).wait_recv()
        tot[mine] = pb[i, y].astype(F32) + rb[i].astype(F32)
        tot[other] = ra[i, 0].astype(F32) + ra[i, 1].astype(F32)
        total = tot[...].astype(BF16)
        to_row = lax.broadcasted_iota(jnp.int32, (ROWS, CHUNK), 0)
        of_row = lax.broadcasted_iota(jnp.int32, (ROWS, CHUNK), 1)
        base = CAP * lax.shift_right_logical(to_row, 4)
        inner = to_row & (PACK - 1)

        def move(hit, values):
            return jnp.dot(hit.astype(F32).astype(BF16), values, preferred_element_type=F32)

        first = move(of_row == base + inner, total)
        sbuf[i, :, :, pl.ds(0, FEAT)] = first.astype(BF16).reshape(NX * NC, PACK, FEAT)
        last = jnp.zeros((ROWS, ROWS), F32)
        for q in range(4):
            hit = (of_row == base + PACK + inner - 4 * q) & (inner >= 4 * q) & (inner < 4 * q + 4)
            last = last + move(hit, total[:, q * 128 : (q + 1) * 128])
        sbuf[i, :, :, pl.ds(FEAT, 128)] = last.astype(BF16).reshape(NX * NC, PACK, 128)

        def go(b, carry):
            to, copy = back(i, b)

            @pl.when(to != e)
            def _():
                copy.start()

            @pl.when(to == e)
            def _():
                rbuf[e] = sbuf[i, b]

            return carry

        lax.fori_loop(0, NX * NC, go, 0)

    def stage_tables():
        for k in range(3):
            spread(lg, 3, k).wait_recv()
        logits = (lg[0] + lg[1]) + (lg[2] + lg[3])
        mine = jnp.transpose(names)
        lane = c_i.astype(F32)
        count = jnp.zeros((ROWS, ROWS), F32)
        for k in range(TOP):
            count = count + (mine[:, k : k + 1] == lane).astype(F32)
        chosen = count > 0.5
        top = jnp.max(jnp.where(chosen, logits, -jnp.inf), axis=1, keepdims=True)
        weight = jnp.where(chosen, jnp.exp(jnp.where(chosen, logits - top, 0.0)), 0.0)
        gates = weight / jnp.sum(weight, axis=1, keepdims=True)
        place = jnp.dot(
            (c_i < r_i).astype(F32).astype(BF16), count.astype(BF16), preferred_element_type=F32
        )
        place = jnp.where(chosen, place, 255.0).astype(BF16)
        high = gates.astype(BF16)
        low = (gates - high.astype(F32)).astype(BF16)

        def fill(b, carry):
            ee = lax.broadcasted_iota(jnp.int32, (ROWS, 256), 0)
            jj = lax.broadcasted_iota(jnp.int32, (ROWS, 256), 1)
            inner = jj & (PACK - 1)
            mat = (ee == lax.shift_right_logical(jj, 4) + b * PACK).astype(F32).astype(BF16)
            where = jnp.dot(place, mat, preferred_element_type=F32)
            at = pl.ds(pl.multiple_of(b * 256, 256), 256)
            for h, g in enumerate((high, low)):
                spaced = jnp.dot(g, mat, preferred_element_type=F32)
                for q, want in enumerate((inner, PACK + (inner & 3))):
                    hit = jnp.where(where == want.astype(F32), spaced, 0.0)
                    tab[q, pl.ds(h * ROWS, ROWS), at] = hit.astype(BF16)
            return carry

        lax.fori_loop(0, NE * PACK // 256, fill, 0)

    def step(j, carry):
        def only(cond, do):
            @pl.when(cond)
            def _():
                do()

        only((j >= 1) & (j < NZ + 1), lambda: stage_relay(j - 1))
        only(j >= 3, lambda: stage_reduce(j - 3))
        only(j < NZ, lambda: stage_rows(j))

        @pl.when(j == 0)
        def _():
            shared_relay()
            wz_step(3)

        @pl.when(j == 1)
        def _():
            for d in (1, -1):
                wz_got(3, d)
            wx(0).start()
            wx(1).start()
            wsib(0, c).start()

        @pl.when(j == 4)
        def _():
            wx_got(0)
            wx(2).start()
            wx_got(1)
            wx(3).start()
            wsib(3, c).start()
            wsib(1, c).start()

        @pl.when(j == 6)
        def _():
            wx_got(2)
            wx_got(3)
            wsib(2, c).start()

        only(j == SHARED_AT + 1, shared_reduce)

        @pl.when(j == 2)
        def _():
            for load in loads:
                load.wait()
            for k in range(8):
                pair(k).wait_recv()

        only((j >= 2) & (j < NZ + 2), lambda: stage_experts(j - 2))
        only(j >= 3, lambda: stage_return(j - 3))
        only(j == 1, stage_tables)
        only(j == SHARED_AT, stage_shared)
        only(j == SHARED_AT + 2, shared_total)
        for t, when in ((1, 0), (2, 0), (3, 2), (4, 3)):
            only(j == when, lambda t=t: ring(t))
        return carry

    lax.fori_loop(0, NZ + 3, step, 0)

    def arrive(k, carry):
        s = lax.rem(e + k, NE)
        send(rbuf.at[s], rbuf.at[s], os_.at[0], or_.at[s], sib, y).wait_recv()
        return carry

    lax.fori_loop(1, NE, arrive, 0)
    back_rows = rbuf[:, :, pl.ds(0, FEAT)].reshape(NE * PACK, FEAT)
    pieces = rbuf[:, :, pl.ds(FEAT, 128)].reshape(NE * PACK, 128).astype(F32)
    part_of = lax.shift_right_logical(
        lax.broadcasted_iota(jnp.int32, (NE * PACK, 128), 0) & (PACK - 1), 2
    )
    extra = jnp.concatenate(
        [jnp.where(part_of == q, pieces, 0.0).astype(BF16) for q in range(4)], axis=1
    )
    both = jnp.dot(tab[0], back_rows, preferred_element_type=F32) + jnp.dot(
        tab[1], extra, preferred_element_type=F32
    )
    base_o[...] = mixed[...] + shared[...]
    out[...] = both[:ROWS] + both[ROWS:]

    for k in range(3):
        ax(k).wait_send()
        spread(sq, 0, k).wait_send()
        spread(lg, 3, k).wait_send()
    for t in range(4):
        for d in (1, -1):
            for k in range(NX):
                if az_goes(k, t, d):
                    az(k, t, d).wait_send()
            if t < 3 or d > 0:
                bz(t, d).wait_send()
            wz(t, d).wait_send()
            tz0(t, d).wait_send()
            if t > 0:
                tz(t, d).wait_send()
        b_sib(t, c).wait_send()
        wx(t).wait_send()
        wsib(t, c).wait_send()
        tx(t).wait_send()
    for q in range(NZ):
        for k in range(3):
            bx(q, k).wait_send()
    for d in (0, -1, 1, -2, 2, -3, 3, 4):
        a_sib(d, c).wait_send()
    for k in range(2):
        pa(k).wait_send()
        pb2(k).wait_send()

    def drain(i, carry):
        across(i, lax.rem(z + i, NZ), c).wait_send()

        def sent(b, inner):
            to, copy = back(i, b)

            @pl.when(to != e)
            def _():
                copy.wait_send()

            return inner

        lax.fori_loop(0, NX * NC, sent, 0)
        for k in range(6):
            ag(i, k).wait_send()
            rs(i, k).wait_send()
        return carry

    lax.fori_loop(0, NZ, drain, 0)
    for k in range(8):
        pair(k).wait_send()
        sh(k).wait_send()


def mixer(ctx, opt, ids, hid, gain, router, wsh, win, wout):
    vm = pl.BlockSpec(memory_space=pltpu.VMEM)
    hbm = pl.BlockSpec(memory_space=pl.ANY)

    def pairs(*shapes):
        return [pltpu.SemaphoreType.DMA(s) for s in shapes for _ in range(2)]

    return pl.pallas_call(
        mixer_kernel,
        name="mixer_tail",
        out_shape=[jax.ShapeDtypeStruct((ROWS, FEAT), F32)] * 2,
        in_specs=[vm] * 7 + [hbm] * 2,
        out_specs=[vm] * 2,
        scratch_shapes=[
            pltpu.VMEM((NE, 16, FEAT + ROWS), BF16),
            pltpu.VMEM((NE, 16, FEAT), BF16),
            pltpu.VMEM((NY, ROWS, FEAT), F32),
            pltpu.VMEM((2, ROWS // 2, FEAT), F32),
            pltpu.VMEM((2, ROWS, FEAT), F32),
            pltpu.VMEM((4, 8, ROWS), F32),
            pltpu.VMEM((4, ROWS, ROWS), F32),
            pltpu.VMEM((ROWS, FEAT), F32),
            pltpu.VMEM((ROWS, FEAT), F32),
            pltpu.VMEM((2, 2 * ROWS, NE * PACK), BF16),
            pltpu.VMEM((NE, ROWS, FEAT), BF16),
            pltpu.VMEM((NE, ROWS), F32),
            pltpu.VMEM((NZ, CHUNK, FEAT), BF16),
            pltpu.VMEM((NZ, NY, HALF, FEAT), BF16),
            pltpu.VMEM((NZ, 2, HALF, 256), BF16),
            pltpu.VMEM((NZ, NY, HALF, FEAT), BF16),
            pltpu.VMEM((NZ, 2, HALF, FEAT), BF16),
            pltpu.VMEM((NZ, HALF, FEAT), BF16),
            pltpu.VMEM((NZ, 2, HALF, 256), BF16),
            pltpu.VMEM((NY, ROWS, FEAT), BF16),
            pltpu.VMEM((NY, ROWS, FEAT), BF16),
            pltpu.VMEM((2, ROWS // 2, FEAT), BF16),
            pltpu.VMEM((2, ROWS, FEAT), BF16),
            pltpu.VMEM((NE, 32, 3 * SPAD), BF16),
            pltpu.VMEM((2, QPAD, WIDTH), BF16),
            pltpu.VMEM((QPAD, WIDTH), BF16),
            pltpu.VMEM((NZ, NX * NC, PACK, PWIDTH), BF16),
            pltpu.VMEM((NE, PACK, PWIDTH), BF16),
            pltpu.VMEM((ROWS, 2 * SPAD), F32),
            pltpu.VMEM((CHUNK, FEAT), F32),
            pltpu.SemaphoreType.DMA((3,)),
        ]
        + pairs((3,), (32,), (8,), (8,), (3, NZ), (4,), (4,), (6,))
        + pairs((4,), (8,), (6,), (8,), (8,), (4,), (4,))
        + pairs((8,), (6, NZ), (6, NZ), (8,), (NE,)),
        compiler_params=pltpu.CompilerParams(
            collective_id=0, has_side_effects=True, vmem_limit_bytes=VMEM_LIMIT
        ),
    )(ctx, opt, ids, hid, gain, router, wsh, win, wout)


def per_device(
    hidden_state, context, out_proj, norm_gain, router_weight,
    expert_in, expert_out, shared_in, shared_out, route_ids,
):
    gap = ((0, 0), (0, 0), (0, SPAD - SWIDTH))
    shard = jnp.concatenate(
        [
            jnp.pad(shared_in, gap).reshape(32, 2 * SPAD),
            jnp.pad(shared_out.T, ((0, 0), (0, SPAD - SWIDTH))),
        ],
        axis=1,
    )
    win = jnp.transpose(expert_in[0], (1, 2, 0))
    routed, base = mixer(
        context, out_proj.T, route_ids.T, hidden_state, norm_gain[None, :],
        router_weight.T, shard, win, expert_out[0],
    )
    return base + routed


def solution(mesh):
    return jax.shard_map(
        per_device,
        mesh=mesh,
        in_specs=(
            P("expert", "mp"),
            P("expert", "mp"),
            P("mp", "expert"),
            P("mp"),
            P("mp", None),
            P("expert", None, None, "mp"),
            P("expert", "mp", None),
            P("expert", None, "mp"),
            P("mp", "expert"),
            P("expert", None),
        ),
        out_specs=P("expert", "mp"),
        check_vma=False,
    )
```

```python
import jax
import jax.numpy as jnp
from jax import lax
from jax.experimental import pallas as pl
from jax.experimental.pallas import tpu as pltpu
from jax.sharding import PartitionSpec as P

NZ, NX, NC, NY = 8, 4, 2, 4
NE = NZ * NX * NC
ROWS, FEAT, WIDTH = 128, 512, 2048
TOP, CAP, PACK, PWIDTH = 6, 20, 16, 640
QUARTER, QPAD = 352, 768
EIGHTH = QUARTER // 2
SWIDTH, SPAD = 704, 768
CHUNK = NX * NC * CAP
HALF = CHUNK // 2
SHARED_AT = 7
ORDER = sum(d << (3 * k) for k, d in enumerate((0, 6, 2, 5, 4, 3, 7, 1)))
F32, BF16 = jnp.float32, jnp.bfloat16
VMEM_LIMIT = 64 * 1024 * 1024 - 65536


def coords():
    e = lax.axis_index("expert")
    y = lax.axis_index("mp")
    z = lax.div(e, NX * NC)
    x = lax.rem(lax.div(e, NC), NX)
    c = lax.rem(e, NC)
    return e, z, x, c, y


def eid(z, x, c):
    return z * (NX * NC) + x * NC + c


def blk(z, c, x):
    return z * (NX * NC) + c * NX + x


def send(src, dst, ssem, rsem, e, y):
    return pltpu.make_async_remote_copy(
        src_ref=src,
        dst_ref=dst,
        send_sem=ssem,
        recv_sem=rsem,
        device_id={"expert": e, "mp": y},
        device_id_type=pl.DeviceIdType.MESH,
    )


def greet(e, y):
    pl.semaphore_signal(
        pltpu.get_barrier_semaphore(),
        inc=1,
        device_id={"expert": e, "mp": y},
        device_id_type=pl.DeviceIdType.MESH,
    )


def nt(a, b):
    return lax.dot_general(a, b, (((1,), (1,)), ((), ())), preferred_element_type=F32)


def mixer_kernel(
    ctx, opt, ids, hid, gain, router, wsh, win, wout,
    out, base_o,
    wga, wgb, part, p1, p2, sq, lg, mixed, shared, tab,
    tok, slot, xo, xg, tr, pb, ra, rb, tq, xsh, psh, s1, s2,
    wb, wi, wo, sbuf, rbuf, acc, tot,
    wsem,
    axs, axr, azs, azr, ass, asr, bzs, bzr, bxs, bxr, bss, bsr,
    ys, yr, qs, qr,
    xs, xr, z0s, z0r, zs, zr, ss, sr,
    wzs, wzr, wxs, wxr, wss, wsr,
    hs, hr, gs, gr, ps, pr, vs, vr, os_, or_,
):
    e, z, x, c, y = coords()
    xr_, xl_, xo_ = lax.rem(x + 1, NX), lax.rem(x + NX - 1, NX), lax.rem(x + 2, NX)
    to_r, to_l = eid(z, xr_, c), eid(z, xl_, c)
    to_u, to_d = eid(lax.rem(z + 1, NZ), x, c), eid(lax.rem(z + NZ - 1, NZ), x, c)
    sib = eid(z, x, 1 - c)
    yu, yd, yo = lax.rem(y + 1, NY), lax.rem(y + NY - 1, NY), lax.rem(y + 2, NY)
    left_, right_ = pl.ds(0, 256), pl.ds(256, 256)
    par = lax.rem(y, 2)
    mine = pl.ds(pl.multiple_of(par * HALF, 16), HALF)
    other = pl.ds(pl.multiple_of((1 - par) * HALF, 16), HALF)
    near = y + 1 - 2 * par
    next_ = lax.rem(y + 3 + 2 * par, NY)
    far = lax.rem(z + 4, NZ)

    def zat(d):
        return lax.rem(z + NZ + d, NZ)

    def hello(k, carry):
        greet(lax.rem(e + k, NE), y)
        return carry

    lax.fori_loop(1, NE, hello, 0)
    for t in (yu, yd, yo):
        greet(e, t)

    loads = [
        pltpu.make_async_copy(win.at[0], wi.at[0, pl.ds(0, QUARTER)], wsem.at[0]),
        pltpu.make_async_copy(win.at[1], wi.at[1, pl.ds(0, QUARTER)], wsem.at[1]),
        pltpu.make_async_copy(wout, wo.at[pl.ds(0, QUARTER)], wsem.at[2]),
    ]
    for load in loads:
        load.start()

    def wblk(zz, cc, xx):
        return cc * (NX * NZ) + xx * NZ + zz

    own, wown = blk(z, c, x), wblk(z, c, x)
    names = jnp.concatenate(
        [ids[...].astype(F32), jnp.full((ROWS - TOP, ROWS), -1.0, F32)], axis=0
    )
    wga[own, :, pl.ds(0, FEAT)] = opt[0:16, :]
    wga[own, :, pl.ds(FEAT, ROWS)] = names[:16].astype(BF16)
    wgb[wown] = opt[16:32, :]
    wb[wown] = wsh[...]
    pl.semaphore_wait(pltpu.get_barrier_semaphore(), NE + 2)

    def pair(k):
        src, dst, at, to, n, where = (
            (win.at[0], wi.at[0], 0, near, EIGHTH, QUARTER),
            (win.at[0], wi.at[0], EIGHTH, next_, EIGHTH, QUARTER + EIGHTH),
            (win.at[1], wi.at[1], 0, near, 80, QUARTER),
            (win.at[1], wi.at[1], EIGHTH, next_, 80, QUARTER + EIGHTH),
            (win.at[1], wi.at[1], 80, near, EIGHTH - 80, QUARTER + 80),
            (win.at[1], wi.at[1], EIGHTH + 80, next_, EIGHTH - 80, QUARTER + EIGHTH + 80),
            (wout, wo, 0, near, EIGHTH, QUARTER),
            (wout, wo, EIGHTH, next_, EIGHTH, QUARTER + EIGHTH),
        )[k]
        return send(src.at[pl.ds(at, n)], dst.at[pl.ds(where, n)], hs.at[k], hr.at[k], e, to)

    def ax(k):
        b, to = [(own, to_r), (own, to_l), (blk(z, c, xl_), to_r)][k]
        return send(wga.at[b], wga.at[b], axs.at[k], axr.at[k], to, y)

    def ax_got(k):
        b = blk(z, c, [xl_, xr_, xo_][k])
        send(wga.at[b], wga.at[b], axs.at[k], axr.at[k], to_r, y).wait_recv()

    def a_plane(p, cc, n=NX, off=0):
        return wga.at[pl.ds(p * (NX * NC) + cc * NX + off, n)]

    def az(t, d):
        p = zat(-d * t)
        r = a_plane(p, c) if t < 3 else a_plane(p, c, 2, 0 if d > 0 else 2)
        k = t if d > 0 else 4 + t
        return send(r, r, azs.at[k], azr.at[k], to_u if d > 0 else to_d, y)

    def az_got(t, d):
        p = zat(-d * (t + 1))
        r = a_plane(p, c) if t < 3 else a_plane(p, c, 2, 0 if d > 0 else 2)
        k = t if d > 0 else 4 + t
        send(r, r, azs.at[k], azr.at[k], to_u, y).wait_recv()

    def a_sib(d, cc):
        r = a_plane(zat(d), cc)
        return send(r, r, ass.at[d % NZ], asr.at[d % NZ], sib, y)

    def bz(t, d):
        r = wgb.at[wblk(zat(-d * t), c, x)]
        k = t if d > 0 else 4 + t
        return send(r, r, bzs.at[k], bzr.at[k], to_u if d > 0 else to_d, y)

    def bz_got(t, d):
        r = wgb.at[wblk(zat(-d * (t + 1)), c, x)]
        k = t if d > 0 else 4 + t
        send(r, r, bzs.at[k], bzr.at[k], to_u, y).wait_recv()

    def b_col(xx, cc, n=NZ, off=0):
        return wgb.at[pl.ds(cc * (NX * NZ) + xx * NZ + off, n)]

    def bx(k):
        r, to = [
            (b_col(x, c), to_r), (b_col(x, c), to_l),
            (b_col(xl_, c, 4, 0), to_r), (b_col(xr_, c, 4, 4), to_l),
        ][k]
        return send(r, r, bxs.at[k], bxr.at[k], to, y)

    def bx_got(k):
        r = [b_col(xl_, c), b_col(xr_, c), b_col(xo_, c, 4, 0), b_col(xo_, c, 4, 4)][k]
        send(r, r, bxs.at[k], bxr.at[k], to_r, y).wait_recv()

    xoff = (x, xr_, xo_, xl_)

    def b_sib(k, cc):
        r = b_col(xoff[k], cc)
        return send(r, r, bss.at[k], bsr.at[k], sib, y)

    for k in range(4):
        pair(k).start()
    ax(0).start()
    ax(1).start()
    bz(0, 1).start()
    bz(0, -1).start()
    ax_got(0)
    ax(2).start()
    ax_got(1)
    bz_got(0, 1)
    bz(1, 1).start()
    bz_got(0, -1)
    bz(1, -1).start()
    ax_got(2)
    az(0, 1).start()
    az(0, -1).start()
    a_sib(0, c).start()
    bz_got(1, 1)
    bz(2, 1).start()
    bz_got(1, -1)
    bz(2, -1).start()
    az_got(0, 1)
    az(1, 1).start()
    az_got(0, -1)
    az(1, -1).start()
    a_sib(-1, c).start()
    a_sib(1, c).start()
    bz_got(2, 1)
    bz(3, 1).start()
    bz_got(2, -1)
    az_got(1, 1)
    az(2, 1).start()
    az_got(1, -1)
    az(2, -1).start()
    bz_got(3, 1)
    bx(0).start()
    bx(1).start()
    a_sib(-2, c).start()
    a_sib(2, c).start()
    b_sib(0, c).start()
    az_got(2, 1)
    az(3, 1).start()
    az_got(2, -1)
    az(3, -1).start()
    a_sib(-3, c).start()
    a_sib(3, c).start()
    bx_got(0)
    bx(2).start()
    bx_got(1)
    bx(3).start()
    b_sib(3, c).start()
    b_sib(1, c).start()
    az_got(3, 1)
    az_got(3, -1)
    a_sib(4, c).start()
    bx_got(2)
    bx_got(3)
    b_sib(2, c).start()

    def wz(t, d):
        r = wb.at[wblk(zat(-d * t), c, x)]
        if t == 3:
            r = wb.at[wblk(zat(-d * t), c, x), pl.ds(0 if d > 0 else 16, 16)]
        k = t if d > 0 else 4 + t
        return send(r, r, wzs.at[k], wzr.at[k], to_u if d > 0 else to_d, y)

    def wz_got(t, d):
        r = wb.at[wblk(zat(-d * (t + 1)), c, x)]
        if t == 3:
            r = wb.at[wblk(zat(-d * (t + 1)), c, x), pl.ds(0 if d > 0 else 16, 16)]
        k = t if d > 0 else 4 + t
        send(r, r, wzs.at[k], wzr.at[k], to_u, y).wait_recv()

    def wz_step(t):
        for d in (1, -1):
            wz_got(t - 1, d)
            wz(t, d).start()

    def col(xx, cc, n=NZ, off=0):
        return wb.at[pl.ds(cc * (NX * NZ) + xx * NZ + off, n)]

    def wx(k):
        r, to = [
            (col(x, c), to_r), (col(x, c), to_l),
            (col(xl_, c, 4, 0), to_r), (col(xr_, c, 4, 4), to_l),
        ][k]
        return send(r, r, wxs.at[k], wxr.at[k], to, y)

    def wx_got(k):
        r = [col(xl_, c), col(xr_, c), col(xo_, c, 4, 0), col(xo_, c, 4, 4)][k]
        send(r, r, wxs.at[k], wxr.at[k], to_r, y).wait_recv()

    def wsib(k, cc):
        r = col(xoff[k], cc)
        return send(r, r, wss.at[k], wsr.at[k], sib, y)

    wz(0, 1).start()
    wz(0, -1).start()
    for d in (0, -1, 1, -2, 2, -3, 3, 4):
        a_sib(d, 1 - c).wait_recv()
    for k in range(NX):
        b_sib(k, 1 - c).wait_recv()

    def columns(d):
        blocks = []
        for zz in range(2):
            for xx in range(NX):
                for cc in range(NC):
                    p = 2 * d + zz
                    blocks.append(wga[blk(p, cc, xx), :, pl.ds(0, FEAT)])
                    blocks.append(wgb[wblk(p, cc, xx)])
        return nt(ctx[...], jnp.concatenate(blocks, axis=0))

    hrows = ROWS // 2
    plo, phi = pl.ds(0, hrows), pl.ds(hrows, hrows)

    def pa(k):
        rows, to = [(plo, yu), (phi, yd)][k]
        return send(part.at[yo, rows], p1.at[k], ys.at[k], yr.at[k], e, to)

    def pb2(k):
        to = [yu, yd][k]
        return send(part.at[to], p2.at[k], ys.at[2 + k], yr.at[2 + k], e, to)

    part[yo] = columns(yo)
    pa(0).start()
    pa(1).start()
    part[yu] = columns(yu)
    part[yd] = columns(yd)
    pa(0).wait_recv()
    part[yu, plo] = part[yu, plo] + p1[0]
    pb2(0).start()
    pa(1).wait_recv()
    part[yd, phi] = part[yd, phi] + p1[1]
    pb2(1).start()
    part[y] = columns(y)
    wz_step(1)

    def mark(b, carry):
        same = (wga[b, :, pl.ds(FEAT, ROWS)].astype(F32) == e.astype(F32)).astype(F32)
        slot[pl.ds(b, 1), :] = jnp.sum(same, axis=0, keepdims=True)
        return carry

    lax.fori_loop(0, NE, mark, 0)
    r_i = lax.broadcasted_iota(jnp.int32, (ROWS, ROWS), 0)
    c_i = lax.broadcasted_iota(jnp.int32, (ROWS, ROWS), 1)
    named = slot[...]
    rank = jnp.dot(
        named.astype(BF16), (r_i < c_i).astype(F32).astype(BF16), preferred_element_type=F32
    )
    slot[...] = jnp.where(named > 0.5, rank, -1000.0)
    gap = pl.ds(2 * QUARTER, QPAD - 2 * QUARTER)
    wi[0, gap] = jnp.zeros((QPAD - 2 * QUARTER, WIDTH), BF16)
    wi[1, gap] = jnp.zeros((QPAD - 2 * QUARTER, WIDTH), BF16)
    wo[gap] = jnp.zeros((QPAD - 2 * QUARTER, WIDTH), BF16)

    pb2(0).wait_recv()
    pb2(1).wait_recv()
    mix = hid[...].astype(F32) + (part[y] + p2[0] + p2[1])
    mixed[...] = mix

    def spread(buf, base, k):
        return send(
            buf.at[3], buf.at[k], qs.at[base + k], qr.at[base + k], e, (yu, yd, yo)[k]
        )

    sums = jnp.broadcast_to(jnp.sum(mix * mix, axis=1, keepdims=True), (ROWS, ROWS))
    sq[3] = jnp.transpose(sums)[:8]
    for k in range(3):
        spread(sq, 0, k).start()
    for k in range(4, 8):
        pair(k).start()
    wz_step(2)
    for k in range(3):
        spread(sq, 0, k).wait_recv()
    inverse = lax.rsqrt(((sq[0] + sq[1]) + (sq[2] + sq[3])) / WIDTH + 1e-06)
    inverse = jnp.transpose(jnp.broadcast_to(inverse[:1], (ROWS, ROWS)))[:, :1]
    normed32 = mix * inverse * gain[...].astype(F32)
    tok[own] = normed32.astype(BF16)
    xsh[y] = normed32.astype(BF16)

    def tx(k):
        half = ROWS // 2
        r, to = [
            (tok.at[own], to_r), (tok.at[own], to_l),
            (tok.at[blk(z, c, xl_), pl.ds(0, half)], to_r),
            (tok.at[blk(z, c, xr_), pl.ds(half, half)], to_l),
        ][k]
        return send(r, r, xs.at[k], xr.at[k], to, y)

    def tx_got(k):
        half = ROWS // 2
        r = [
            tok.at[blk(z, c, xl_)], tok.at[blk(z, c, xr_)],
            tok.at[blk(z, c, xo_), pl.ds(0, half)], tok.at[blk(z, c, xo_), pl.ds(half, half)],
        ][k]
        send(r, r, xs.at[k], xr.at[k], to_r, y).wait_recv()

    def tz0(k, d):
        r = tok.at[blk(z, c, xoff[k])]
        q = k if d > 0 else NX + k
        return send(r, r, z0s.at[q], z0r.at[q], to_u if d > 0 else to_d, y)

    def tz0_got(k, d):
        r = tok.at[blk(zat(-d), c, xoff[k])]
        q = k if d > 0 else NX + k
        send(r, r, z0s.at[q], z0r.at[q], to_u, y).wait_recv()

    def plane(p, cc, n=NX, off=0):
        return tok.at[pl.ds(p * (NX * NC) + cc * NX + off, n)]

    def tz(t, d):
        p = zat(-d * t)
        r = plane(p, c) if t < 3 else plane(p, c, 2, 0 if d > 0 else 2)
        k = t - 1 if d > 0 else 2 + t
        return send(r, r, zs.at[k], zr.at[k], to_u if d > 0 else to_d, y)

    def tz_got(t, d):
        p = zat(-d * (t + 1))
        r = plane(p, c) if t < 3 else plane(p, c, 2, 0 if d > 0 else 2)
        k = t - 1 if d > 0 else 2 + t
        send(r, r, zs.at[k], zr.at[k], to_u, y).wait_recv()

    def across(d, p, cc):
        r = plane(p, cc)
        return send(r, r, ss.at[d], sr.at[d], sib, y)

    def ag(i, k, copy=True):
        src, dst, to = (
            (xo.at[i, other], xg.at[i, y if copy else yd], yu),
            (xo.at[i, other], xg.at[i, y if copy else yu], yd),
            (xo.at[i, mine, left_], tr.at[i, 0], yu),
            (xo.at[i, mine, right_], tr.at[i, 1], yd),
            (tr.at[i, 0], xg.at[i, yd if copy else yo, :, left_], yu),
            (tr.at[i, 1], xg.at[i, yu if copy else yo, :, right_], yd),
        )[k]
        return send(src, dst, gs.at[k, i], gr.at[k, i], e, to)

    def rs(i, k):
        src, dst, to = (
            (pb.at[i, yu], ra.at[i, 0], yu),
            (pb.at[i, yd], ra.at[i, 1], yd),
            (pb.at[i, yo, :, left_], tq.at[i, 0], yu),
            (pb.at[i, yo, :, right_], tq.at[i, 1], yd),
            (tq.at[i, 0], rb.at[i, :, left_], yu),
            (tq.at[i, 1], rb.at[i, :, right_], yd),
        )[k]
        return send(src, dst, ps.at[k, i], pr.at[k, i], e, to)

    def sh(k, who=None):
        src, dst, to = (
            (xsh.at[y], xsh.at[y if who is None else who], yu),
            (xsh.at[y], xsh.at[y if who is None else who], yd),
            (xsh.at[yd, plo], xsh.at[yd if who is None else who, plo], yu),
            (xsh.at[yu, phi], xsh.at[yu if who is None else who, phi], yd),
            (psh.at[yo, plo], s1.at[0], yu),
            (psh.at[yo, phi], s1.at[1], yd),
            (psh.at[yu], s2.at[0], yu),
            (psh.at[yd], s2.at[1], yd),
        )[k]
        return send(src, dst, vs.at[k], vr.at[k], e, to)

    tx(0).start()
    tx(1).start()
    tz0(0, 1).start()
    tz0(0, -1).start()
    sh(0).start()
    sh(1).start()
    wide = jnp.concatenate([router[...], jnp.zeros((ROWS - NE, FEAT), F32)], axis=0)
    lg[3] = lax.dot_general(
        normed32, wide, (((1,), (1,)), ((), ())),
        precision=lax.Precision.HIGHEST, preferred_element_type=F32,
    )
    for k in range(3):
        spread(lg, 3, k).start()
    tx_got(0)
    tx(2).start()
    tz0(3, 1).start()
    tz0(3, -1).start()
    tx_got(1)
    tx(3).start()
    tz0(1, 1).start()
    tz0(1, -1).start()
    tx_got(2)
    tx_got(3)
    tz0(2, 1).start()
    tz0(2, -1).start()
    across(0, z, c).start()

    def ring(t):
        for d in (1, -1):
            if t == 1:
                for k in (0, 3, 1, 2):
                    tz0_got(k, d)
            else:
                tz_got(t - 1, d)
            if t < 4:
                tz(t, d).start()
                p = zat(-d * t)
                across((-d * t) % NZ, p, c).start()
        if t == 4:
            across(4, far, c).start()

    def offset_of(k):
        return lax.shift_right_logical(jnp.int32(ORDER), 3 * k) & 7

    def plane_of(k):
        return lax.rem(z + offset_of(k), NZ)

    def stage_rows(i):
        p = plane_of(i)
        across(offset_of(i), p, 1 - c).wait_recv()
        rows = lax.broadcasted_iota(jnp.int32, (CHUNK, ROWS), 0).astype(F32)
        total = jnp.zeros((CHUNK, FEAT), F32)
        for b in range(0, NX * NC, 2):
            k = p * (NX * NC) + b
            onehot = jnp.concatenate(
                [
                    (rows == slot[pl.ds(k + h, 1), :] + float(CAP * (b + h))).astype(F32)
                    for h in range(2)
                ],
                axis=1,
            ).astype(BF16)
            pair = tok[pl.ds(k, 2)].reshape(2 * ROWS, FEAT)
            total = total + jnp.dot(onehot, pair, preferred_element_type=F32)
        xo[i] = total.astype(BF16)
        for k in (2, 3, 0, 1):
            ag(i, k).start()
        xg[i, y] = xo[i, mine]

    def stage_relay(i):
        for k in (2, 3):
            ag(i, k, False).wait_recv()
            ag(i, k + 2).start()

    def gated(gate, value):
        return (gate / (1.0 + jnp.exp(-gate)) * value).astype(BF16)

    def stage_experts(i):
        for k in (0, 1, 4, 5):
            ag(i, k, False).wait_recv()
        both = []
        for h in range(2):
            total = jnp.zeros((HALF, QPAD), F32)
            for k in range(NY):
                total = total + nt(xg[i, k], wi[h, :, k * FEAT : (k + 1) * FEAT])
            both.append(total)
        hidden = gated(both[0], both[1])

        def down(k, carry):
            d = lax.rem(yo + k, NY)
            w = wo[:, pl.ds(pl.multiple_of(d * FEAT, FEAT), FEAT)]
            pb[i, d] = jnp.dot(hidden, w, preferred_element_type=F32).astype(BF16)
            return carry

        lax.fori_loop(0, 1, down, 0)
        rs(i, 2).start()
        rs(i, 3).start()
        lax.fori_loop(1, NY, down, 0)
        rs(i, 0).start()
        rs(i, 1).start()

    def stage_shared():
        sh(2, yo).wait_recv()
        sh(3, yo).wait_recv()
        for k in range(NX):
            wsib(k, 1 - c).wait_recv()
        acc[...] = jnp.zeros((ROWS, 2 * SPAD), F32)

        def into(zz, carry):
            w = jnp.concatenate(
                [
                    wb[wblk(zz, cc, xx), :, pl.ds(0, 2 * SPAD)]
                    for xx in range(NX)
                    for cc in range(NC)
                ],
                axis=0,
            )
            off = pl.multiple_of(lax.rem(zz, 2) * 256, 256)
            acc[...] += jnp.dot(
                xsh[lax.div(zz, 2), :, pl.ds(off, 256)],
                w,
                preferred_element_type=F32,
            )
            return carry

        lax.fori_loop(0, NZ, into, 0)
        hidden = gated(acc[:, :SPAD], acc[:, SPAD:])

        def project(k, carry):
            d = lax.rem(yo + k, NY)
            w = jnp.concatenate(
                [
                    wb[wblk(2 * d + zz, cc, xx), :, pl.ds(2 * SPAD, SPAD)]
                    for zz in range(2)
                    for xx in range(NX)
                    for cc in range(NC)
                ],
                axis=0,
            )
            psh[d] = nt(hidden, w).astype(BF16)
            return carry

        lax.fori_loop(0, NY, project, 0)
        sh(4).start()
        sh(5).start()

    def stage_reduce(i):
        for k in (2, 3):
            rs(i, k).wait_recv()
            rs(i, k + 2).start()

    def shared_relay():
        sh(0, yd).wait_recv()
        sh(2).start()
        sh(1, yu).wait_recv()
        sh(3).start()

    def shared_reduce():
        sh(4).wait_recv()
        psh[yu, plo] = (psh[yu, plo].astype(F32) + s1[0].astype(F32)).astype(BF16)
        sh(6).start()
        sh(5).wait_recv()
        psh[yd, phi] = (psh[yd, phi].astype(F32) + s1[1].astype(F32)).astype(BF16)
        sh(7).start()

    def shared_total():
        sh(6).wait_recv()
        sh(7).wait_recv()
        shared[...] = psh[y].astype(F32) + s2[0].astype(F32) + s2[1].astype(F32)

    def back(i, b):
        to = eid(plane_of(i), lax.rem(b, NX), lax.div(b, NX))
        return to, send(sbuf.at[i, b], rbuf.at[e], os_.at[i * (NX * NC) + b], or_.at[e], to, y)

    def stage_return(i):
        for k in (0, 1, 4, 5):
            rs(i, k).wait_recv()
        tot[mine] = pb[i, y].astype(F32) + rb[i].astype(F32)
        tot[other] = ra[i, 0].astype(F32) + ra[i, 1].astype(F32)
        total = tot[...].astype(BF16)
        to_row = lax.broadcasted_iota(jnp.int32, (ROWS, CHUNK), 0)
        of_row = lax.broadcasted_iota(jnp.int32, (ROWS, CHUNK), 1)
        base = CAP * lax.shift_right_logical(to_row, 4)
        inner = to_row & (PACK - 1)

        def move(hit, values):
            return jnp.dot(hit.astype(F32).astype(BF16), values, preferred_element_type=F32)

        first = move(of_row == base + inner, total)
        sbuf[i, :, :, pl.ds(0, FEAT)] = first.astype(BF16).reshape(NX * NC, PACK, FEAT)
        last = jnp.zeros((ROWS, ROWS), F32)
        for q in range(4):
            hit = (of_row == base + PACK + inner - 4 * q) & (inner >= 4 * q) & (inner < 4 * q + 4)
            last = last + move(hit, total[:, q * 128 : (q + 1) * 128])
        sbuf[i, :, :, pl.ds(FEAT, 128)] = last.astype(BF16).reshape(NX * NC, PACK, 128)

        def go(b, carry):
            to, copy = back(i, b)

            @pl.when(to != e)
            def _():
                copy.start()

            @pl.when(to == e)
            def _():
                rbuf[e] = sbuf[i, b]

            return carry

        lax.fori_loop(0, NX * NC, go, 0)

    def stage_tables():
        for k in range(3):
            spread(lg, 3, k).wait_recv()
        logits = (lg[0] + lg[1]) + (lg[2] + lg[3])
        mine = jnp.transpose(names)
        lane = c_i.astype(F32)
        count = jnp.zeros((ROWS, ROWS), F32)
        for k in range(TOP):
            count = count + (mine[:, k : k + 1] == lane).astype(F32)
        chosen = count > 0.5
        top = jnp.max(jnp.where(chosen, logits, -jnp.inf), axis=1, keepdims=True)
        weight = jnp.where(chosen, jnp.exp(jnp.where(chosen, logits - top, 0.0)), 0.0)
        gates = weight / jnp.sum(weight, axis=1, keepdims=True)
        place = jnp.dot(
            (c_i < r_i).astype(F32).astype(BF16), count.astype(BF16), preferred_element_type=F32
        )
        place = jnp.where(chosen, place, 255.0).astype(BF16)
        high = gates.astype(BF16)
        low = (gates - high.astype(F32)).astype(BF16)

        def fill(b, carry):
            ee = lax.broadcasted_iota(jnp.int32, (ROWS, 256), 0)
            jj = lax.broadcasted_iota(jnp.int32, (ROWS, 256), 1)
            inner = jj & (PACK - 1)
            mat = (ee == lax.shift_right_logical(jj, 4) + b * PACK).astype(F32).astype(BF16)
            where = jnp.dot(place, mat, preferred_element_type=F32)
            at = pl.ds(pl.multiple_of(b * 256, 256), 256)
            for h, g in enumerate((high, low)):
                spaced = jnp.dot(g, mat, preferred_element_type=F32)
                for q, want in enumerate((inner, PACK + (inner & 3))):
                    hit = jnp.where(where == want.astype(F32), spaced, 0.0)
                    tab[q, pl.ds(h * ROWS, ROWS), at] = hit.astype(BF16)
            return carry

        lax.fori_loop(0, NE * PACK // 256, fill, 0)

    def step(j, carry):
        def only(cond, do):
            @pl.when(cond)
            def _():
                do()

        only((j >= 1) & (j < NZ + 1), lambda: stage_relay(j - 1))
        only(j >= 3, lambda: stage_reduce(j - 3))
        only(j < NZ, lambda: stage_rows(j))

        @pl.when(j == 0)
        def _():
            shared_relay()
            wz_step(3)

        @pl.when(j == 1)
        def _():
            for d in (1, -1):
                wz_got(3, d)
            wx(0).start()
            wx(1).start()
            wsib(0, c).start()

        @pl.when(j == 4)
        def _():
            wx_got(0)
            wx(2).start()
            wx_got(1)
            wx(3).start()
            wsib(3, c).start()
            wsib(1, c).start()

        @pl.when(j == 6)
        def _():
            wx_got(2)
            wx_got(3)
            wsib(2, c).start()

        only(j == SHARED_AT + 1, shared_reduce)

        @pl.when(j == 2)
        def _():
            for load in loads:
                load.wait()
            for k in range(8):
                pair(k).wait_recv()

        only((j >= 2) & (j < NZ + 2), lambda: stage_experts(j - 2))
        only(j >= 3, lambda: stage_return(j - 3))
        only(j == 1, stage_tables)
        only(j == SHARED_AT, stage_shared)
        only(j == SHARED_AT + 2, shared_total)
        for t, when in ((1, 0), (2, 0), (3, 2), (4, 3)):
            only(j == when, lambda t=t: ring(t))
        return carry

    lax.fori_loop(0, NZ + 3, step, 0)

    def arrive(k, carry):
        s = lax.rem(e + k, NE)
        send(rbuf.at[s], rbuf.at[s], os_.at[0], or_.at[s], sib, y).wait_recv()
        return carry

    lax.fori_loop(1, NE, arrive, 0)
    back_rows = rbuf[:, :, pl.ds(0, FEAT)].reshape(NE * PACK, FEAT)
    pieces = rbuf[:, :, pl.ds(FEAT, 128)].reshape(NE * PACK, 128).astype(F32)
    part_of = lax.shift_right_logical(
        lax.broadcasted_iota(jnp.int32, (NE * PACK, 128), 0) & (PACK - 1), 2
    )
    extra = jnp.concatenate(
        [jnp.where(part_of == q, pieces, 0.0).astype(BF16) for q in range(4)], axis=1
    )
    both = jnp.dot(tab[0], back_rows, preferred_element_type=F32) + jnp.dot(
        tab[1], extra, preferred_element_type=F32
    )
    base_o[...] = mixed[...] + shared[...]
    out[...] = both[:ROWS] + both[ROWS:]

    for k in range(3):
        ax(k).wait_send()
        spread(sq, 0, k).wait_send()
        spread(lg, 3, k).wait_send()
    for t in range(4):
        for d in (1, -1):
            az(t, d).wait_send()
            if t < 3 or d > 0:
                bz(t, d).wait_send()
            wz(t, d).wait_send()
            tz0(t, d).wait_send()
            if t > 0:
                tz(t, d).wait_send()
        bx(t).wait_send()
        b_sib(t, c).wait_send()
        wx(t).wait_send()
        wsib(t, c).wait_send()
        tx(t).wait_send()
    for d in (0, -1, 1, -2, 2, -3, 3, 4):
        a_sib(d, c).wait_send()
    for k in range(2):
        pa(k).wait_send()
        pb2(k).wait_send()

    def drain(i, carry):
        across(i, lax.rem(z + i, NZ), c).wait_send()

        def sent(b, inner):
            to, copy = back(i, b)

            @pl.when(to != e)
            def _():
                copy.wait_send()

            return inner

        lax.fori_loop(0, NX * NC, sent, 0)
        for k in range(6):
            ag(i, k).wait_send()
            rs(i, k).wait_send()
        return carry

    lax.fori_loop(0, NZ, drain, 0)
    for k in range(8):
        pair(k).wait_send()
        sh(k).wait_send()


def mixer(ctx, opt, ids, hid, gain, router, wsh, win, wout):
    vm = pl.BlockSpec(memory_space=pltpu.VMEM)
    hbm = pl.BlockSpec(memory_space=pl.ANY)

    def pairs(*shapes):
        return [pltpu.SemaphoreType.DMA(s) for s in shapes for _ in range(2)]

    return pl.pallas_call(
        mixer_kernel,
        name="mixer_tail",
        out_shape=[jax.ShapeDtypeStruct((ROWS, FEAT), F32)] * 2,
        in_specs=[vm] * 7 + [hbm] * 2,
        out_specs=[vm] * 2,
        scratch_shapes=[
            pltpu.VMEM((NE, 16, FEAT + ROWS), BF16),
            pltpu.VMEM((NE, 16, FEAT), BF16),
            pltpu.VMEM((NY, ROWS, FEAT), F32),
            pltpu.VMEM((2, ROWS // 2, FEAT), F32),
            pltpu.VMEM((2, ROWS, FEAT), F32),
            pltpu.VMEM((4, 8, ROWS), F32),
            pltpu.VMEM((4, ROWS, ROWS), F32),
            pltpu.VMEM((ROWS, FEAT), F32),
            pltpu.VMEM((ROWS, FEAT), F32),
            pltpu.VMEM((2, 2 * ROWS, NE * PACK), BF16),
            pltpu.VMEM((NE, ROWS, FEAT), BF16),
            pltpu.VMEM((NE, ROWS), F32),
            pltpu.VMEM((NZ, CHUNK, FEAT), BF16),
            pltpu.VMEM((NZ, NY, HALF, FEAT), BF16),
            pltpu.VMEM((NZ, 2, HALF, 256), BF16),
            pltpu.VMEM((NZ, NY, HALF, FEAT), BF16),
            pltpu.VMEM((NZ, 2, HALF, FEAT), BF16),
            pltpu.VMEM((NZ, HALF, FEAT), BF16),
            pltpu.VMEM((NZ, 2, HALF, 256), BF16),
            pltpu.VMEM((NY, ROWS, FEAT), BF16),
            pltpu.VMEM((NY, ROWS, FEAT), BF16),
            pltpu.VMEM((2, ROWS // 2, FEAT), BF16),
            pltpu.VMEM((2, ROWS, FEAT), BF16),
            pltpu.VMEM((NE, 32, 3 * SPAD), BF16),
            pltpu.VMEM((2, QPAD, WIDTH), BF16),
            pltpu.VMEM((QPAD, WIDTH), BF16),
            pltpu.VMEM((NZ, NX * NC, PACK, PWIDTH), BF16),
            pltpu.VMEM((NE, PACK, PWIDTH), BF16),
            pltpu.VMEM((ROWS, 2 * SPAD), F32),
            pltpu.VMEM((CHUNK, FEAT), F32),
            pltpu.SemaphoreType.DMA((3,)),
        ]
        + pairs((3,), (8,), (8,), (8,), (4,), (4,), (4,), (6,))
        + pairs((4,), (8,), (6,), (8,), (8,), (4,), (4,))
        + pairs((8,), (6, NZ), (6, NZ), (8,), (NE,)),
        compiler_params=pltpu.CompilerParams(
            collective_id=0, has_side_effects=True, vmem_limit_bytes=VMEM_LIMIT
        ),
    )(ctx, opt, ids, hid, gain, router, wsh, win, wout)


def per_device(
    hidden_state, context, out_proj, norm_gain, router_weight,
    expert_in, expert_out, shared_in, shared_out, route_ids,
):
    gap = ((0, 0), (0, 0), (0, SPAD - SWIDTH))
    shard = jnp.concatenate(
        [
            jnp.pad(shared_in, gap).reshape(32, 2 * SPAD),
            jnp.pad(shared_out.T, ((0, 0), (0, SPAD - SWIDTH))),
        ],
        axis=1,
    )
    win = jnp.transpose(expert_in[0], (1, 2, 0))
    routed, base = mixer(
        context, out_proj.T, route_ids.T, hidden_state, norm_gain[None, :],
        router_weight.T, shard, win, expert_out[0],
    )
    return base + routed


def solution(mesh):
    return jax.shard_map(
        per_device,
        mesh=mesh,
        in_specs=(
            P("expert", "mp"),
            P("expert", "mp"),
            P("mp", "expert"),
            P("mp"),
            P("mp", None),
            P("expert", None, None, "mp"),
            P("expert", "mp", None),
            P("expert", None, "mp"),
            P("mp", "expert"),
            P("expert", None),
        ),
        out_specs=P("expert", "mp"),
        check_vma=False,
    )
```

```python
import jax
import jax.numpy as jnp
from jax import lax
from jax.experimental import pallas as pl
from jax.experimental.pallas import tpu as pltpu
from jax.sharding import PartitionSpec as P

NZ, NX, NC, NY = 8, 4, 2, 4
NE = NZ * NX * NC
ROWS, FEAT, WIDTH = 128, 512, 2048
TOP, CAP, PACK, PWIDTH = 6, 20, 16, 640
QUARTER, QPAD = 352, 768
EIGHTH = QUARTER // 2
SWIDTH, SPAD = 704, 768
CHUNK = NX * NC * CAP
HALF = CHUNK // 2
SHARED_AT = 8
ORDER = sum(d << (3 * k) for k, d in enumerate((0, 7, 1, 2, 5, 4, 3, 6)))
F32, BF16 = jnp.float32, jnp.bfloat16
VMEM_LIMIT = 64 * 1024 * 1024 - 65536


def coords():
    e = lax.axis_index("expert")
    y = lax.axis_index("mp")
    z = lax.div(e, NX * NC)
    x = lax.rem(lax.div(e, NC), NX)
    c = lax.rem(e, NC)
    return e, z, x, c, y


def eid(z, x, c):
    return z * (NX * NC) + x * NC + c


def blk(z, c, x):
    return z * (NX * NC) + c * NX + x


def send(src, dst, ssem, rsem, e, y):
    return pltpu.make_async_remote_copy(
        src_ref=src,
        dst_ref=dst,
        send_sem=ssem,
        recv_sem=rsem,
        device_id={"expert": e, "mp": y},
        device_id_type=pl.DeviceIdType.MESH,
    )


def greet(e, y):
    pl.semaphore_signal(
        pltpu.get_barrier_semaphore(),
        inc=1,
        device_id={"expert": e, "mp": y},
        device_id_type=pl.DeviceIdType.MESH,
    )


def nt(a, b):
    return lax.dot_general(a, b, (((1,), (1,)), ((), ())), preferred_element_type=F32)


def mixer_kernel(
    ctx, opt, ids, hid, gain, router, win_s, wout_s, win, wout,
    out, base_o,
    wga, wgb, part, p1, p2, sq, lg, mixed, shared, tab,
    tok, slot, xo, xg, tr, pb, ra, rb, tq, xsh, psh, s1, s2,
    wb, wi, wo, sbuf, rbuf, acc, tot,
    wsem,
    axs, axr, azs, azr, ass, asr, bzs, bzr, bxs, bxr, bss, bsr,
    ys, yr, qs, qr,
    xs, xr, z0s, z0r, zs, zr, ss, sr,
    wzs, wzr, wxs, wxr, wss, wsr,
    hs, hr, gs, gr, ps, pr, vs, vr, os_, or_,
):
    e, z, x, c, y = coords()
    xr_, xl_, xo_ = lax.rem(x + 1, NX), lax.rem(x + NX - 1, NX), lax.rem(x + 2, NX)
    to_r, to_l = eid(z, xr_, c), eid(z, xl_, c)
    to_u, to_d = eid(lax.rem(z + 1, NZ), x, c), eid(lax.rem(z + NZ - 1, NZ), x, c)
    sib = eid(z, x, 1 - c)
    yu, yd, yo = lax.rem(y + 1, NY), lax.rem(y + NY - 1, NY), lax.rem(y + 2, NY)
    left_, right_ = pl.ds(0, 256), pl.ds(256, 256)
    par = lax.rem(y, 2)
    mine = pl.ds(pl.multiple_of(par * HALF, 16), HALF)
    other = pl.ds(pl.multiple_of((1 - par) * HALF, 16), HALF)
    near = y + 1 - 2 * par
    next_ = lax.rem(y + 3 + 2 * par, NY)
    far = lax.rem(z + 4, NZ)

    def zat(d):
        return lax.rem(z + NZ + d, NZ)

    def hello(k, carry):
        greet(lax.rem(e + k, NE), y)
        return carry

    lax.fori_loop(1, NE, hello, 0)
    for t in (yu, yd, yo):
        greet(e, t)

    loads = [
        pltpu.make_async_copy(win.at[0], wi.at[0, pl.ds(0, QUARTER)], wsem.at[0]),
        pltpu.make_async_copy(win.at[1], wi.at[1, pl.ds(0, QUARTER)], wsem.at[1]),
        pltpu.make_async_copy(wout, wo.at[pl.ds(0, QUARTER)], wsem.at[2]),
    ]
    for load in loads:
        load.start()

    def wblk(zz, cc, xx):
        return cc * (NX * NZ) + xx * NZ + zz

    own, wown = blk(z, c, x), wblk(z, c, x)
    names = jnp.concatenate(
        [ids[...].astype(F32), jnp.full((ROWS - TOP, ROWS), -1.0, F32)], axis=0
    )
    wga[own, :, pl.ds(0, FEAT)] = opt[0:16, :]
    wga[own, :, pl.ds(FEAT, ROWS)] = names[:16].astype(BF16)
    wgb[wown] = opt[16:32, :]
    none = jnp.zeros((32, SPAD - SWIDTH), BF16)
    for h in range(3):
        piece = win_s[:, h, :] if h < 2 else wout_s[...]
        wb[wown, :, pl.ds(h * SPAD, SPAD)] = jnp.concatenate([piece, none], axis=1)
    pl.semaphore_wait(pltpu.get_barrier_semaphore(), NE + 2)

    def pair(k):
        src, dst, at, to, n, where = (
            (win.at[0], wi.at[0], 0, near, EIGHTH, QUARTER),
            (win.at[0], wi.at[0], EIGHTH, next_, EIGHTH, QUARTER + EIGHTH),
            (win.at[1], wi.at[1], 0, near, 80, QUARTER),
            (win.at[1], wi.at[1], EIGHTH, next_, 80, QUARTER + EIGHTH),
            (win.at[1], wi.at[1], 80, near, EIGHTH - 80, QUARTER + 80),
            (win.at[1], wi.at[1], EIGHTH + 80, next_, EIGHTH - 80, QUARTER + EIGHTH + 80),
            (wout, wo, 0, near, EIGHTH, QUARTER),
            (wout, wo, EIGHTH, next_, EIGHTH, QUARTER + EIGHTH),
        )[k]
        return send(src.at[pl.ds(at, n)], dst.at[pl.ds(where, n)], hs.at[k], hr.at[k], e, to)

    def ax(k):
        b, to = [(own, to_r), (own, to_l), (blk(z, c, xl_), to_r)][k]
        return send(wga.at[b], wga.at[b], axs.at[k], axr.at[k], to, y)

    def ax_got(k):
        b = blk(z, c, [xl_, xr_, xo_][k])
        send(wga.at[b], wga.at[b], axs.at[k], axr.at[k], to_r, y).wait_recv()

    def a_plane(p, cc, n=NX, off=0):
        return wga.at[pl.ds(p * (NX * NC) + cc * NX + off, n)]

    def az(t, d):
        p = zat(-d * t)
        r = a_plane(p, c) if t < 3 else a_plane(p, c, 2, 0 if d > 0 else 2)
        k = t if d > 0 else 4 + t
        return send(r, r, azs.at[k], azr.at[k], to_u if d > 0 else to_d, y)

    def az_got(t, d):
        p = zat(-d * (t + 1))
        r = a_plane(p, c) if t < 3 else a_plane(p, c, 2, 0 if d > 0 else 2)
        k = t if d > 0 else 4 + t
        send(r, r, azs.at[k], azr.at[k], to_u, y).wait_recv()

    def a_sib(d, cc):
        r = a_plane(zat(d), cc)
        return send(r, r, ass.at[d % NZ], asr.at[d % NZ], sib, y)

    def bz(t, d):
        r = wgb.at[wblk(zat(-d * t), c, x)]
        k = t if d > 0 else 4 + t
        return send(r, r, bzs.at[k], bzr.at[k], to_u if d > 0 else to_d, y)

    def bz_got(t, d):
        r = wgb.at[wblk(zat(-d * (t + 1)), c, x)]
        k = t if d > 0 else 4 + t
        send(r, r, bzs.at[k], bzr.at[k], to_u, y).wait_recv()

    def b_col(xx, cc, n=NZ, off=0):
        return wgb.at[pl.ds(cc * (NX * NZ) + xx * NZ + off, n)]

    def bx(k):
        r, to = [
            (b_col(x, c), to_r), (b_col(x, c), to_l),
            (b_col(xl_, c, 4, 0), to_r), (b_col(xr_, c, 4, 4), to_l),
        ][k]
        return send(r, r, bxs.at[k], bxr.at[k], to, y)

    def bx_got(k):
        r = [b_col(xl_, c), b_col(xr_, c), b_col(xo_, c, 4, 0), b_col(xo_, c, 4, 4)][k]
        send(r, r, bxs.at[k], bxr.at[k], to_r, y).wait_recv()

    xoff = (x, xr_, xo_, xl_)

    def b_sib(k, cc):
        r = b_col(xoff[k], cc)
        return send(r, r, bss.at[k], bsr.at[k], sib, y)

    for k in range(4):
        pair(k).start()
    ax(0).start()
    ax(1).start()
    bz(0, 1).start()
    bz(0, -1).start()
    ax_got(0)
    ax(2).start()
    ax_got(1)
    bz_got(0, 1)
    bz(1, 1).start()
    bz_got(0, -1)
    bz(1, -1).start()
    ax_got(2)
    az(0, 1).start()
    az(0, -1).start()
    a_sib(0, c).start()
    bz_got(1, 1)
    bz(2, 1).start()
    bz_got(1, -1)
    bz(2, -1).start()
    az_got(0, 1)
    az(1, 1).start()
    az_got(0, -1)
    az(1, -1).start()
    a_sib(-1, c).start()
    a_sib(1, c).start()
    bz_got(2, 1)
    bz(3, 1).start()
    bz_got(2, -1)
    az_got(1, 1)
    az(2, 1).start()
    az_got(1, -1)
    az(2, -1).start()
    bz_got(3, 1)
    bx(0).start()
    bx(1).start()
    a_sib(-2, c).start()
    a_sib(2, c).start()
    b_sib(0, c).start()
    az_got(2, 1)
    az(3, 1).start()
    az_got(2, -1)
    az(3, -1).start()
    a_sib(-3, c).start()
    a_sib(3, c).start()
    bx_got(0)
    bx(2).start()
    bx_got(1)
    bx(3).start()
    b_sib(3, c).start()
    b_sib(1, c).start()
    az_got(3, 1)
    az_got(3, -1)
    a_sib(4, c).start()
    bx_got(2)
    bx_got(3)
    b_sib(2, c).start()

    def wz(t, d):
        r = wb.at[wblk(zat(-d * t), c, x)]
        if t == 3:
            r = wb.at[wblk(zat(-d * t), c, x), pl.ds(0 if d > 0 else 16, 16)]
        k = t if d > 0 else 4 + t
        return send(r, r, wzs.at[k], wzr.at[k], to_u if d > 0 else to_d, y)

    def wz_got(t, d):
        r = wb.at[wblk(zat(-d * (t + 1)), c, x)]
        if t == 3:
            r = wb.at[wblk(zat(-d * (t + 1)), c, x), pl.ds(0 if d > 0 else 16, 16)]
        k = t if d > 0 else 4 + t
        send(r, r, wzs.at[k], wzr.at[k], to_u, y).wait_recv()

    def wz_step(t):
        for d in (1, -1):
            wz_got(t - 1, d)
            wz(t, d).start()

    def col(xx, cc, n=NZ, off=0):
        return wb.at[pl.ds(cc * (NX * NZ) + xx * NZ + off, n)]

    def wx(k):
        r, to = [
            (col(x, c), to_r), (col(x, c), to_l),
            (col(xl_, c, 4, 0), to_r), (col(xr_, c, 4, 4), to_l),
        ][k]
        return send(r, r, wxs.at[k], wxr.at[k], to, y)

    def wx_got(k):
        r = [col(xl_, c), col(xr_, c), col(xo_, c, 4, 0), col(xo_, c, 4, 4)][k]
        send(r, r, wxs.at[k], wxr.at[k], to_r, y).wait_recv()

    def wsib(k, cc):
        r = col(xoff[k], cc)
        return send(r, r, wss.at[k], wsr.at[k], sib, y)

    wz(0, 1).start()
    wz(0, -1).start()
    for d in (0, -1, 1, -2, 2, -3, 3, 4):
        a_sib(d, 1 - c).wait_recv()
    for k in range(NX):
        b_sib(k, 1 - c).wait_recv()

    def columns(d):
        blocks = []
        for zz in range(2):
            for xx in range(NX):
                for cc in range(NC):
                    p = 2 * d + zz
                    blocks.append(wga[blk(p, cc, xx), :, pl.ds(0, FEAT)])
                    blocks.append(wgb[wblk(p, cc, xx)])
        return nt(ctx[...], jnp.concatenate(blocks, axis=0))

    hrows = ROWS // 2
    plo, phi = pl.ds(0, hrows), pl.ds(hrows, hrows)

    def pa(k):
        rows, to = [(plo, yu), (phi, yd)][k]
        return send(part.at[yo, rows], p1.at[k], ys.at[k], yr.at[k], e, to)

    def pb2(k):
        to = [yu, yd][k]
        return send(part.at[to], p2.at[k], ys.at[2 + k], yr.at[2 + k], e, to)

    part[yo] = columns(yo)
    pa(0).start()
    pa(1).start()
    part[yu] = columns(yu)
    part[yd] = columns(yd)
    pa(0).wait_recv()
    part[yu, plo] = part[yu, plo] + p1[0]
    pb2(0).start()
    pa(1).wait_recv()
    part[yd, phi] = part[yd, phi] + p1[1]
    pb2(1).start()
    pair(4).start()
    pair(5).start()
    part[y] = columns(y)
    wz_step(1)

    def mark(b, carry):
        same = (wga[b, :, pl.ds(FEAT, ROWS)].astype(F32) == e.astype(F32)).astype(F32)
        slot[pl.ds(b, 1), :] = jnp.sum(same, axis=0, keepdims=True)
        return carry

    lax.fori_loop(0, NE, mark, 0)
    r_i = lax.broadcasted_iota(jnp.int32, (ROWS, ROWS), 0)
    c_i = lax.broadcasted_iota(jnp.int32, (ROWS, ROWS), 1)
    named = slot[...]
    rank = jnp.dot(
        named.astype(BF16), (r_i < c_i).astype(F32).astype(BF16), preferred_element_type=F32
    )
    slot[...] = jnp.where(named > 0.5, rank, -1000.0)
    gap = pl.ds(2 * QUARTER, QPAD - 2 * QUARTER)
    wi[0, gap] = jnp.zeros((QPAD - 2 * QUARTER, WIDTH), BF16)
    wi[1, gap] = jnp.zeros((QPAD - 2 * QUARTER, WIDTH), BF16)
    wo[gap] = jnp.zeros((QPAD - 2 * QUARTER, WIDTH), BF16)

    pb2(0).wait_recv()
    pb2(1).wait_recv()
    mix = hid[...].astype(F32) + (part[y] + p2[0] + p2[1])
    mixed[...] = mix

    def spread(buf, base, k):
        return send(
            buf.at[3], buf.at[k], qs.at[base + k], qr.at[base + k], e, (yu, yd, yo)[k]
        )

    sums = jnp.broadcast_to(jnp.sum(mix * mix, axis=1, keepdims=True), (ROWS, ROWS))
    sq[3] = jnp.transpose(sums)[:8]
    for k in range(3):
        spread(sq, 0, k).start()
    for k in range(6, 8):
        pair(k).start()
    wz_step(2)
    for k in range(3):
        spread(sq, 0, k).wait_recv()
    inverse = lax.rsqrt(((sq[0] + sq[1]) + (sq[2] + sq[3])) / WIDTH + 1e-06)
    inverse = jnp.transpose(jnp.broadcast_to(inverse[:1], (ROWS, ROWS)))[:, :1]
    gains = jnp.concatenate([gain[k : k + 1] for k in range(4)], axis=1)
    normed32 = mix * inverse * gains.astype(F32)
    tok[own] = normed32.astype(BF16)
    xsh[y] = normed32.astype(BF16)

    def tx(k):
        half = ROWS // 2
        r, to = [
            (tok.at[own], to_r), (tok.at[own], to_l),
            (tok.at[blk(z, c, xl_), pl.ds(0, half)], to_r),
            (tok.at[blk(z, c, xr_), pl.ds(half, half)], to_l),
        ][k]
        return send(r, r, xs.at[k], xr.at[k], to, y)

    def tx_got(k):
        half = ROWS // 2
        r = [
            tok.at[blk(z, c, xl_)], tok.at[blk(z, c, xr_)],
            tok.at[blk(z, c, xo_), pl.ds(0, half)], tok.at[blk(z, c, xo_), pl.ds(half, half)],
        ][k]
        send(r, r, xs.at[k], xr.at[k], to_r, y).wait_recv()

    def tz0(k, d):
        r = tok.at[blk(z, c, xoff[k])]
        q = k if d > 0 else NX + k
        return send(r, r, z0s.at[q], z0r.at[q], to_u if d > 0 else to_d, y)

    def tz0_got(k, d):
        r = tok.at[blk(zat(-d), c, xoff[k])]
        q = k if d > 0 else NX + k
        send(r, r, z0s.at[q], z0r.at[q], to_u, y).wait_recv()

    def plane(p, cc, n=NX, off=0):
        return tok.at[pl.ds(p * (NX * NC) + cc * NX + off, n)]

    def tz(t, d):
        p = zat(-d * t)
        r = plane(p, c) if t < 3 else plane(p, c, 2, 0 if d > 0 else 2)
        k = t - 1 if d > 0 else 2 + t
        return send(r, r, zs.at[k], zr.at[k], to_u if d > 0 else to_d, y)

    def tz_got(t, d):
        p = zat(-d * (t + 1))
        r = plane(p, c) if t < 3 else plane(p, c, 2, 0 if d > 0 else 2)
        k = t - 1 if d > 0 else 2 + t
        send(r, r, zs.at[k], zr.at[k], to_u, y).wait_recv()

    def across(d, p, cc):
        r = plane(p, cc)
        return send(r, r, ss.at[d], sr.at[d], sib, y)

    def ag(i, k, copy=True):
        src, dst, to = (
            (xo.at[i, other], xg.at[i, y if copy else yd], yu),
            (xo.at[i, other], xg.at[i, y if copy else yu], yd),
            (xo.at[i, mine, left_], tr.at[i, 0], yu),
            (xo.at[i, mine, right_], tr.at[i, 1], yd),
            (tr.at[i, 0], xg.at[i, yd if copy else yo, :, left_], yu),
            (tr.at[i, 1], xg.at[i, yu if copy else yo, :, right_], yd),
        )[k]
        return send(src, dst, gs.at[k, i], gr.at[k, i], e, to)

    def rs(i, k):
        src, dst, to = (
            (pb.at[i, yu], ra.at[i, 0], yu),
            (pb.at[i, yd], ra.at[i, 1], yd),
            (pb.at[i, yo, :, left_], tq.at[i, 0], yu),
            (pb.at[i, yo, :, right_], tq.at[i, 1], yd),
            (tq.at[i, 0], rb.at[i, :, left_], yu),
            (tq.at[i, 1], rb.at[i, :, right_], yd),
        )[k]
        return send(src, dst, ps.at[k, i], pr.at[k, i], e, to)

    def sh(k, who=None):
        src, dst, to = (
            (xsh.at[y], xsh.at[y if who is None else who], yu),
            (xsh.at[y], xsh.at[y if who is None else who], yd),
            (xsh.at[yd, plo], xsh.at[yd if who is None else who, plo], yu),
            (xsh.at[yu, phi], xsh.at[yu if who is None else who, phi], yd),
            (psh.at[yo, plo], s1.at[0], yu),
            (psh.at[yo, phi], s1.at[1], yd),
            (psh.at[yu], s2.at[0], yu),
            (psh.at[yd], s2.at[1], yd),
        )[k]
        return send(src, dst, vs.at[k], vr.at[k], e, to)

    tx(0).start()
    tx(1).start()
    tz0(0, 1).start()
    tz0(0, -1).start()
    sh(0).start()
    sh(1).start()
    wide = jnp.concatenate([router[...], jnp.zeros((ROWS - NE, FEAT), F32)], axis=0)
    lg[3] = lax.dot_general(
        normed32, wide, (((1,), (1,)), ((), ())),
        precision=lax.Precision.HIGHEST, preferred_element_type=F32,
    )
    for k in range(3):
        spread(lg, 3, k).start()
    tx_got(0)
    tx(2).start()
    tz0(3, 1).start()
    tz0(3, -1).start()
    tx_got(1)
    tx(3).start()
    tz0(1, 1).start()
    tz0(1, -1).start()
    tx_got(2)
    tx_got(3)
    tz0(2, 1).start()
    tz0(2, -1).start()
    across(0, z, c).start()

    def ring(t):
        for d in (1, -1):
            if t == 1:
                for k in (0, 3, 1, 2):
                    tz0_got(k, d)
            else:
                tz_got(t - 1, d)
            if t < 4:
                tz(t, d).start()
                p = zat(-d * t)
                across((-d * t) % NZ, p, c).start()
        if t == 4:
            across(4, far, c).start()

    def offset_of(k):
        return lax.shift_right_logical(jnp.int32(ORDER), 3 * k) & 7

    def plane_of(k):
        return lax.rem(z + offset_of(k), NZ)

    def stage_rows(i):
        p = plane_of(i)
        across(offset_of(i), p, 1 - c).wait_recv()
        rows = lax.broadcasted_iota(jnp.int32, (CHUNK, ROWS), 0).astype(F32)
        total = jnp.zeros((CHUNK, FEAT), F32)
        for b in range(0, NX * NC, 2):
            k = p * (NX * NC) + b
            onehot = jnp.concatenate(
                [
                    (rows == slot[pl.ds(k + h, 1), :] + float(CAP * (b + h))).astype(F32)
                    for h in range(2)
                ],
                axis=1,
            ).astype(BF16)
            pair = tok[pl.ds(k, 2)].reshape(2 * ROWS, FEAT)
            total = total + jnp.dot(onehot, pair, preferred_element_type=F32)
        xo[i] = total.astype(BF16)
        for k in (2, 3, 0, 1):
            ag(i, k).start()
        xg[i, y] = xo[i, mine]

    def stage_relay(i):
        for k in (2, 3):
            ag(i, k, False).wait_recv()
            ag(i, k + 2).start()

    def gated(gate, value):
        return (gate / (1.0 + jnp.exp(-gate)) * value).astype(BF16)

    def stage_experts(i):
        for k in (0, 1, 4, 5):
            ag(i, k, False).wait_recv()
        both = []
        for h in range(2):
            total = jnp.zeros((HALF, QPAD), F32)
            for k in range(NY):
                total = total + nt(xg[i, k], wi[h, :, k * FEAT : (k + 1) * FEAT])
            both.append(total)
        hidden = gated(both[0], both[1])

        def down(k, carry):
            d = lax.rem(yo + k, NY)
            w = wo[:, pl.ds(pl.multiple_of(d * FEAT, FEAT), FEAT)]
            pb[i, d] = jnp.dot(hidden, w, preferred_element_type=F32).astype(BF16)
            return carry

        lax.fori_loop(0, 1, down, 0)
        rs(i, 2).start()
        rs(i, 3).start()
        lax.fori_loop(1, NY, down, 0)
        rs(i, 0).start()
        rs(i, 1).start()

    def stage_shared():
        sh(2, yo).wait_recv()
        sh(3, yo).wait_recv()
        for k in range(NX):
            wsib(k, 1 - c).wait_recv()
        acc[...] = jnp.zeros((ROWS, 2 * SPAD), F32)

        def into(zz, carry):
            w = jnp.concatenate(
                [
                    wb[wblk(zz, cc, xx), :, pl.ds(0, 2 * SPAD)]
                    for xx in range(NX)
                    for cc in range(NC)
                ],
                axis=0,
            )
            off = pl.multiple_of(lax.rem(zz, 2) * 256, 256)
            acc[...] += jnp.dot(
                xsh[lax.div(zz, 2), :, pl.ds(off, 256)],
                w,
                preferred_element_type=F32,
            )
            return carry

        lax.fori_loop(0, NZ, into, 0)
        hidden = gated(acc[:, :SPAD], acc[:, SPAD:])

        def project(k, carry):
            d = lax.rem(yo + k, NY)
            w = jnp.concatenate(
                [
                    wb[wblk(2 * d + zz, cc, xx), :, pl.ds(2 * SPAD, SPAD)]
                    for zz in range(2)
                    for xx in range(NX)
                    for cc in range(NC)
                ],
                axis=0,
            )
            psh[d] = nt(hidden, w).astype(BF16)
            return carry

        lax.fori_loop(0, NY, project, 0)
        sh(4).start()
        sh(5).start()

    def stage_reduce(i):
        for k in (2, 3):
            rs(i, k).wait_recv()
            rs(i, k + 2).start()

    def shared_relay():
        sh(0, yd).wait_recv()
        sh(2).start()
        sh(1, yu).wait_recv()
        sh(3).start()

    def shared_reduce():
        sh(4).wait_recv()
        psh[yu, plo] = (psh[yu, plo].astype(F32) + s1[0].astype(F32)).astype(BF16)
        sh(6).start()
        sh(5).wait_recv()
        psh[yd, phi] = (psh[yd, phi].astype(F32) + s1[1].astype(F32)).astype(BF16)
        sh(7).start()

    def shared_total():
        sh(6).wait_recv()
        sh(7).wait_recv()
        shared[...] = psh[y].astype(F32) + s2[0].astype(F32) + s2[1].astype(F32)

    def back(i, b):
        to = eid(plane_of(i), lax.rem(b, NX), lax.div(b, NX))
        return to, send(sbuf.at[i, b], rbuf.at[e], os_.at[i * (NX * NC) + b], or_.at[e], to, y)

    def stage_return(i):
        for k in (0, 1, 4, 5):
            rs(i, k).wait_recv()
        tot[mine] = pb[i, y].astype(F32) + rb[i].astype(F32)
        tot[other] = ra[i, 0].astype(F32) + ra[i, 1].astype(F32)
        total = tot[...].astype(BF16)
        to_row = lax.broadcasted_iota(jnp.int32, (ROWS, CHUNK), 0)
        of_row = lax.broadcasted_iota(jnp.int32, (ROWS, CHUNK), 1)
        base = CAP * lax.shift_right_logical(to_row, 4)
        inner = to_row & (PACK - 1)

        def move(hit, values):
            return jnp.dot(hit.astype(F32).astype(BF16), values, preferred_element_type=F32)

        first = move(of_row == base + inner, total)
        sbuf[i, :, :, pl.ds(0, FEAT)] = first.astype(BF16).reshape(NX * NC, PACK, FEAT)
        last = jnp.zeros((ROWS, ROWS), F32)
        for q in range(4):
            hit = (of_row == base + PACK + inner - 4 * q) & (inner >= 4 * q) & (inner < 4 * q + 4)
            last = last + move(hit, total[:, q * 128 : (q + 1) * 128])
        sbuf[i, :, :, pl.ds(FEAT, 128)] = last.astype(BF16).reshape(NX * NC, PACK, 128)

        def go(b, carry):
            to, copy = back(i, b)

            @pl.when(to != e)
            def _():
                copy.start()

            @pl.when(to == e)
            def _():
                rbuf[e] = sbuf[i, b]

            return carry

        lax.fori_loop(0, NX * NC, go, 0)

    def stage_tables():
        for k in range(3):
            spread(lg, 3, k).wait_recv()
        logits = (lg[0] + lg[1]) + (lg[2] + lg[3])
        mine = jnp.transpose(names)
        lane = c_i.astype(F32)
        count = jnp.zeros((ROWS, ROWS), F32)
        for k in range(TOP):
            count = count + (mine[:, k : k + 1] == lane).astype(F32)
        chosen = count > 0.5
        top = jnp.max(jnp.where(chosen, logits, -jnp.inf), axis=1, keepdims=True)
        weight = jnp.where(chosen, jnp.exp(jnp.where(chosen, logits - top, 0.0)), 0.0)
        gates = weight / jnp.sum(weight, axis=1, keepdims=True)
        place = jnp.dot(
            (c_i < r_i).astype(F32).astype(BF16), count.astype(BF16), preferred_element_type=F32
        )
        place = jnp.where(chosen, place, 255.0).astype(BF16)
        high = gates.astype(BF16)
        low = (gates - high.astype(F32)).astype(BF16)

        def fill(b, carry):
            ee = lax.broadcasted_iota(jnp.int32, (ROWS, 256), 0)
            jj = lax.broadcasted_iota(jnp.int32, (ROWS, 256), 1)
            inner = jj & (PACK - 1)
            mat = (ee == lax.shift_right_logical(jj, 4) + b * PACK).astype(F32).astype(BF16)
            where = jnp.dot(place, mat, preferred_element_type=F32)
            at = pl.ds(pl.multiple_of(b * 256, 256), 256)
            for h, g in enumerate((high, low)):
                spaced = jnp.dot(g, mat, preferred_element_type=F32)
                for q, want in enumerate((inner, PACK + (inner & 3))):
                    hit = jnp.where(where == want.astype(F32), spaced, 0.0)
                    tab[q, pl.ds(h * ROWS, ROWS), at] = hit.astype(BF16)
            return carry

        lax.fori_loop(0, NE * PACK // 256, fill, 0)

    def step(j, carry):
        @pl.when((j >= 1) & (j < NZ + 1))
        def _():
            stage_relay(j - 1)

        @pl.when(j < NZ)
        def _():
            stage_rows(j)

        @pl.when(j == 0)
        def _():
            shared_relay()
            wz_step(3)

        @pl.when(j == 1)
        def _():
            for d in (1, -1):
                wz_got(3, d)
            wx(0).start()
            wx(1).start()
            wsib(0, c).start()

        @pl.when(j == 5)
        def _():
            wx_got(0)
            wx(2).start()
            wx_got(1)
            wx(3).start()
            wsib(3, c).start()
            wsib(1, c).start()

        @pl.when(j == 7)
        def _():
            wx_got(2)
            wx_got(3)
            wsib(2, c).start()

        @pl.when(j == 2)
        def _():
            for load in loads:
                load.wait()
            for k in range(8):
                pair(k).wait_recv()

        @pl.when((j >= 2) & (j < NZ + 2))
        def _():
            stage_experts(j - 2)

        @pl.when((j >= 3) & (j < NZ + 3))
        def _():
            stage_reduce(j - 3)

        @pl.when(j >= 4)
        def _():
            stage_return(j - 4)

        @pl.when(j == 1)
        def _():
            stage_tables()

        @pl.when(j == SHARED_AT)
        def _():
            stage_shared()

        @pl.when(j == SHARED_AT + 1)
        def _():
            shared_reduce()

        @pl.when(j == SHARED_AT + 2)
        def _():
            shared_total()

        for t, at in ((1, 0), (2, 2), (3, 3), (4, 4)):

            @pl.when(j == at)
            def _(t=t):
                ring(t)

        return carry

    lax.fori_loop(0, NZ + 4, step, 0)

    def arrive(k, carry):
        s = lax.rem(e + k, NE)
        send(rbuf.at[s], rbuf.at[s], os_.at[0], or_.at[s], sib, y).wait_recv()
        return carry

    lax.fori_loop(1, NE, arrive, 0)
    back_rows = rbuf[:, :, pl.ds(0, FEAT)].reshape(NE * PACK, FEAT)
    pieces = rbuf[:, :, pl.ds(FEAT, 128)].reshape(NE * PACK, 128).astype(F32)
    part_of = lax.shift_right_logical(
        lax.broadcasted_iota(jnp.int32, (NE * PACK, 128), 0) & (PACK - 1), 2
    )
    extra = jnp.concatenate(
        [jnp.where(part_of == q, pieces, 0.0).astype(BF16) for q in range(4)], axis=1
    )
    both = jnp.dot(tab[0], back_rows, preferred_element_type=F32) + jnp.dot(
        tab[1], extra, preferred_element_type=F32
    )
    base_o[...] = mixed[...] + shared[...]
    out[...] = both[:ROWS] + both[ROWS:]

    for k in range(3):
        ax(k).wait_send()
        spread(sq, 0, k).wait_send()
        spread(lg, 3, k).wait_send()
    for t in range(4):
        for d in (1, -1):
            az(t, d).wait_send()
            if t < 3 or d > 0:
                bz(t, d).wait_send()
            wz(t, d).wait_send()
            tz0(t, d).wait_send()
            if t > 0:
                tz(t, d).wait_send()
        bx(t).wait_send()
        b_sib(t, c).wait_send()
        wx(t).wait_send()
        wsib(t, c).wait_send()
        tx(t).wait_send()
    for d in (0, -1, 1, -2, 2, -3, 3, 4):
        a_sib(d, c).wait_send()
    for k in range(2):
        pa(k).wait_send()
        pb2(k).wait_send()

    def drain(i, carry):
        across(i, lax.rem(z + i, NZ), c).wait_send()

        def sent(b, inner):
            to, copy = back(i, b)

            @pl.when(to != e)
            def _():
                copy.wait_send()

            return inner

        lax.fori_loop(0, NX * NC, sent, 0)
        for k in range(6):
            ag(i, k).wait_send()
            rs(i, k).wait_send()
        return carry

    lax.fori_loop(0, NZ, drain, 0)
    for k in range(8):
        pair(k).wait_send()
        sh(k).wait_send()


def mixer(ctx, opt, ids, hid, gain, router, win_s, wout_s, win, wout):
    vm = pl.BlockSpec(memory_space=pltpu.VMEM)
    hbm = pl.BlockSpec(memory_space=pl.ANY)

    def pairs(*shapes):
        return [pltpu.SemaphoreType.DMA(s) for s in shapes for _ in range(2)]

    return pl.pallas_call(
        mixer_kernel,
        name="mixer_tail",
        out_shape=[jax.ShapeDtypeStruct((ROWS, FEAT), F32)] * 2,
        in_specs=[vm] * 8 + [hbm] * 2,
        out_specs=[vm] * 2,
        scratch_shapes=[
            pltpu.VMEM((NE, 16, FEAT + ROWS), BF16),
            pltpu.VMEM((NE, 16, FEAT), BF16),
            pltpu.VMEM((NY, ROWS, FEAT), F32),
            pltpu.VMEM((2, ROWS // 2, FEAT), F32),
            pltpu.VMEM((2, ROWS, FEAT), F32),
            pltpu.VMEM((4, 8, ROWS), F32),
            pltpu.VMEM((4, ROWS, ROWS), F32),
            pltpu.VMEM((ROWS, FEAT), F32),
            pltpu.VMEM((ROWS, FEAT), F32),
            pltpu.VMEM((2, 2 * ROWS, NE * PACK), BF16),
            pltpu.VMEM((NE, ROWS, FEAT), BF16),
            pltpu.VMEM((NE, ROWS), F32),
            pltpu.VMEM((NZ, CHUNK, FEAT), BF16),
            pltpu.VMEM((NZ, NY, HALF, FEAT), BF16),
            pltpu.VMEM((NZ, 2, HALF, 256), BF16),
            pltpu.VMEM((NZ, NY, HALF, FEAT), BF16),
            pltpu.VMEM((NZ, 2, HALF, FEAT), BF16),
            pltpu.VMEM((NZ, HALF, FEAT), BF16),
            pltpu.VMEM((NZ, 2, HALF, 256), BF16),
            pltpu.VMEM((NY, ROWS, FEAT), BF16),
            pltpu.VMEM((NY, ROWS, FEAT), BF16),
            pltpu.VMEM((2, ROWS // 2, FEAT), BF16),
            pltpu.VMEM((2, ROWS, FEAT), BF16),
            pltpu.VMEM((NE, 32, 3 * SPAD), BF16),
            pltpu.VMEM((2, QPAD, WIDTH), BF16),
            pltpu.VMEM((QPAD, WIDTH), BF16),
            pltpu.VMEM((NZ, NX * NC, PACK, PWIDTH), BF16),
            pltpu.VMEM((NE, PACK, PWIDTH), BF16),
            pltpu.VMEM((ROWS, 2 * SPAD), F32),
            pltpu.VMEM((CHUNK, FEAT), F32),
            pltpu.SemaphoreType.DMA((3,)),
        ]
        + pairs((3,), (8,), (8,), (8,), (4,), (4,), (4,), (6,))
        + pairs((4,), (8,), (6,), (8,), (8,), (4,), (4,))
        + pairs((8,), (6, NZ), (6, NZ), (8,), (NE,)),
        compiler_params=pltpu.CompilerParams(
            collective_id=0, has_side_effects=True, vmem_limit_bytes=VMEM_LIMIT
        ),
    )(ctx, opt, ids, hid, gain, router, win_s, wout_s, win, wout)


def per_device(
    hidden_state, context, out_proj, norm_gain, router_weight,
    expert_in, expert_out, shared_in, shared_out, route_ids,
):
    win = jnp.transpose(expert_in[0], (1, 2, 0))
    routed, base = mixer(
        context, out_proj.T, route_ids.T, hidden_state, norm_gain.reshape(4, 128),
        router_weight.T, shared_in, shared_out.T, win, expert_out[0],
    )
    return base + routed


def solution(mesh):
    return jax.shard_map(
        per_device,
        mesh=mesh,
        in_specs=(
            P("expert", "mp"),
            P("expert", "mp"),
            P("mp", "expert"),
            P("mp"),
            P("mp", None),
            P("expert", None, None, "mp"),
            P("expert", "mp", None),
            P("expert", None, "mp"),
            P("mp", "expert"),
            P("expert", None),
        ),
        out_specs=P("expert", "mp"),
        check_vma=False,
    )
```

```python
import jax
import jax.numpy as jnp
from jax import lax
from jax.experimental import pallas as pl
from jax.experimental.pallas import tpu as pltpu
from jax.sharding import PartitionSpec as P

NZ, NX, NC, NY = 8, 4, 2, 4
NE = NZ * NX * NC
ROWS, FEAT, WIDTH = 128, 512, 2048
TOP, CAP, PACK, PWIDTH = 6, 20, 16, 640
QUARTER, QPAD = 352, 768
EIGHTH = QUARTER // 2
SWIDTH, SPAD = 704, 768
CHUNK = NX * NC * CAP
HALF = CHUNK // 2
SHARED_AT = 8
ORDER = sum(d << (3 * k) for k, d in enumerate((0, 7, 1, 2, 5, 4, 3, 6)))
F32, BF16 = jnp.float32, jnp.bfloat16
VMEM_LIMIT = 64 * 1024 * 1024 - 65536


def coords():
    e = lax.axis_index("expert")
    y = lax.axis_index("mp")
    z = lax.div(e, NX * NC)
    x = lax.rem(lax.div(e, NC), NX)
    c = lax.rem(e, NC)
    return e, z, x, c, y


def eid(z, x, c):
    return z * (NX * NC) + x * NC + c


def blk(z, c, x):
    return z * (NX * NC) + c * NX + x


def send(src, dst, ssem, rsem, e, y):
    return pltpu.make_async_remote_copy(
        src_ref=src,
        dst_ref=dst,
        send_sem=ssem,
        recv_sem=rsem,
        device_id={"expert": e, "mp": y},
        device_id_type=pl.DeviceIdType.MESH,
    )


def greet(e, y):
    pl.semaphore_signal(
        pltpu.get_barrier_semaphore(),
        inc=1,
        device_id={"expert": e, "mp": y},
        device_id_type=pl.DeviceIdType.MESH,
    )


def nt(a, b):
    return lax.dot_general(a, b, (((1,), (1,)), ((), ())), preferred_element_type=F32)


def mixer_kernel(
    ctx, opt, ids, hid, gain, router, win_s, wout_s, win, wout,
    out, base_o,
    wga, wgb, part, p1, p2, sq, lg, mixed, shared, tab,
    tok, slot, xo, xg, tr, pb, ra, rb, tq, xsh, psh, s1, s2,
    wb, wi, wo, sbuf, rbuf, acc, tot,
    wsem,
    axs, axr, azs, azr, ass, asr, bzs, bzr, bxs, bxr, bss, bsr,
    ys, yr, qs, qr,
    xs, xr, z0s, z0r, zs, zr, ss, sr,
    wzs, wzr, wxs, wxr, wss, wsr,
    hs, hr, gs, gr, ps, pr, vs, vr, os_, or_,
):
    e, z, x, c, y = coords()
    xr_, xl_, xo_ = lax.rem(x + 1, NX), lax.rem(x + NX - 1, NX), lax.rem(x + 2, NX)
    to_r, to_l = eid(z, xr_, c), eid(z, xl_, c)
    to_u, to_d = eid(lax.rem(z + 1, NZ), x, c), eid(lax.rem(z + NZ - 1, NZ), x, c)
    sib = eid(z, x, 1 - c)
    yu, yd, yo = lax.rem(y + 1, NY), lax.rem(y + NY - 1, NY), lax.rem(y + 2, NY)
    left_, right_ = pl.ds(0, 256), pl.ds(256, 256)
    par = lax.rem(y, 2)
    mine = pl.ds(pl.multiple_of(par * HALF, 16), HALF)
    other = pl.ds(pl.multiple_of((1 - par) * HALF, 16), HALF)
    near = y + 1 - 2 * par
    next_ = lax.rem(y + 3 + 2 * par, NY)
    far = lax.rem(z + 4, NZ)

    def zat(d):
        return lax.rem(z + NZ + d, NZ)

    def hello(k, carry):
        greet(lax.rem(e + k, NE), y)
        return carry

    lax.fori_loop(1, NE, hello, 0)
    for t in (yu, yd, yo):
        greet(e, t)

    loads = [
        pltpu.make_async_copy(win.at[0], wi.at[0, pl.ds(0, QUARTER)], wsem.at[0]),
        pltpu.make_async_copy(win.at[1], wi.at[1, pl.ds(0, QUARTER)], wsem.at[1]),
        pltpu.make_async_copy(wout, wo.at[pl.ds(0, QUARTER)], wsem.at[2]),
    ]
    for load in loads:
        load.start()

    def wblk(zz, cc, xx):
        return cc * (NX * NZ) + xx * NZ + zz

    own, wown = blk(z, c, x), wblk(z, c, x)
    names = jnp.concatenate(
        [ids[...].astype(F32), jnp.full((ROWS - TOP, ROWS), -1.0, F32)], axis=0
    )
    wga[own, :, pl.ds(0, FEAT)] = opt[0:16, :]
    wga[own, :, pl.ds(FEAT, ROWS)] = names[:16].astype(BF16)
    wgb[wown] = opt[16:32, :]
    none = jnp.zeros((32, SPAD - SWIDTH), BF16)
    for h in range(3):
        piece = win_s[:, h, :] if h < 2 else wout_s[...]
        wb[wown, :, pl.ds(h * SPAD, SPAD)] = jnp.concatenate([piece, none], axis=1)
    pl.semaphore_wait(pltpu.get_barrier_semaphore(), NE + 2)

    def pair(k):
        src, dst, at, to, n, where = (
            (win.at[0], wi.at[0], 0, near, EIGHTH, QUARTER),
            (win.at[0], wi.at[0], EIGHTH, next_, EIGHTH, QUARTER + EIGHTH),
            (win.at[1], wi.at[1], 0, near, 80, QUARTER),
            (win.at[1], wi.at[1], EIGHTH, next_, 80, QUARTER + EIGHTH),
            (win.at[1], wi.at[1], 80, near, EIGHTH - 80, QUARTER + 80),
            (win.at[1], wi.at[1], EIGHTH + 80, next_, EIGHTH - 80, QUARTER + EIGHTH + 80),
            (wout, wo, 0, near, EIGHTH, QUARTER),
            (wout, wo, EIGHTH, next_, EIGHTH, QUARTER + EIGHTH),
        )[k]
        return send(src.at[pl.ds(at, n)], dst.at[pl.ds(where, n)], hs.at[k], hr.at[k], e, to)

    def ax(k):
        b, to = [(own, to_r), (own, to_l), (blk(z, c, xl_), to_r)][k]
        return send(wga.at[b], wga.at[b], axs.at[k], axr.at[k], to, y)

    def ax_got(k):
        b = blk(z, c, [xl_, xr_, xo_][k])
        send(wga.at[b], wga.at[b], axs.at[k], axr.at[k], to_r, y).wait_recv()

    def a_plane(p, cc, n=NX, off=0):
        return wga.at[pl.ds(p * (NX * NC) + cc * NX + off, n)]

    def az(t, d):
        p = zat(-d * t)
        r = a_plane(p, c) if t < 3 else a_plane(p, c, 2, 0 if d > 0 else 2)
        k = t if d > 0 else 4 + t
        return send(r, r, azs.at[k], azr.at[k], to_u if d > 0 else to_d, y)

    def az_got(t, d):
        p = zat(-d * (t + 1))
        r = a_plane(p, c) if t < 3 else a_plane(p, c, 2, 0 if d > 0 else 2)
        k = t if d > 0 else 4 + t
        send(r, r, azs.at[k], azr.at[k], to_u, y).wait_recv()

    def a_sib(d, cc):
        r = a_plane(zat(d), cc)
        return send(r, r, ass.at[d % NZ], asr.at[d % NZ], sib, y)

    def bz(t, d):
        r = wgb.at[wblk(zat(-d * t), c, x)]
        k = t if d > 0 else 4 + t
        return send(r, r, bzs.at[k], bzr.at[k], to_u if d > 0 else to_d, y)

    def bz_got(t, d):
        r = wgb.at[wblk(zat(-d * (t + 1)), c, x)]
        k = t if d > 0 else 4 + t
        send(r, r, bzs.at[k], bzr.at[k], to_u, y).wait_recv()

    def b_col(xx, cc, n=NZ, off=0):
        return wgb.at[pl.ds(cc * (NX * NZ) + xx * NZ + off, n)]

    def bx(k):
        r, to = [
            (b_col(x, c), to_r), (b_col(x, c), to_l),
            (b_col(xl_, c, 4, 0), to_r), (b_col(xr_, c, 4, 4), to_l),
        ][k]
        return send(r, r, bxs.at[k], bxr.at[k], to, y)

    def bx_got(k):
        r = [b_col(xl_, c), b_col(xr_, c), b_col(xo_, c, 4, 0), b_col(xo_, c, 4, 4)][k]
        send(r, r, bxs.at[k], bxr.at[k], to_r, y).wait_recv()

    xoff = (x, xr_, xo_, xl_)

    def b_sib(k, cc):
        r = b_col(xoff[k], cc)
        return send(r, r, bss.at[k], bsr.at[k], sib, y)

    for k in range(4):
        pair(k).start()
    ax(0).start()
    ax(1).start()
    bz(0, 1).start()
    bz(0, -1).start()
    ax_got(0)
    ax(2).start()
    ax_got(1)
    bz_got(0, 1)
    bz(1, 1).start()
    bz_got(0, -1)
    bz(1, -1).start()
    ax_got(2)
    az(0, 1).start()
    az(0, -1).start()
    a_sib(0, c).start()
    bz_got(1, 1)
    bz(2, 1).start()
    bz_got(1, -1)
    bz(2, -1).start()
    az_got(0, 1)
    az(1, 1).start()
    az_got(0, -1)
    az(1, -1).start()
    a_sib(-1, c).start()
    a_sib(1, c).start()
    bz_got(2, 1)
    bz(3, 1).start()
    bz_got(2, -1)
    az_got(1, 1)
    az(2, 1).start()
    az_got(1, -1)
    az(2, -1).start()
    bz_got(3, 1)
    bx(0).start()
    bx(1).start()
    a_sib(-2, c).start()
    a_sib(2, c).start()
    b_sib(0, c).start()
    az_got(2, 1)
    az(3, 1).start()
    az_got(2, -1)
    az(3, -1).start()
    a_sib(-3, c).start()
    a_sib(3, c).start()
    bx_got(0)
    bx(2).start()
    bx_got(1)
    bx(3).start()
    b_sib(3, c).start()
    b_sib(1, c).start()
    az_got(3, 1)
    az_got(3, -1)
    a_sib(4, c).start()
    bx_got(2)
    bx_got(3)
    b_sib(2, c).start()

    def wz(t, d):
        r = wb.at[wblk(zat(-d * t), c, x)]
        if t == 3:
            r = wb.at[wblk(zat(-d * t), c, x), pl.ds(0 if d > 0 else 16, 16)]
        k = t if d > 0 else 4 + t
        return send(r, r, wzs.at[k], wzr.at[k], to_u if d > 0 else to_d, y)

    def wz_got(t, d):
        r = wb.at[wblk(zat(-d * (t + 1)), c, x)]
        if t == 3:
            r = wb.at[wblk(zat(-d * (t + 1)), c, x), pl.ds(0 if d > 0 else 16, 16)]
        k = t if d > 0 else 4 + t
        send(r, r, wzs.at[k], wzr.at[k], to_u, y).wait_recv()

    def wz_step(t):
        for d in (1, -1):
            wz_got(t - 1, d)
            wz(t, d).start()

    def col(xx, cc, n=NZ, off=0):
        return wb.at[pl.ds(cc * (NX * NZ) + xx * NZ + off, n)]

    def wx(k):
        r, to = [
            (col(x, c), to_r), (col(x, c), to_l),
            (col(xl_, c, 4, 0), to_r), (col(xr_, c, 4, 4), to_l),
        ][k]
        return send(r, r, wxs.at[k], wxr.at[k], to, y)

    def wx_got(k):
        r = [col(xl_, c), col(xr_, c), col(xo_, c, 4, 0), col(xo_, c, 4, 4)][k]
        send(r, r, wxs.at[k], wxr.at[k], to_r, y).wait_recv()

    def wsib(k, cc):
        r = col(xoff[k], cc)
        return send(r, r, wss.at[k], wsr.at[k], sib, y)

    wz(0, 1).start()
    wz(0, -1).start()
    for d in (0, -1, 1, -2, 2, -3, 3, 4):
        a_sib(d, 1 - c).wait_recv()
    for k in range(NX):
        b_sib(k, 1 - c).wait_recv()

    def columns(d):
        blocks = []
        for zz in range(2):
            for xx in range(NX):
                for cc in range(NC):
                    p = 2 * d + zz
                    blocks.append(wga[blk(p, cc, xx), :, pl.ds(0, FEAT)])
                    blocks.append(wgb[wblk(p, cc, xx)])
        return nt(ctx[...], jnp.concatenate(blocks, axis=0))

    hrows = ROWS // 2
    plo, phi = pl.ds(0, hrows), pl.ds(hrows, hrows)

    def pa(k):
        rows, to = [(plo, yu), (phi, yd)][k]
        return send(part.at[yo, rows], p1.at[k], ys.at[k], yr.at[k], e, to)

    def pb2(k):
        to = [yu, yd][k]
        return send(part.at[to], p2.at[k], ys.at[2 + k], yr.at[2 + k], e, to)

    part[yo] = columns(yo)
    pa(0).start()
    pa(1).start()
    part[yu] = columns(yu)
    part[yd] = columns(yd)
    pa(0).wait_recv()
    part[yu, plo] = part[yu, plo] + p1[0]
    pb2(0).start()
    pa(1).wait_recv()
    part[yd, phi] = part[yd, phi] + p1[1]
    pb2(1).start()
    pair(4).start()
    pair(5).start()
    part[y] = columns(y)
    wz_step(1)

    def mark(b, carry):
        same = (wga[b, :, pl.ds(FEAT, ROWS)].astype(F32) == e.astype(F32)).astype(F32)
        slot[pl.ds(b, 1), :] = jnp.sum(same, axis=0, keepdims=True)
        return carry

    lax.fori_loop(0, NE, mark, 0)
    r_i = lax.broadcasted_iota(jnp.int32, (ROWS, ROWS), 0)
    c_i = lax.broadcasted_iota(jnp.int32, (ROWS, ROWS), 1)
    named = slot[...]
    rank = jnp.dot(
        named.astype(BF16), (r_i < c_i).astype(F32).astype(BF16), preferred_element_type=F32
    )
    slot[...] = jnp.where(named > 0.5, rank, -1000.0)
    gap = pl.ds(2 * QUARTER, QPAD - 2 * QUARTER)
    wi[0, gap] = jnp.zeros((QPAD - 2 * QUARTER, WIDTH), BF16)
    wi[1, gap] = jnp.zeros((QPAD - 2 * QUARTER, WIDTH), BF16)
    wo[gap] = jnp.zeros((QPAD - 2 * QUARTER, WIDTH), BF16)

    pb2(0).wait_recv()
    pb2(1).wait_recv()
    mix = hid[...].astype(F32) + (part[y] + p2[0] + p2[1])
    mixed[...] = mix

    def spread(buf, base, k):
        return send(
            buf.at[3], buf.at[k], qs.at[base + k], qr.at[base + k], e, (yu, yd, yo)[k]
        )

    sums = jnp.broadcast_to(jnp.sum(mix * mix, axis=1, keepdims=True), (ROWS, ROWS))
    sq[3] = jnp.transpose(sums)[:8]
    for k in range(3):
        spread(sq, 0, k).start()
    for k in range(6, 8):
        pair(k).start()
    wz_step(2)
    for k in range(3):
        spread(sq, 0, k).wait_recv()
    inverse = lax.rsqrt(((sq[0] + sq[1]) + (sq[2] + sq[3])) / WIDTH + 1e-06)
    inverse = jnp.transpose(jnp.broadcast_to(inverse[:1], (ROWS, ROWS)))[:, :1]
    gains = jnp.concatenate([gain[k : k + 1] for k in range(4)], axis=1)
    normed32 = mix * inverse * gains.astype(F32)
    tok[own] = normed32.astype(BF16)
    xsh[y] = normed32.astype(BF16)

    def tx(k):
        half = ROWS // 2
        r, to = [
            (tok.at[own], to_r), (tok.at[own], to_l),
            (tok.at[blk(z, c, xl_), pl.ds(0, half)], to_r),
            (tok.at[blk(z, c, xr_), pl.ds(half, half)], to_l),
        ][k]
        return send(r, r, xs.at[k], xr.at[k], to, y)

    def tx_got(k):
        half = ROWS // 2
        r = [
            tok.at[blk(z, c, xl_)], tok.at[blk(z, c, xr_)],
            tok.at[blk(z, c, xo_), pl.ds(0, half)], tok.at[blk(z, c, xo_), pl.ds(half, half)],
        ][k]
        send(r, r, xs.at[k], xr.at[k], to_r, y).wait_recv()

    def tz0(k, d):
        r = tok.at[blk(z, c, xoff[k])]
        q = k if d > 0 else NX + k
        return send(r, r, z0s.at[q], z0r.at[q], to_u if d > 0 else to_d, y)

    def tz0_got(k, d):
        r = tok.at[blk(zat(-d), c, xoff[k])]
        q = k if d > 0 else NX + k
        send(r, r, z0s.at[q], z0r.at[q], to_u, y).wait_recv()

    def plane(p, cc, n=NX, off=0):
        return tok.at[pl.ds(p * (NX * NC) + cc * NX + off, n)]

    def tz(t, d):
        p = zat(-d * t)
        r = plane(p, c) if t < 3 else plane(p, c, 2, 0 if d > 0 else 2)
        k = t - 1 if d > 0 else 2 + t
        return send(r, r, zs.at[k], zr.at[k], to_u if d > 0 else to_d, y)

    def tz_got(t, d):
        p = zat(-d * (t + 1))
        r = plane(p, c) if t < 3 else plane(p, c, 2, 0 if d > 0 else 2)
        k = t - 1 if d > 0 else 2 + t
        send(r, r, zs.at[k], zr.at[k], to_u, y).wait_recv()

    def across(d, p, cc):
        r = plane(p, cc)
        return send(r, r, ss.at[d], sr.at[d], sib, y)

    def ag(i, k, copy=True):
        src, dst, to = (
            (xo.at[i, other], xg.at[i, y if copy else yd], yu),
            (xo.at[i, other], xg.at[i, y if copy else yu], yd),
            (xo.at[i, mine, left_], tr.at[i, 0], yu),
            (xo.at[i, mine, right_], tr.at[i, 1], yd),
            (tr.at[i, 0], xg.at[i, yd if copy else yo, :, left_], yu),
            (tr.at[i, 1], xg.at[i, yu if copy else yo, :, right_], yd),
        )[k]
        return send(src, dst, gs.at[k, i], gr.at[k, i], e, to)

    def rs(i, k):
        src, dst, to = (
            (pb.at[i, yu], ra.at[i, 0], yu),
            (pb.at[i, yd], ra.at[i, 1], yd),
            (pb.at[i, yo, :, left_], tq.at[i, 0], yu),
            (pb.at[i, yo, :, right_], tq.at[i, 1], yd),
            (tq.at[i, 0], rb.at[i, :, left_], yu),
            (tq.at[i, 1], rb.at[i, :, right_], yd),
        )[k]
        return send(src, dst, ps.at[k, i], pr.at[k, i], e, to)

    def sh(k, who=None):
        src, dst, to = (
            (xsh.at[y], xsh.at[y if who is None else who], yu),
            (xsh.at[y], xsh.at[y if who is None else who], yd),
            (xsh.at[yd, plo], xsh.at[yd if who is None else who, plo], yu),
            (xsh.at[yu, phi], xsh.at[yu if who is None else who, phi], yd),
            (psh.at[yo, plo], s1.at[0], yu),
            (psh.at[yo, phi], s1.at[1], yd),
            (psh.at[yu], s2.at[0], yu),
            (psh.at[yd], s2.at[1], yd),
        )[k]
        return send(src, dst, vs.at[k], vr.at[k], e, to)

    tx(0).start()
    tx(1).start()
    tz0(0, 1).start()
    tz0(0, -1).start()
    sh(0).start()
    sh(1).start()
    wide = jnp.concatenate([router[...], jnp.zeros((ROWS - NE, FEAT), F32)], axis=0)
    lg[3] = lax.dot_general(
        normed32, wide, (((1,), (1,)), ((), ())),
        precision=lax.Precision.HIGHEST, preferred_element_type=F32,
    )
    for k in range(3):
        spread(lg, 3, k).start()
    tx_got(0)
    tx(2).start()
    tz0(3, 1).start()
    tz0(3, -1).start()
    tx_got(1)
    tx(3).start()
    tz0(1, 1).start()
    tz0(1, -1).start()
    tx_got(2)
    tx_got(3)
    tz0(2, 1).start()
    tz0(2, -1).start()
    across(0, z, c).start()

    def ring(t):
        for d in (1, -1):
            if t == 1:
                for k in (0, 3, 1, 2):
                    tz0_got(k, d)
            else:
                tz_got(t - 1, d)
            if t < 4:
                tz(t, d).start()
                p = zat(-d * t)
                across((-d * t) % NZ, p, c).start()
        if t == 4:
            across(4, far, c).start()

    def offset_of(k):
        return lax.shift_right_logical(jnp.int32(ORDER), 3 * k) & 7

    def plane_of(k):
        return lax.rem(z + offset_of(k), NZ)

    def stage_rows(i):
        p = plane_of(i)
        across(offset_of(i), p, 1 - c).wait_recv()
        rows = lax.broadcasted_iota(jnp.int32, (CHUNK, ROWS), 0).astype(F32)
        total = jnp.zeros((CHUNK, FEAT), F32)
        for b in range(0, NX * NC, 2):
            k = p * (NX * NC) + b
            onehot = jnp.concatenate(
                [
                    (rows == slot[pl.ds(k + h, 1), :] + float(CAP * (b + h))).astype(F32)
                    for h in range(2)
                ],
                axis=1,
            ).astype(BF16)
            pair = tok[pl.ds(k, 2)].reshape(2 * ROWS, FEAT)
            total = total + jnp.dot(onehot, pair, preferred_element_type=F32)
        xo[i] = total.astype(BF16)
        for k in (2, 3, 0, 1):
            ag(i, k).start()
        xg[i, y] = xo[i, mine]

    def stage_relay(i):
        for k in (2, 3):
            ag(i, k, False).wait_recv()
            ag(i, k + 2).start()

    def gated(gate, value):
        return (gate / (1.0 + jnp.exp(-gate)) * value).astype(BF16)

    def stage_experts(i):
        for k in (0, 1, 4, 5):
            ag(i, k, False).wait_recv()
        both = []
        for h in range(2):
            total = jnp.zeros((HALF, QPAD), F32)
            for k in range(NY):
                total = total + nt(xg[i, k], wi[h, :, k * FEAT : (k + 1) * FEAT])
            both.append(total)
        hidden = gated(both[0], both[1])

        def down(k, carry):
            d = lax.rem(yo + k, NY)
            w = wo[:, pl.ds(pl.multiple_of(d * FEAT, FEAT), FEAT)]
            pb[i, d] = jnp.dot(hidden, w, preferred_element_type=F32).astype(BF16)
            return carry

        lax.fori_loop(0, 1, down, 0)
        rs(i, 2).start()
        rs(i, 3).start()
        lax.fori_loop(1, NY, down, 0)
        rs(i, 0).start()
        rs(i, 1).start()

    def stage_shared():
        sh(2, yo).wait_recv()
        sh(3, yo).wait_recv()
        for k in range(NX):
            wsib(k, 1 - c).wait_recv()
        acc[...] = jnp.zeros((ROWS, 2 * SPAD), F32)

        def into(zz, carry):
            w = jnp.concatenate(
                [
                    wb[wblk(zz, cc, xx), :, pl.ds(0, 2 * SPAD)]
                    for xx in range(NX)
                    for cc in range(NC)
                ],
                axis=0,
            )
            off = pl.multiple_of(lax.rem(zz, 2) * 256, 256)
            acc[...] += jnp.dot(
                xsh[lax.div(zz, 2), :, pl.ds(off, 256)],
                w,
                preferred_element_type=F32,
            )
            return carry

        lax.fori_loop(0, NZ, into, 0)
        hidden = gated(acc[:, :SPAD], acc[:, SPAD:])

        def project(k, carry):
            d = lax.rem(yo + k, NY)
            w = jnp.concatenate(
                [
                    wb[wblk(2 * d + zz, cc, xx), :, pl.ds(2 * SPAD, SPAD)]
                    for zz in range(2)
                    for xx in range(NX)
                    for cc in range(NC)
                ],
                axis=0,
            )
            psh[d] = nt(hidden, w).astype(BF16)
            return carry

        lax.fori_loop(0, NY, project, 0)
        sh(4).start()
        sh(5).start()

    def stage_reduce(i):
        for k in (2, 3):
            rs(i, k).wait_recv()
            rs(i, k + 2).start()

    def shared_relay():
        sh(0, yd).wait_recv()
        sh(2).start()
        sh(1, yu).wait_recv()
        sh(3).start()

    def shared_reduce():
        sh(4).wait_recv()
        psh[yu, plo] = (psh[yu, plo].astype(F32) + s1[0].astype(F32)).astype(BF16)
        sh(6).start()
        sh(5).wait_recv()
        psh[yd, phi] = (psh[yd, phi].astype(F32) + s1[1].astype(F32)).astype(BF16)
        sh(7).start()

    def shared_total():
        sh(6).wait_recv()
        sh(7).wait_recv()
        shared[...] = psh[y].astype(F32) + s2[0].astype(F32) + s2[1].astype(F32)

    def back(i, b):
        to = eid(plane_of(i), lax.rem(b, NX), lax.div(b, NX))
        return to, send(sbuf.at[i, b], rbuf.at[e], os_.at[i * (NX * NC) + b], or_.at[e], to, y)

    def stage_return(i):
        for k in (0, 1, 4, 5):
            rs(i, k).wait_recv()
        tot[mine] = pb[i, y].astype(F32) + rb[i].astype(F32)
        tot[other] = ra[i, 0].astype(F32) + ra[i, 1].astype(F32)
        total = tot[...].astype(BF16)
        to_row = lax.broadcasted_iota(jnp.int32, (ROWS, CHUNK), 0)
        of_row = lax.broadcasted_iota(jnp.int32, (ROWS, CHUNK), 1)
        base = CAP * lax.shift_right_logical(to_row, 4)
        inner = to_row & (PACK - 1)

        def move(hit, values):
            return jnp.dot(hit.astype(F32).astype(BF16), values, preferred_element_type=F32)

        first = move(of_row == base + inner, total)
        sbuf[i, :, :, pl.ds(0, FEAT)] = first.astype(BF16).reshape(NX * NC, PACK, FEAT)
        last = jnp.zeros((ROWS, ROWS), F32)
        for q in range(4):
            hit = (of_row == base + PACK + inner - 4 * q) & (inner >= 4 * q) & (inner < 4 * q + 4)
            last = last + move(hit, total[:, q * 128 : (q + 1) * 128])
        sbuf[i, :, :, pl.ds(FEAT, 128)] = last.astype(BF16).reshape(NX * NC, PACK, 128)

        def go(b, carry):
            to, copy = back(i, b)

            @pl.when(to != e)
            def _():
                copy.start()

            @pl.when(to == e)
            def _():
                rbuf[e] = sbuf[i, b]

            return carry

        lax.fori_loop(0, NX * NC, go, 0)

    def stage_tables():
        for k in range(3):
            spread(lg, 3, k).wait_recv()
        logits = (lg[0] + lg[1]) + (lg[2] + lg[3])
        mine = jnp.transpose(names)
        lane = c_i.astype(F32)
        count = jnp.zeros((ROWS, ROWS), F32)
        for k in range(TOP):
            count = count + (mine[:, k : k + 1] == lane).astype(F32)
        chosen = count > 0.5
        top = jnp.max(jnp.where(chosen, logits, -jnp.inf), axis=1, keepdims=True)
        weight = jnp.where(chosen, jnp.exp(jnp.where(chosen, logits - top, 0.0)), 0.0)
        gates = weight / jnp.sum(weight, axis=1, keepdims=True)
        place = jnp.dot(
            (c_i < r_i).astype(F32).astype(BF16), count.astype(BF16), preferred_element_type=F32
        )
        place = jnp.where(chosen, place, 255.0).astype(BF16)
        high = gates.astype(BF16)
        low = (gates - high.astype(F32)).astype(BF16)

        def fill(b, carry):
            ee = lax.broadcasted_iota(jnp.int32, (ROWS, 256), 0)
            jj = lax.broadcasted_iota(jnp.int32, (ROWS, 256), 1)
            inner = jj & (PACK - 1)
            mat = (ee == lax.shift_right_logical(jj, 4) + b * PACK).astype(F32).astype(BF16)
            where = jnp.dot(place, mat, preferred_element_type=F32)
            at = pl.ds(pl.multiple_of(b * 256, 256), 256)
            for h, g in enumerate((high, low)):
                spaced = jnp.dot(g, mat, preferred_element_type=F32)
                for q, want in enumerate((inner, PACK + (inner & 3))):
                    hit = jnp.where(where == want.astype(F32), spaced, 0.0)
                    tab[q, pl.ds(h * ROWS, ROWS), at] = hit.astype(BF16)
            return carry

        lax.fori_loop(0, NE * PACK // 256, fill, 0)

    def step(j, carry):
        @pl.when((j >= 1) & (j < NZ + 1))
        def _():
            stage_relay(j - 1)

        @pl.when(j < NZ)
        def _():
            stage_rows(j)

        @pl.when(j == 0)
        def _():
            wz_step(3)

        @pl.when(j == 1)
        def _():
            for d in (1, -1):
                wz_got(3, d)
            wx(0).start()
            wx(1).start()
            wsib(0, c).start()

        @pl.when(j == 5)
        def _():
            wx_got(0)
            wx(2).start()
            wx_got(1)
            wx(3).start()
            wsib(3, c).start()
            wsib(1, c).start()

        @pl.when(j == 7)
        def _():
            wx_got(2)
            wx_got(3)
            wsib(2, c).start()

        @pl.when(j == 2)
        def _():
            for load in loads:
                load.wait()
            for k in range(8):
                pair(k).wait_recv()
            shared_relay()

        @pl.when((j >= 2) & (j < NZ + 2))
        def _():
            stage_experts(j - 2)

        @pl.when((j >= 3) & (j < NZ + 3))
        def _():
            stage_reduce(j - 3)

        @pl.when(j >= 4)
        def _():
            stage_return(j - 4)

        @pl.when(j == 5)
        def _():
            stage_tables()

        @pl.when(j == SHARED_AT)
        def _():
            stage_shared()

        @pl.when(j == SHARED_AT + 1)
        def _():
            shared_reduce()

        @pl.when(j == SHARED_AT + 2)
        def _():
            shared_total()

        for t, at in ((1, 0), (2, 1), (3, 2), (4, 3)):

            @pl.when(j == at)
            def _(t=t):
                ring(t)

        return carry

    lax.fori_loop(0, NZ + 4, step, 0)

    def arrive(k, carry):
        s = lax.rem(e + k, NE)
        send(rbuf.at[s], rbuf.at[s], os_.at[0], or_.at[s], sib, y).wait_recv()
        return carry

    lax.fori_loop(1, NE, arrive, 0)
    back_rows = rbuf[:, :, pl.ds(0, FEAT)].reshape(NE * PACK, FEAT)
    pieces = rbuf[:, :, pl.ds(FEAT, 128)].reshape(NE * PACK, 128).astype(F32)
    part_of = lax.shift_right_logical(
        lax.broadcasted_iota(jnp.int32, (NE * PACK, 128), 0) & (PACK - 1), 2
    )
    extra = jnp.concatenate(
        [jnp.where(part_of == q, pieces, 0.0).astype(BF16) for q in range(4)], axis=1
    )
    both = jnp.dot(tab[0], back_rows, preferred_element_type=F32) + jnp.dot(
        tab[1], extra, preferred_element_type=F32
    )
    base_o[...] = mixed[...] + shared[...]
    out[...] = both[:ROWS] + both[ROWS:]

    for k in range(3):
        ax(k).wait_send()
        spread(sq, 0, k).wait_send()
        spread(lg, 3, k).wait_send()
    for t in range(4):
        for d in (1, -1):
            az(t, d).wait_send()
            if t < 3 or d > 0:
                bz(t, d).wait_send()
            wz(t, d).wait_send()
            tz0(t, d).wait_send()
            if t > 0:
                tz(t, d).wait_send()
        bx(t).wait_send()
        b_sib(t, c).wait_send()
        wx(t).wait_send()
        wsib(t, c).wait_send()
        tx(t).wait_send()
    for d in (0, -1, 1, -2, 2, -3, 3, 4):
        a_sib(d, c).wait_send()
    for k in range(2):
        pa(k).wait_send()
        pb2(k).wait_send()

    def drain(i, carry):
        across(i, lax.rem(z + i, NZ), c).wait_send()

        def sent(b, inner):
            to, copy = back(i, b)

            @pl.when(to != e)
            def _():
                copy.wait_send()

            return inner

        lax.fori_loop(0, NX * NC, sent, 0)
        for k in range(6):
            ag(i, k).wait_send()
            rs(i, k).wait_send()
        return carry

    lax.fori_loop(0, NZ, drain, 0)
    for k in range(8):
        pair(k).wait_send()
        sh(k).wait_send()


def mixer(ctx, opt, ids, hid, gain, router, win_s, wout_s, win, wout):
    vm = pl.BlockSpec(memory_space=pltpu.VMEM)
    hbm = pl.BlockSpec(memory_space=pl.ANY)

    def pairs(*shapes):
        return [pltpu.SemaphoreType.DMA(s) for s in shapes for _ in range(2)]

    return pl.pallas_call(
        mixer_kernel,
        name="mixer_tail",
        out_shape=[jax.ShapeDtypeStruct((ROWS, FEAT), F32)] * 2,
        in_specs=[vm] * 8 + [hbm] * 2,
        out_specs=[vm] * 2,
        scratch_shapes=[
            pltpu.VMEM((NE, 16, FEAT + ROWS), BF16),
            pltpu.VMEM((NE, 16, FEAT), BF16),
            pltpu.VMEM((NY, ROWS, FEAT), F32),
            pltpu.VMEM((2, ROWS // 2, FEAT), F32),
            pltpu.VMEM((2, ROWS, FEAT), F32),
            pltpu.VMEM((4, 8, ROWS), F32),
            pltpu.VMEM((4, ROWS, ROWS), F32),
            pltpu.VMEM((ROWS, FEAT), F32),
            pltpu.VMEM((ROWS, FEAT), F32),
            pltpu.VMEM((2, 2 * ROWS, NE * PACK), BF16),
            pltpu.VMEM((NE, ROWS, FEAT), BF16),
            pltpu.VMEM((NE, ROWS), F32),
            pltpu.VMEM((NZ, CHUNK, FEAT), BF16),
            pltpu.VMEM((NZ, NY, HALF, FEAT), BF16),
            pltpu.VMEM((NZ, 2, HALF, 256), BF16),
            pltpu.VMEM((NZ, NY, HALF, FEAT), BF16),
            pltpu.VMEM((NZ, 2, HALF, FEAT), BF16),
            pltpu.VMEM((NZ, HALF, FEAT), BF16),
            pltpu.VMEM((NZ, 2, HALF, 256), BF16),
            pltpu.VMEM((NY, ROWS, FEAT), BF16),
            pltpu.VMEM((NY, ROWS, FEAT), BF16),
            pltpu.VMEM((2, ROWS // 2, FEAT), BF16),
            pltpu.VMEM((2, ROWS, FEAT), BF16),
            pltpu.VMEM((NE, 32, 3 * SPAD), BF16),
            pltpu.VMEM((2, QPAD, WIDTH), BF16),
            pltpu.VMEM((QPAD, WIDTH), BF16),
            pltpu.VMEM((NZ, NX * NC, PACK, PWIDTH), BF16),
            pltpu.VMEM((NE, PACK, PWIDTH), BF16),
            pltpu.VMEM((ROWS, 2 * SPAD), F32),
            pltpu.VMEM((CHUNK, FEAT), F32),
            pltpu.SemaphoreType.DMA((3,)),
        ]
        + pairs((3,), (8,), (8,), (8,), (4,), (4,), (4,), (6,))
        + pairs((4,), (8,), (6,), (8,), (8,), (4,), (4,))
        + pairs((8,), (6, NZ), (6, NZ), (8,), (NE,)),
        compiler_params=pltpu.CompilerParams(
            collective_id=0, has_side_effects=True, vmem_limit_bytes=VMEM_LIMIT
        ),
    )(ctx, opt, ids, hid, gain, router, win_s, wout_s, win, wout)


def per_device(
    hidden_state, context, out_proj, norm_gain, router_weight,
    expert_in, expert_out, shared_in, shared_out, route_ids,
):
    win = jnp.transpose(expert_in[0], (1, 2, 0))
    routed, base = mixer(
        context, out_proj.T, route_ids.T, hidden_state, norm_gain.reshape(4, 128),
        router_weight.T, shared_in, shared_out.T, win, expert_out[0],
    )
    return base + routed


def solution(mesh):
    return jax.shard_map(
        per_device,
        mesh=mesh,
        in_specs=(
            P("expert", "mp"),
            P("expert", "mp"),
            P("mp", "expert"),
            P("mp"),
            P("mp", None),
            P("expert", None, None, "mp"),
            P("expert", "mp", None),
            P("expert", None, "mp"),
            P("mp", "expert"),
            P("expert", None),
        ),
        out_specs=P("expert", "mp"),
        check_vma=False,
    )
```

```python
import jax
import jax.numpy as jnp
from jax import lax
from jax.experimental import pallas as pl
from jax.experimental.pallas import tpu as pltpu
from jax.sharding import PartitionSpec as P

NZ, NX, NC, NY = 8, 4, 2, 4
NE = NZ * NX * NC
ROWS, FEAT, WIDTH = 128, 512, 2048
TOP, CAP, PACK, PWIDTH = 6, 20, 16, 640
QUARTER, QPAD = 352, 768
EIGHTH = QUARTER // 2
SWIDTH, SPAD = 704, 768
CHUNK = NX * NC * CAP
HALF = CHUNK // 2
SHARED_AT = 8
ORDER = sum(d << (3 * k) for k, d in enumerate((0, 7, 2, 6, 3, 4, 5, 1)))
F32, BF16 = jnp.float32, jnp.bfloat16
VMEM_LIMIT = 64 * 1024 * 1024 - 65536


def coords():
    e = lax.axis_index("expert")
    y = lax.axis_index("mp")
    z = lax.div(e, NX * NC)
    x = lax.rem(lax.div(e, NC), NX)
    c = lax.rem(e, NC)
    return e, z, x, c, y


def eid(z, x, c):
    return z * (NX * NC) + x * NC + c


def blk(z, c, x):
    return z * (NX * NC) + c * NX + x


def send(src, dst, ssem, rsem, e, y):
    return pltpu.make_async_remote_copy(
        src_ref=src,
        dst_ref=dst,
        send_sem=ssem,
        recv_sem=rsem,
        device_id={"expert": e, "mp": y},
        device_id_type=pl.DeviceIdType.MESH,
    )


def greet(e, y):
    pl.semaphore_signal(
        pltpu.get_barrier_semaphore(),
        inc=1,
        device_id={"expert": e, "mp": y},
        device_id_type=pl.DeviceIdType.MESH,
    )


def nt(a, b):
    return lax.dot_general(a, b, (((1,), (1,)), ((), ())), preferred_element_type=F32)


def mixer_kernel(
    ctx, opt, ids, hid, gain, router, win_s, wout_s, win, wout,
    out, base_o,
    wga, wgb, part, p1, p2, sq, lg, mixed, shared, tab,
    tok, slot, xo, xg, tr, pb, ra, rb, tq, xsh, psh, s1, s2,
    wb, wi, wo, sbuf, rbuf, acc, tot,
    wsem,
    axs, axr, azs, azr, ass, asr, bzs, bzr, bxs, bxr, bss, bsr,
    ys, yr, qs, qr,
    xs, xr, z0s, z0r, zs, zr, ss, sr,
    wzs, wzr, wxs, wxr, wss, wsr,
    hs, hr, gs, gr, ps, pr, vs, vr, os_, or_,
):
    e, z, x, c, y = coords()
    xr_, xl_, xo_ = lax.rem(x + 1, NX), lax.rem(x + NX - 1, NX), lax.rem(x + 2, NX)
    to_r, to_l = eid(z, xr_, c), eid(z, xl_, c)
    to_u, to_d = eid(lax.rem(z + 1, NZ), x, c), eid(lax.rem(z + NZ - 1, NZ), x, c)
    sib = eid(z, x, 1 - c)
    yu, yd, yo = lax.rem(y + 1, NY), lax.rem(y + NY - 1, NY), lax.rem(y + 2, NY)
    left_, right_ = pl.ds(0, 256), pl.ds(256, 256)
    par = lax.rem(y, 2)
    mine = pl.ds(pl.multiple_of(par * HALF, 16), HALF)
    other = pl.ds(pl.multiple_of((1 - par) * HALF, 16), HALF)
    near = y + 1 - 2 * par
    next_ = lax.rem(y + 3 + 2 * par, NY)
    far = lax.rem(z + 4, NZ)

    def zat(d):
        return lax.rem(z + NZ + d, NZ)

    def hello(k, carry):
        greet(lax.rem(e + k, NE), y)
        return carry

    lax.fori_loop(1, NE, hello, 0)
    for t in (yu, yd, yo):
        greet(e, t)

    loads = [
        pltpu.make_async_copy(win.at[0], wi.at[0, pl.ds(0, QUARTER)], wsem.at[0]),
        pltpu.make_async_copy(win.at[1], wi.at[1, pl.ds(0, QUARTER)], wsem.at[1]),
        pltpu.make_async_copy(wout, wo.at[pl.ds(0, QUARTER)], wsem.at[2]),
    ]
    for load in loads:
        load.start()

    def wblk(zz, cc, xx):
        return cc * (NX * NZ) + xx * NZ + zz

    own, wown = blk(z, c, x), wblk(z, c, x)
    names = jnp.concatenate(
        [ids[...].astype(F32), jnp.full((ROWS - TOP, ROWS), -1.0, F32)], axis=0
    )
    wga[own, :, pl.ds(0, FEAT)] = opt[0:16, :]
    wga[own, :, pl.ds(FEAT, ROWS)] = names[:16].astype(BF16)
    wgb[wown] = opt[16:32, :]
    none = jnp.zeros((32, SPAD - SWIDTH), BF16)
    for h in range(3):
        piece = win_s[:, h, :] if h < 2 else wout_s[...]
        wb[wown, :, pl.ds(h * SPAD, SPAD)] = jnp.concatenate([piece, none], axis=1)
    pl.semaphore_wait(pltpu.get_barrier_semaphore(), NE + 2)

    def pair(k):
        src, dst, at, to, n, where = (
            (win.at[0], wi.at[0], 0, near, EIGHTH, QUARTER),
            (win.at[0], wi.at[0], EIGHTH, next_, EIGHTH, QUARTER + EIGHTH),
            (win.at[1], wi.at[1], 0, near, 80, QUARTER),
            (win.at[1], wi.at[1], EIGHTH, next_, 80, QUARTER + EIGHTH),
            (win.at[1], wi.at[1], 80, near, EIGHTH - 80, QUARTER + 80),
            (win.at[1], wi.at[1], EIGHTH + 80, next_, EIGHTH - 80, QUARTER + EIGHTH + 80),
            (wout, wo, 0, near, EIGHTH, QUARTER),
            (wout, wo, EIGHTH, next_, EIGHTH, QUARTER + EIGHTH),
        )[k]
        return send(src.at[pl.ds(at, n)], dst.at[pl.ds(where, n)], hs.at[k], hr.at[k], e, to)

    def ax(k):
        b, to = [(own, to_r), (own, to_l), (blk(z, c, xl_), to_r)][k]
        return send(wga.at[b], wga.at[b], axs.at[k], axr.at[k], to, y)

    def ax_got(k):
        b = blk(z, c, [xl_, xr_, xo_][k])
        send(wga.at[b], wga.at[b], axs.at[k], axr.at[k], to_r, y).wait_recv()

    def a_plane(p, cc, n=NX, off=0):
        return wga.at[pl.ds(p * (NX * NC) + cc * NX + off, n)]

    def az(t, d):
        p = zat(-d * t)
        r = a_plane(p, c) if t < 3 else a_plane(p, c, 2, 0 if d > 0 else 2)
        k = t if d > 0 else 4 + t
        return send(r, r, azs.at[k], azr.at[k], to_u if d > 0 else to_d, y)

    def az_got(t, d):
        p = zat(-d * (t + 1))
        r = a_plane(p, c) if t < 3 else a_plane(p, c, 2, 0 if d > 0 else 2)
        k = t if d > 0 else 4 + t
        send(r, r, azs.at[k], azr.at[k], to_u, y).wait_recv()

    def a_sib(d, cc):
        r = a_plane(zat(d), cc)
        return send(r, r, ass.at[d % NZ], asr.at[d % NZ], sib, y)

    def bz(t, d):
        r = wgb.at[wblk(zat(-d * t), c, x)]
        k = t if d > 0 else 4 + t
        return send(r, r, bzs.at[k], bzr.at[k], to_u if d > 0 else to_d, y)

    def bz_got(t, d):
        r = wgb.at[wblk(zat(-d * (t + 1)), c, x)]
        k = t if d > 0 else 4 + t
        send(r, r, bzs.at[k], bzr.at[k], to_u, y).wait_recv()

    def b_col(xx, cc, n=NZ, off=0):
        return wgb.at[pl.ds(cc * (NX * NZ) + xx * NZ + off, n)]

    def bx(k):
        r, to = [
            (b_col(x, c), to_r), (b_col(x, c), to_l),
            (b_col(xl_, c, 4, 0), to_r), (b_col(xr_, c, 4, 4), to_l),
        ][k]
        return send(r, r, bxs.at[k], bxr.at[k], to, y)

    def bx_got(k):
        r = [b_col(xl_, c), b_col(xr_, c), b_col(xo_, c, 4, 0), b_col(xo_, c, 4, 4)][k]
        send(r, r, bxs.at[k], bxr.at[k], to_r, y).wait_recv()

    xoff = (x, xr_, xo_, xl_)

    def b_sib(k, cc):
        r = b_col(xoff[k], cc)
        return send(r, r, bss.at[k], bsr.at[k], sib, y)

    for k in range(4):
        pair(k).start()
    ax(0).start()
    ax(1).start()
    bz(0, 1).start()
    bz(0, -1).start()
    ax_got(0)
    ax(2).start()
    ax_got(1)
    bz_got(0, 1)
    bz(1, 1).start()
    bz_got(0, -1)
    bz(1, -1).start()
    ax_got(2)
    az(0, 1).start()
    az(0, -1).start()
    a_sib(0, c).start()
    bz_got(1, 1)
    bz(2, 1).start()
    bz_got(1, -1)
    bz(2, -1).start()
    az_got(0, 1)
    az(1, 1).start()
    az_got(0, -1)
    az(1, -1).start()
    a_sib(-1, c).start()
    a_sib(1, c).start()
    bz_got(2, 1)
    bz(3, 1).start()
    bz_got(2, -1)
    az_got(1, 1)
    az(2, 1).start()
    az_got(1, -1)
    az(2, -1).start()
    bz_got(3, 1)
    bx(0).start()
    bx(1).start()
    a_sib(-2, c).start()
    a_sib(2, c).start()
    b_sib(0, c).start()
    az_got(2, 1)
    az(3, 1).start()
    az_got(2, -1)
    az(3, -1).start()
    a_sib(-3, c).start()
    a_sib(3, c).start()
    bx_got(0)
    bx(2).start()
    bx_got(1)
    bx(3).start()
    b_sib(3, c).start()
    b_sib(1, c).start()
    az_got(3, 1)
    az_got(3, -1)
    a_sib(4, c).start()
    bx_got(2)
    bx_got(3)
    b_sib(2, c).start()

    def wz(t, d):
        r = wb.at[wblk(zat(-d * t), c, x)]
        if t == 3:
            r = wb.at[wblk(zat(-d * t), c, x), pl.ds(0 if d > 0 else 16, 16)]
        k = t if d > 0 else 4 + t
        return send(r, r, wzs.at[k], wzr.at[k], to_u if d > 0 else to_d, y)

    def wz_got(t, d):
        r = wb.at[wblk(zat(-d * (t + 1)), c, x)]
        if t == 3:
            r = wb.at[wblk(zat(-d * (t + 1)), c, x), pl.ds(0 if d > 0 else 16, 16)]
        k = t if d > 0 else 4 + t
        send(r, r, wzs.at[k], wzr.at[k], to_u, y).wait_recv()

    def wz_step(t):
        for d in (1, -1):
            wz_got(t - 1, d)
            wz(t, d).start()

    def col(xx, cc, n=NZ, off=0):
        return wb.at[pl.ds(cc * (NX * NZ) + xx * NZ + off, n)]

    def wx(k):
        r, to = [
            (col(x, c), to_r), (col(x, c), to_l),
            (col(xl_, c, 4, 0), to_r), (col(xr_, c, 4, 4), to_l),
        ][k]
        return send(r, r, wxs.at[k], wxr.at[k], to, y)

    def wx_got(k):
        r = [col(xl_, c), col(xr_, c), col(xo_, c, 4, 0), col(xo_, c, 4, 4)][k]
        send(r, r, wxs.at[k], wxr.at[k], to_r, y).wait_recv()

    def wsib(k, cc):
        r = col(xoff[k], cc)
        return send(r, r, wss.at[k], wsr.at[k], sib, y)

    wz(0, 1).start()
    wz(0, -1).start()
    for d in (0, -1, 1, -2, 2, -3, 3, 4):
        a_sib(d, 1 - c).wait_recv()
    for k in range(NX):
        b_sib(k, 1 - c).wait_recv()

    def columns(d):
        blocks = []
        for zz in range(2):
            for xx in range(NX):
                for cc in range(NC):
                    p = 2 * d + zz
                    blocks.append(wga[blk(p, cc, xx), :, pl.ds(0, FEAT)])
                    blocks.append(wgb[wblk(p, cc, xx)])
        return nt(ctx[...], jnp.concatenate(blocks, axis=0))

    hrows = ROWS // 2
    plo, phi = pl.ds(0, hrows), pl.ds(hrows, hrows)

    def pa(k):
        rows, to = [(plo, yu), (phi, yd)][k]
        return send(part.at[yo, rows], p1.at[k], ys.at[k], yr.at[k], e, to)

    def pb2(k):
        to = [yu, yd][k]
        return send(part.at[to], p2.at[k], ys.at[2 + k], yr.at[2 + k], e, to)

    part[yo] = columns(yo)
    pa(0).start()
    pa(1).start()
    part[yu] = columns(yu)
    part[yd] = columns(yd)
    pa(0).wait_recv()
    part[yu, plo] = part[yu, plo] + p1[0]
    pb2(0).start()
    pa(1).wait_recv()
    part[yd, phi] = part[yd, phi] + p1[1]
    pb2(1).start()
    pair(4).start()
    pair(5).start()
    part[y] = columns(y)
    wz_step(1)

    def mark(b, carry):
        same = (wga[b, :, pl.ds(FEAT, ROWS)].astype(F32) == e.astype(F32)).astype(F32)
        slot[pl.ds(b, 1), :] = jnp.sum(same, axis=0, keepdims=True)
        return carry

    lax.fori_loop(0, NE, mark, 0)
    r_i = lax.broadcasted_iota(jnp.int32, (ROWS, ROWS), 0)
    c_i = lax.broadcasted_iota(jnp.int32, (ROWS, ROWS), 1)
    named = slot[...]
    rank = jnp.dot(
        named.astype(BF16), (r_i < c_i).astype(F32).astype(BF16), preferred_element_type=F32
    )
    slot[...] = jnp.where(named > 0.5, rank, -1000.0)
    gap = pl.ds(2 * QUARTER, QPAD - 2 * QUARTER)
    wi[0, gap] = jnp.zeros((QPAD - 2 * QUARTER, WIDTH), BF16)
    wi[1, gap] = jnp.zeros((QPAD - 2 * QUARTER, WIDTH), BF16)
    wo[gap] = jnp.zeros((QPAD - 2 * QUARTER, WIDTH), BF16)

    pb2(0).wait_recv()
    pb2(1).wait_recv()
    mix = hid[...].astype(F32) + (part[y] + p2[0] + p2[1])
    mixed[...] = mix

    def spread(buf, base, k):
        return send(
            buf.at[3], buf.at[k], qs.at[base + k], qr.at[base + k], e, (yu, yd, yo)[k]
        )

    sums = jnp.broadcast_to(jnp.sum(mix * mix, axis=1, keepdims=True), (ROWS, ROWS))
    sq[3] = jnp.transpose(sums)[:8]
    for k in range(3):
        spread(sq, 0, k).start()
    for k in range(6, 8):
        pair(k).start()
    wz_step(2)
    for k in range(3):
        spread(sq, 0, k).wait_recv()
    inverse = lax.rsqrt(((sq[0] + sq[1]) + (sq[2] + sq[3])) / WIDTH + 1e-06)
    inverse = jnp.transpose(jnp.broadcast_to(inverse[:1], (ROWS, ROWS)))[:, :1]
    gains = jnp.concatenate([gain[k : k + 1] for k in range(4)], axis=1)
    normed32 = mix * inverse * gains.astype(F32)
    tok[own] = normed32.astype(BF16)
    xsh[y] = normed32.astype(BF16)

    def tx(k):
        half = ROWS // 2
        r, to = [
            (tok.at[own], to_r), (tok.at[own], to_l),
            (tok.at[blk(z, c, xl_), pl.ds(0, half)], to_r),
            (tok.at[blk(z, c, xr_), pl.ds(half, half)], to_l),
        ][k]
        return send(r, r, xs.at[k], xr.at[k], to, y)

    def tx_got(k):
        half = ROWS // 2
        r = [
            tok.at[blk(z, c, xl_)], tok.at[blk(z, c, xr_)],
            tok.at[blk(z, c, xo_), pl.ds(0, half)], tok.at[blk(z, c, xo_), pl.ds(half, half)],
        ][k]
        send(r, r, xs.at[k], xr.at[k], to_r, y).wait_recv()

    def tz0(k, d):
        r = tok.at[blk(z, c, xoff[k])]
        q = k if d > 0 else NX + k
        return send(r, r, z0s.at[q], z0r.at[q], to_u if d > 0 else to_d, y)

    def tz0_got(k, d):
        r = tok.at[blk(zat(-d), c, xoff[k])]
        q = k if d > 0 else NX + k
        send(r, r, z0s.at[q], z0r.at[q], to_u, y).wait_recv()

    def plane(p, cc, n=NX, off=0):
        return tok.at[pl.ds(p * (NX * NC) + cc * NX + off, n)]

    def tz(t, d):
        p = zat(-d * t)
        r = plane(p, c) if t < 3 else plane(p, c, 2, 0 if d > 0 else 2)
        k = t - 1 if d > 0 else 2 + t
        return send(r, r, zs.at[k], zr.at[k], to_u if d > 0 else to_d, y)

    def tz_got(t, d):
        p = zat(-d * (t + 1))
        r = plane(p, c) if t < 3 else plane(p, c, 2, 0 if d > 0 else 2)
        k = t - 1 if d > 0 else 2 + t
        send(r, r, zs.at[k], zr.at[k], to_u, y).wait_recv()

    def across(d, p, cc):
        r = plane(p, cc)
        return send(r, r, ss.at[d], sr.at[d], sib, y)

    def ag(i, k, copy=True):
        src, dst, to = (
            (xo.at[i, other], xg.at[i, y if copy else yd], yu),
            (xo.at[i, other], xg.at[i, y if copy else yu], yd),
            (xo.at[i, mine, left_], tr.at[i, 0], yu),
            (xo.at[i, mine, right_], tr.at[i, 1], yd),
            (tr.at[i, 0], xg.at[i, yd if copy else yo, :, left_], yu),
            (tr.at[i, 1], xg.at[i, yu if copy else yo, :, right_], yd),
        )[k]
        return send(src, dst, gs.at[k, i], gr.at[k, i], e, to)

    def rs(i, k):
        src, dst, to = (
            (pb.at[i, yu], ra.at[i, 0], yu),
            (pb.at[i, yd], ra.at[i, 1], yd),
            (pb.at[i, yo, :, left_], tq.at[i, 0], yu),
            (pb.at[i, yo, :, right_], tq.at[i, 1], yd),
            (tq.at[i, 0], rb.at[i, :, left_], yu),
            (tq.at[i, 1], rb.at[i, :, right_], yd),
        )[k]
        return send(src, dst, ps.at[k, i], pr.at[k, i], e, to)

    def sh(k, who=None):
        src, dst, to = (
            (xsh.at[y], xsh.at[y if who is None else who], yu),
            (xsh.at[y], xsh.at[y if who is None else who], yd),
            (xsh.at[yd, plo], xsh.at[yd if who is None else who, plo], yu),
            (xsh.at[yu, phi], xsh.at[yu if who is None else who, phi], yd),
            (psh.at[yo, plo], s1.at[0], yu),
            (psh.at[yo, phi], s1.at[1], yd),
            (psh.at[yu], s2.at[0], yu),
            (psh.at[yd], s2.at[1], yd),
        )[k]
        return send(src, dst, vs.at[k], vr.at[k], e, to)

    tx(0).start()
    tx(1).start()
    tz0(0, 1).start()
    tz0(0, -1).start()
    sh(0).start()
    sh(1).start()
    wide = jnp.concatenate([router[...], jnp.zeros((ROWS - NE, FEAT), F32)], axis=0)
    lg[3] = lax.dot_general(
        normed32, wide, (((1,), (1,)), ((), ())),
        precision=lax.Precision.HIGHEST, preferred_element_type=F32,
    )
    for k in range(3):
        spread(lg, 3, k).start()
    tx_got(0)
    tx(2).start()
    tz0(3, 1).start()
    tz0(3, -1).start()
    tx_got(1)
    tx(3).start()
    tz0(1, 1).start()
    tz0(1, -1).start()
    tx_got(2)
    tx_got(3)
    tz0(2, 1).start()
    tz0(2, -1).start()
    across(0, z, c).start()

    def ring(t):
        for d in (1, -1):
            if t == 1:
                for k in (0, 3, 1, 2):
                    tz0_got(k, d)
            else:
                tz_got(t - 1, d)
            if t < 4:
                tz(t, d).start()
                p = zat(-d * t)
                across((-d * t) % NZ, p, c).start()
        if t == 4:
            across(4, far, c).start()

    def offset_of(k):
        return lax.shift_right_logical(jnp.int32(ORDER), 3 * k) & 7

    def plane_of(k):
        return lax.rem(z + offset_of(k), NZ)

    def stage_rows(i):
        p = plane_of(i)
        across(offset_of(i), p, 1 - c).wait_recv()
        rows = lax.broadcasted_iota(jnp.int32, (CHUNK, ROWS), 0).astype(F32)
        total = jnp.zeros((CHUNK, FEAT), F32)
        for b in range(0, NX * NC, 2):
            k = p * (NX * NC) + b
            onehot = jnp.concatenate(
                [
                    (rows == slot[pl.ds(k + h, 1), :] + float(CAP * (b + h))).astype(F32)
                    for h in range(2)
                ],
                axis=1,
            ).astype(BF16)
            pair = tok[pl.ds(k, 2)].reshape(2 * ROWS, FEAT)
            total = total + jnp.dot(onehot, pair, preferred_element_type=F32)
        xo[i] = total.astype(BF16)
        for k in (2, 3, 0, 1):
            ag(i, k).start()
        xg[i, y] = xo[i, mine]

    def stage_relay(i):
        for k in (2, 3):
            ag(i, k, False).wait_recv()
            ag(i, k + 2).start()

    def gated(gate, value):
        return (gate / (1.0 + jnp.exp(-gate)) * value).astype(BF16)

    def stage_experts(i):
        for k in (0, 1, 4, 5):
            ag(i, k, False).wait_recv()
        both = []
        for h in range(2):
            total = jnp.zeros((HALF, QPAD), F32)
            for k in range(NY):
                total = total + nt(xg[i, k], wi[h, :, k * FEAT : (k + 1) * FEAT])
            both.append(total)
        hidden = gated(both[0], both[1])

        def down(k, carry):
            d = lax.rem(yo + k, NY)
            w = wo[:, pl.ds(pl.multiple_of(d * FEAT, FEAT), FEAT)]
            pb[i, d] = jnp.dot(hidden, w, preferred_element_type=F32).astype(BF16)
            return carry

        lax.fori_loop(0, 1, down, 0)
        rs(i, 2).start()
        rs(i, 3).start()
        lax.fori_loop(1, NY, down, 0)
        rs(i, 0).start()
        rs(i, 1).start()

    def stage_shared():
        sh(2, yo).wait_recv()
        sh(3, yo).wait_recv()
        for k in range(NX):
            wsib(k, 1 - c).wait_recv()
        acc[...] = jnp.zeros((ROWS, 2 * SPAD), F32)

        def into(zz, carry):
            w = jnp.concatenate(
                [
                    wb[wblk(zz, cc, xx), :, pl.ds(0, 2 * SPAD)]
                    for xx in range(NX)
                    for cc in range(NC)
                ],
                axis=0,
            )
            off = pl.multiple_of(lax.rem(zz, 2) * 256, 256)
            acc[...] += jnp.dot(
                xsh[lax.div(zz, 2), :, pl.ds(off, 256)],
                w,
                preferred_element_type=F32,
            )
            return carry

        lax.fori_loop(0, NZ, into, 0)
        hidden = gated(acc[:, :SPAD], acc[:, SPAD:])

        def project(k, carry):
            d = lax.rem(yo + k, NY)
            w = jnp.concatenate(
                [
                    wb[wblk(2 * d + zz, cc, xx), :, pl.ds(2 * SPAD, SPAD)]
                    for zz in range(2)
                    for xx in range(NX)
                    for cc in range(NC)
                ],
                axis=0,
            )
            psh[d] = nt(hidden, w).astype(BF16)
            return carry

        lax.fori_loop(0, NY, project, 0)
        sh(4).start()
        sh(5).start()

    def stage_reduce(i):
        for k in (2, 3):
            rs(i, k).wait_recv()
            rs(i, k + 2).start()

    def shared_relay():
        sh(0, yd).wait_recv()
        sh(2).start()
        sh(1, yu).wait_recv()
        sh(3).start()

    def shared_reduce():
        sh(4).wait_recv()
        psh[yu, plo] = (psh[yu, plo].astype(F32) + s1[0].astype(F32)).astype(BF16)
        sh(6).start()
        sh(5).wait_recv()
        psh[yd, phi] = (psh[yd, phi].astype(F32) + s1[1].astype(F32)).astype(BF16)
        sh(7).start()

    def shared_total():
        sh(6).wait_recv()
        sh(7).wait_recv()
        shared[...] = psh[y].astype(F32) + s2[0].astype(F32) + s2[1].astype(F32)

    def back(i, b):
        to = eid(plane_of(i), lax.rem(b, NX), lax.div(b, NX))
        return to, send(sbuf.at[i, b], rbuf.at[e], os_.at[i * (NX * NC) + b], or_.at[e], to, y)

    def stage_return(i):
        for k in (0, 1, 4, 5):
            rs(i, k).wait_recv()
        tot[mine] = pb[i, y].astype(F32) + rb[i].astype(F32)
        tot[other] = ra[i, 0].astype(F32) + ra[i, 1].astype(F32)
        total = tot[...].astype(BF16)
        to_row = lax.broadcasted_iota(jnp.int32, (ROWS, CHUNK), 0)
        of_row = lax.broadcasted_iota(jnp.int32, (ROWS, CHUNK), 1)
        base = CAP * lax.shift_right_logical(to_row, 4)
        inner = to_row & (PACK - 1)

        def move(hit, values):
            return jnp.dot(hit.astype(F32).astype(BF16), values, preferred_element_type=F32)

        first = move(of_row == base + inner, total)
        sbuf[i, :, :, pl.ds(0, FEAT)] = first.astype(BF16).reshape(NX * NC, PACK, FEAT)
        last = jnp.zeros((ROWS, ROWS), F32)
        for q in range(4):
            hit = (of_row == base + PACK + inner - 4 * q) & (inner >= 4 * q) & (inner < 4 * q + 4)
            last = last + move(hit, total[:, q * 128 : (q + 1) * 128])
        sbuf[i, :, :, pl.ds(FEAT, 128)] = last.astype(BF16).reshape(NX * NC, PACK, 128)

        def go(b, carry):
            to, copy = back(i, b)

            @pl.when(to != e)
            def _():
                copy.start()

            @pl.when(to == e)
            def _():
                rbuf[e] = sbuf[i, b]

            return carry

        lax.fori_loop(0, NX * NC, go, 0)

    def stage_tables():
        for k in range(3):
            spread(lg, 3, k).wait_recv()
        logits = (lg[0] + lg[1]) + (lg[2] + lg[3])
        mine = jnp.transpose(names)
        lane = c_i.astype(F32)
        count = jnp.zeros((ROWS, ROWS), F32)
        for k in range(TOP):
            count = count + (mine[:, k : k + 1] == lane).astype(F32)
        chosen = count > 0.5
        top = jnp.max(jnp.where(chosen, logits, -jnp.inf), axis=1, keepdims=True)
        weight = jnp.where(chosen, jnp.exp(jnp.where(chosen, logits - top, 0.0)), 0.0)
        gates = weight / jnp.sum(weight, axis=1, keepdims=True)
        place = jnp.dot(
            (c_i < r_i).astype(F32).astype(BF16), count.astype(BF16), preferred_element_type=F32
        )
        place = jnp.where(chosen, place, 255.0).astype(BF16)
        high = gates.astype(BF16)
        low = (gates - high.astype(F32)).astype(BF16)

        def fill(b, carry):
            ee = lax.broadcasted_iota(jnp.int32, (ROWS, 256), 0)
            jj = lax.broadcasted_iota(jnp.int32, (ROWS, 256), 1)
            inner = jj & (PACK - 1)
            mat = (ee == lax.shift_right_logical(jj, 4) + b * PACK).astype(F32).astype(BF16)
            where = jnp.dot(place, mat, preferred_element_type=F32)
            at = pl.ds(pl.multiple_of(b * 256, 256), 256)
            for h, g in enumerate((high, low)):
                spaced = jnp.dot(g, mat, preferred_element_type=F32)
                for q, want in enumerate((inner, PACK + (inner & 3))):
                    hit = jnp.where(where == want.astype(F32), spaced, 0.0)
                    tab[q, pl.ds(h * ROWS, ROWS), at] = hit.astype(BF16)
            return carry

        lax.fori_loop(0, NE * PACK // 256, fill, 0)

    def step(j, carry):
        @pl.when((j >= 1) & (j < NZ + 1))
        def _():
            stage_relay(j - 1)

        @pl.when(j < NZ)
        def _():
            stage_rows(j)

        @pl.when(j == 0)
        def _():
            wz_step(3)

        @pl.when(j == 1)
        def _():
            for d in (1, -1):
                wz_got(3, d)
            wx(0).start()
            wx(1).start()
            wsib(0, c).start()

        @pl.when(j == 5)
        def _():
            wx_got(0)
            wx(2).start()
            wx_got(1)
            wx(3).start()
            wsib(3, c).start()
            wsib(1, c).start()

        @pl.when(j == 7)
        def _():
            wx_got(2)
            wx_got(3)
            wsib(2, c).start()

        @pl.when(j == 2)
        def _():
            for load in loads:
                load.wait()
            for k in range(8):
                pair(k).wait_recv()
            shared_relay()

        @pl.when((j >= 2) & (j < NZ + 2))
        def _():
            stage_experts(j - 2)

        @pl.when((j >= 3) & (j < NZ + 3))
        def _():
            stage_reduce(j - 3)

        @pl.when(j >= 4)
        def _():
            stage_return(j - 4)

        @pl.when(j == 5)
        def _():
            stage_tables()

        @pl.when(j == SHARED_AT)
        def _():
            stage_shared()

        @pl.when(j == SHARED_AT + 1)
        def _():
            shared_reduce()

        @pl.when(j == SHARED_AT + 2)
        def _():
            shared_total()

        for t, at in ((1, 0), (2, 1), (3, 2), (4, 3)):

            @pl.when(j == at)
            def _(t=t):
                ring(t)

        return carry

    lax.fori_loop(0, NZ + 4, step, 0)

    def arrive(k, carry):
        s = lax.rem(e + k, NE)
        send(rbuf.at[s], rbuf.at[s], os_.at[0], or_.at[s], sib, y).wait_recv()
        return carry

    lax.fori_loop(1, NE, arrive, 0)
    back_rows = rbuf[:, :, pl.ds(0, FEAT)].reshape(NE * PACK, FEAT)
    pieces = rbuf[:, :, pl.ds(FEAT, 128)].reshape(NE * PACK, 128).astype(F32)
    part_of = lax.shift_right_logical(
        lax.broadcasted_iota(jnp.int32, (NE * PACK, 128), 0) & (PACK - 1), 2
    )
    extra = jnp.concatenate(
        [jnp.where(part_of == q, pieces, 0.0).astype(BF16) for q in range(4)], axis=1
    )
    both = jnp.dot(tab[0], back_rows, preferred_element_type=F32) + jnp.dot(
        tab[1], extra, preferred_element_type=F32
    )
    base_o[...] = mixed[...] + shared[...]
    out[...] = both[:ROWS] + both[ROWS:]

    for k in range(3):
        ax(k).wait_send()
        spread(sq, 0, k).wait_send()
        spread(lg, 3, k).wait_send()
    for t in range(4):
        for d in (1, -1):
            az(t, d).wait_send()
            if t < 3 or d > 0:
                bz(t, d).wait_send()
            wz(t, d).wait_send()
            tz0(t, d).wait_send()
            if t > 0:
                tz(t, d).wait_send()
        bx(t).wait_send()
        b_sib(t, c).wait_send()
        wx(t).wait_send()
        wsib(t, c).wait_send()
        tx(t).wait_send()
    for d in (0, -1, 1, -2, 2, -3, 3, 4):
        a_sib(d, c).wait_send()
    for k in range(2):
        pa(k).wait_send()
        pb2(k).wait_send()

    def drain(i, carry):
        across(i, lax.rem(z + i, NZ), c).wait_send()

        def sent(b, inner):
            to, copy = back(i, b)

            @pl.when(to != e)
            def _():
                copy.wait_send()

            return inner

        lax.fori_loop(0, NX * NC, sent, 0)
        for k in range(6):
            ag(i, k).wait_send()
            rs(i, k).wait_send()
        return carry

    lax.fori_loop(0, NZ, drain, 0)
    for k in range(8):
        pair(k).wait_send()
        sh(k).wait_send()


def mixer(ctx, opt, ids, hid, gain, router, win_s, wout_s, win, wout):
    vm = pl.BlockSpec(memory_space=pltpu.VMEM)
    hbm = pl.BlockSpec(memory_space=pl.ANY)

    def pairs(*shapes):
        return [pltpu.SemaphoreType.DMA(s) for s in shapes for _ in range(2)]

    return pl.pallas_call(
        mixer_kernel,
        name="mixer_tail",
        out_shape=[jax.ShapeDtypeStruct((ROWS, FEAT), F32)] * 2,
        in_specs=[vm] * 8 + [hbm] * 2,
        out_specs=[vm] * 2,
        scratch_shapes=[
            pltpu.VMEM((NE, 16, FEAT + ROWS), BF16),
            pltpu.VMEM((NE, 16, FEAT), BF16),
            pltpu.VMEM((NY, ROWS, FEAT), F32),
            pltpu.VMEM((2, ROWS // 2, FEAT), F32),
            pltpu.VMEM((2, ROWS, FEAT), F32),
            pltpu.VMEM((4, 8, ROWS), F32),
            pltpu.VMEM((4, ROWS, ROWS), F32),
            pltpu.VMEM((ROWS, FEAT), F32),
            pltpu.VMEM((ROWS, FEAT), F32),
            pltpu.VMEM((2, 2 * ROWS, NE * PACK), BF16),
            pltpu.VMEM((NE, ROWS, FEAT), BF16),
            pltpu.VMEM((NE, ROWS), F32),
            pltpu.VMEM((NZ, CHUNK, FEAT), BF16),
            pltpu.VMEM((NZ, NY, HALF, FEAT), BF16),
            pltpu.VMEM((NZ, 2, HALF, 256), BF16),
            pltpu.VMEM((NZ, NY, HALF, FEAT), BF16),
            pltpu.VMEM((NZ, 2, HALF, FEAT), BF16),
            pltpu.VMEM((NZ, HALF, FEAT), BF16),
            pltpu.VMEM((NZ, 2, HALF, 256), BF16),
            pltpu.VMEM((NY, ROWS, FEAT), BF16),
            pltpu.VMEM((NY, ROWS, FEAT), BF16),
            pltpu.VMEM((2, ROWS // 2, FEAT), BF16),
            pltpu.VMEM((2, ROWS, FEAT), BF16),
            pltpu.VMEM((NE, 32, 3 * SPAD), BF16),
            pltpu.VMEM((2, QPAD, WIDTH), BF16),
            pltpu.VMEM((QPAD, WIDTH), BF16),
            pltpu.VMEM((NZ, NX * NC, PACK, PWIDTH), BF16),
            pltpu.VMEM((NE, PACK, PWIDTH), BF16),
            pltpu.VMEM((ROWS, 2 * SPAD), F32),
            pltpu.VMEM((CHUNK, FEAT), F32),
            pltpu.SemaphoreType.DMA((3,)),
        ]
        + pairs((3,), (8,), (8,), (8,), (4,), (4,), (4,), (6,))
        + pairs((4,), (8,), (6,), (8,), (8,), (4,), (4,))
        + pairs((8,), (6, NZ), (6, NZ), (8,), (NE,)),
        compiler_params=pltpu.CompilerParams(
            collective_id=0, has_side_effects=True, vmem_limit_bytes=VMEM_LIMIT
        ),
    )(ctx, opt, ids, hid, gain, router, win_s, wout_s, win, wout)


def per_device(
    hidden_state, context, out_proj, norm_gain, router_weight,
    expert_in, expert_out, shared_in, shared_out, route_ids,
):
    win = jnp.transpose(expert_in[0], (1, 2, 0))
    routed, base = mixer(
        context, out_proj.T, route_ids.T, hidden_state, norm_gain.reshape(4, 128),
        router_weight.T, shared_in, shared_out.T, win, expert_out[0],
    )
    return base + routed


def solution(mesh):
    return jax.shard_map(
        per_device,
        mesh=mesh,
        in_specs=(
            P("expert", "mp"),
            P("expert", "mp"),
            P("mp", "expert"),
            P("mp"),
            P("mp", None),
            P("expert", None, None, "mp"),
            P("expert", "mp", None),
            P("expert", None, "mp"),
            P("mp", "expert"),
            P("expert", None),
        ),
        out_specs=P("expert", "mp"),
        check_vma=False,
    )
```
